128 devices in a mesh: section: 4 (over x), row: 32 (over z, y, core).
Axes of the slice: x: 4, y: 4, z: 4, core: 2. Of those that a mesh axis runs over, the one named last changes fastest.
Arguments:
- tokens: int32 [4, 64, 128], P(None, 'row'), may hold values from 0 to 32
- embed: bfloat16 [33, 768], replicated, may hold values from -6 to 6
- ln_gain: float32 [4, 768], P('section'), may hold values from 0.5 to 1.5
- w_qkv: bfloat16 [4, 768, 2304], P('section'), may hold values from -0.21875 to 0.21875
- w_out: bfloat16 [4, 768, 768], P('section'), may hold values from -0.21875 to 0.21875
- out_grad: bfloat16 [4, 64, 128, 768], P(None, 'row'), may hold values from -0.009887695 to 0.009887695
Outputs:
- grad_qkv: float32 [4, 768, 2304], P('section', 'row')
- grad_out: float32 [4, 768, 768], P('section', 'row')
- grad_gain: float32 [4, 768], P('section', 'row')
The draws below stay inside these ranges and needn't reach their ends.
All inputs are finite; a program needn't handle non-finite values.
Results may differ from the reference program's by a relative error of at most 0.04.
Values may be sent and summed in bfloat16 or wider, within the bound.
A program may use at most 192 MiB of HBM per device.

```python
import jax
import jax.numpy as jnp
from jax import lax

D = 768
HEADS = 12
HEAD_DIM = 64
VOCAB = 33
SEQ = 128
MICRO = 4
LAYERS = 4
ROWS = 64


def touch_ends(values, own_key, low, high):
    longest = values.shape.index(max(values.shape))
    spots = []
    for shift in (0, 1):
        where = [jax.random.randint(jax.random.fold_in(own_key, axis), (), 0, length) for axis, length in enumerate(values.shape)]
        where[longest] = (where[longest] + shift) % values.shape[longest]
        spots.append(tuple(where))
    return values.at[spots[0]].set(low).at[spots[1]].set(high)


def steps_of(stream_key, dims, pieces, least, top_value):
    factor_of = 1.0
    for dim, shards_of in pieces:
        draws = jax.random.uniform(jax.random.fold_in(jax.random.fold_in(stream_key, 6), dim), (shards_of,), jnp.float32, least / len(pieces), top_value / len(pieces))
        factor_of = factor_of * jnp.repeat(jnp.exp(draws), dims[dim] // shards_of).reshape((-1,) + (1,) * (len(dims) - 1 - dim))
    return factor_of


def normal_values(rng, shape, scale, limit, shards=(), held_as=jnp.bfloat16):
    array = jax.random.normal(rng, shape, jnp.float32) * scale
    if len(shards) > 0:
        array = steps_of(rng, shape, shards, -0.22, 0.18) * array
    return jnp.clip(array, min=-limit, max=limit).astype(held_as)


def setup_inputs(seed: int = 0) -> dict:
    seeds = jax.random.split(jax.random.key(seed), 7)
    tokens = touch_ends(jax.random.randint(seeds[0], (MICRO, ROWS, SEQ), 0, VOCAB), jax.random.fold_in(seeds[0], 1), 0, VOCAB - 1).astype(jnp.int32)
    embed = normal_values(seeds[1], (VOCAB, D), 1.0, 6.0)
    ln_gain = jnp.clip(1.0 + 0.1 * jax.random.normal(seeds[2], (LAYERS, D), jnp.float32), 0.5, 1.5)
    w_qkv = normal_values(seeds[3], (LAYERS, D, 3 * D), D ** -0.5, 0.21875, ((0, 4),))
    w_out = normal_values(seeds[4], (LAYERS, D, D), D ** -0.5, 0.21875, ((0, 4),))
    out_grad = normal_values(seeds[5], (MICRO, ROWS, SEQ, D), (0.3 * (MICRO * ROWS * SEQ) ** -0.5), 0.009887695, ((1, 32),))
    return dict(tokens=tokens, embed=embed, ln_gain=ln_gain, w_qkv=w_qkv, w_out=w_out, out_grad=out_grad)


def norm_rows(x, gain):
    values = x.astype(jnp.float32)
    centred = values - lax.optimization_barrier(jnp.mean(values, axis=-1, keepdims=True))
    spread = lax.optimization_barrier(jnp.mean(centred * centred, axis=-1, keepdims=True))
    return (centred * lax.rsqrt(spread + 1e-05) * gain).astype(jnp.bfloat16)

def split_heads(qkv):
    parts = qkv.reshape(qkv.shape[0], qkv.shape[1], 3, HEADS, HEAD_DIM)
    return (parts[:, :, 0], parts[:, :, 1], parts[:, :, 2])

def layer_forward(x, gain, wqkv, wout, scale):
    nrows, seq, width = x.shape
    normed = norm_rows(x, gain)
    qkv = jnp.dot(normed.reshape(-1, width), wqkv, preferred_element_type=jnp.float32).astype(jnp.bfloat16)
    qkv = qkv.reshape(nrows, seq, 3 * width)
    query, keys, values = split_heads(qkv)
    logits = scale * jnp.einsum('rihd,rjhd->ihj', query.astype(jnp.float32), keys.astype(jnp.float32))
    probs = jax.nn.softmax(logits, axis=-1).astype(jnp.bfloat16)
    mixed = jnp.einsum('ihj,rjhd->rihd', probs.astype(jnp.float32), values.astype(jnp.float32)).astype(jnp.bfloat16)
    mixed = mixed.reshape(-1, width)
    output = x + jnp.dot(mixed, wout, preferred_element_type=jnp.float32).reshape(nrows, seq, width)
    return (output, probs, qkv)

def layer_backward(x, gain, wqkv, wout, probs, qkv, upstream, scale):
    nrows, seq, width = x.shape
    query, keys, values = split_heads(qkv)
    normed, norm_back = jax.vjp(norm_rows, x, gain)
    mixed = jnp.einsum('ihj,rjhd->rihd', probs.astype(jnp.float32), values.astype(jnp.float32)).astype(jnp.bfloat16)
    flat_up = upstream.astype(jnp.bfloat16).reshape(-1, width)
    g_out = jnp.dot(mixed.reshape(-1, width).T, flat_up, preferred_element_type=jnp.float32)
    d_mixed = jnp.dot(flat_up, wout.T, preferred_element_type=jnp.float32).astype(jnp.bfloat16)
    d_mixed = d_mixed.reshape(nrows, seq, HEADS, HEAD_DIM)
    d_probs = jnp.einsum('rihd,rjhd->ihj', d_mixed.astype(jnp.float32), values.astype(jnp.float32))
    prob_f = probs.astype(jnp.float32)
    d_logits = (prob_f * (d_probs - lax.optimization_barrier(jnp.sum(d_probs * prob_f, axis=-1, keepdims=True)))).astype(jnp.bfloat16)
    d_values = jnp.einsum('ihj,rihd->rjhd', prob_f, d_mixed.astype(jnp.float32)).astype(jnp.bfloat16)
    d_query = (scale * jnp.einsum('ihj,rjhd->rihd', d_logits.astype(jnp.float32), keys.astype(jnp.float32))).astype(jnp.bfloat16)
    d_keys = (scale * jnp.einsum('ihj,rihd->rjhd', d_logits.astype(jnp.float32), query.astype(jnp.float32))).astype(jnp.bfloat16)
    d_qkv = jnp.stack([d_query, d_keys, d_values], axis=2).reshape(-1, 3 * width)
    g_qkv = jnp.dot(normed.reshape(-1, width).T, d_qkv, preferred_element_type=jnp.float32)
    d_normed = jnp.dot(d_qkv, wqkv.T, preferred_element_type=jnp.float32).astype(jnp.bfloat16)
    d_input, g_gain = norm_back(d_normed.reshape(nrows, seq, width))
    d_x = upstream + d_input
    return (d_x, g_qkv, g_out, g_gain)

def reference(tokens, embed, ln_gain, w_qkv, w_out, out_grad):
    scale = HEAD_DIM ** (-0.5) / ROWS ** 0.5
    grad_qkv = jnp.zeros(w_qkv.shape, jnp.float32)
    grad_out = jnp.zeros(w_out.shape, jnp.float32)
    grad_gain = jnp.zeros(ln_gain.shape, jnp.float32)
    for micro in range(MICRO):
        state = jnp.take(embed, tokens[micro], axis=0).astype(jnp.float32)
        inputs_kept = []
        probs_kept = []
        qkv_kept = []
        for layer in range(LAYERS):
            inputs_kept.append(state)
            state, probs, qkv = layer_forward(state, ln_gain[layer], w_qkv[layer], w_out[layer], scale)
            probs_kept.append(probs)
            qkv_kept.append(qkv)
        upstream = out_grad[micro].astype(jnp.float32)
        for layer in reversed(range(LAYERS)):
            upstream, g_qkv, g_out, g_gain = layer_backward(inputs_kept[layer], ln_gain[layer], w_qkv[layer], w_out[layer], probs_kept[layer], qkv_kept[layer], upstream, scale)
            grad_qkv = grad_qkv.at[layer].add(g_qkv)
            grad_out = grad_out.at[layer].add(g_out)
            grad_gain = grad_gain.at[layer].add(g_gain)
    return (grad_qkv, grad_out, grad_gain)
```

```python
import functools

import jax
import jax.numpy as jnp
from jax import lax
from jax.experimental import pallas as pl
from jax.experimental.pallas import tpu as pltpu
from jax.sharding import PartitionSpec as P

HEADS = 12
HEAD_DIM = 64
LAYERS = 4
PAIRS = HEADS // 2
WIDTH = HEADS * HEAD_DIM
SEQ = 128
MESH = pl.DeviceIdType.MESH
BF = jnp.bfloat16
F32 = jnp.float32


def dot(a, b, ca, cb):
    return lax.dot_general(a, b, (((ca,), (cb,)), ((), ())), preferred_element_type=F32)


def norm_parts(x):
    centred = x - jnp.mean(x, axis=-1, keepdims=True)
    spread = jnp.mean(centred * centred, axis=-1, keepdims=True)
    rstd = lax.rsqrt(spread + 1e-05)
    return centred * rstd, rstd


def kernel(
    n_row,
    scale,
    tok_ref,
    emb_ref,
    gain_ref,
    wqkv_hbm,
    wout_hbm,
    og_hbm,
    gq_hbm,
    go_hbm,
    wq,
    wo,
    xs,
    qkv,
    probs,
    mixed,
    part,
    recv,
    dlog,
    dyf,
    ogb,
    dmix,
    dqkv,
    hbuf,
    dhacc,
    gq,
    go,
    rs_send,
    rs_recv,
    ag_send,
    ag_recv,
    w_sem,
    og_sem,
    g_sem,
):
    sec = lax.axis_index("section")
    me = lax.axis_index("row")
    piece = part.shape[0] // n_row

    barrier = pltpu.get_barrier_semaphore()

    def greet(d, carry):
        peer = lax.rem(me + d, n_row)
        pl.semaphore_signal(barrier, inc=1, device_id=(sec, peer), device_id_type=MESH)
        return carry

    lax.fori_loop(1, n_row, greet, 0)

    for l in range(LAYERS):
        pltpu.make_async_copy(wqkv_hbm.at[l], wq.at[l], w_sem.at[0, l]).start()
        pltpu.make_async_copy(wout_hbm.at[l], wo.at[l], w_sem.at[1, l]).start()
    pltpu.make_async_copy(og_hbm.at[sec], ogb, og_sem).start()

    lane = lax.broadcasted_iota(jnp.int32, (1, SEQ), 1)
    low = (lane < HEAD_DIM).astype(F32).astype(BF)
    high = (lane >= HEAD_DIM).astype(F32).astype(BF)

    def rows_of(k):
        return pl.ds(pl.multiple_of(k * piece, 16), piece)

    def split_block(a0, a1):
        top = jnp.concatenate([a0 * low, a1 * low], axis=1)
        bottom = jnp.concatenate([a0 * high, a1 * high], axis=1)
        return jnp.concatenate([top, bottom], axis=0)

    def pair_scores(left, right, factor):
        for p in range(PAIRS):
            la, ra = left(p), right(p)
            out = dot(split_block(*la), jnp.concatenate(ra, axis=1), 1, 1)
            if factor is not None:
                out = factor * out
            part[pl.ds(2 * SEQ * p, 2 * SEQ), :] = out.astype(BF)

    def rs_copy(d):
        peer = lax.rem(me + d, n_row)
        return pltpu.make_async_remote_copy(
            src_ref=part.at[rows_of(peer)],
            dst_ref=recv.at[d],
            send_sem=rs_send.at[d],
            recv_sem=rs_recv.at[d],
            device_id=(sec, peer),
            device_id_type=MESH,
        )

    def start_reduce():
        def send(d, carry):
            rs_copy(d).start()
            return carry

        lax.fori_loop(1, n_row, send, 0)

    def finish_reduce():
        def take(d, total):
            rs_copy(d).wait_recv()
            return total + recv[d].astype(F32)

        return lax.fori_loop(1, n_row, take, part[rows_of(me), :].astype(F32))

    def ag_copy(buf, d):
        peer = lax.rem(me + d, n_row)
        return pltpu.make_async_remote_copy(
            src_ref=buf.at[rows_of(me)],
            dst_ref=buf.at[rows_of(me)],
            send_sem=ag_send.at[d],
            recv_sem=ag_recv.at[d],
            device_id=(sec, peer),
            device_id_type=MESH,
        )

    def start_gather(buf):
        def send(d, carry):
            ag_copy(buf, d).start()
            return carry

        lax.fori_loop(1, n_row, send, 0)

    def finish_gather(buf):
        def take(d, carry):
            ag_copy(buf, d).wait_recv()
            rs_copy(d).wait_send()
            ag_copy(buf, d).wait_send()
            return carry

        lax.fori_loop(1, n_row, take, 0)

    def halves(ref, base, p):
        cols = pl.ds(base + SEQ * p, SEQ)
        return ref[pl.ds(0, SEQ), cols], ref[pl.ds(SEQ, SEQ), cols]

    def beside(buf, p):
        return jnp.concatenate(
            [buf[pl.ds(2 * SEQ * p, SEQ), :], buf[pl.ds(2 * SEQ * p + SEQ, SEQ), :]], axis=1
        )

    def put_halves(ref, base, p, value):
        cols = pl.ds(base + SEQ * p, SEQ)
        ref[pl.ds(0, SEQ), cols] = value[:, :SEQ]
        ref[pl.ds(SEQ, SEQ), cols] = value[:, SEQ:]

    vocab = emb_ref.shape[0]
    ids = lax.broadcasted_iota(jnp.int32, (tok_ref.shape[0], vocab), 1)
    picks = (tok_ref[...] == ids).astype(F32).astype(BF)
    xs[0] = dot(picks, emb_ref[...], 1, 0)

    def forward(l, carry):
        x = xs[l]
        normal, _ = norm_parts(x)
        h = (normal * gain_ref[l]).astype(BF)
        pltpu.make_async_copy(wqkv_hbm.at[l], wq.at[l], w_sem.at[0, l]).wait()
        here = qkv.at[l]
        for n in range(3):
            cols = pl.ds(WIDTH * n, WIDTH)
            here[:, cols] = dot(h, wq[l, :, cols], 1, 0).astype(BF)
        pair_scores(lambda p: halves(here, 0, p), lambda p: halves(here, WIDTH, p), scale)

        @pl.when(l == 0)
        def _():
            pl.semaphore_wait(barrier, n_row - 1)

        start_reduce()
        logits = finish_reduce()
        shifted = jnp.exp(logits - jnp.max(logits, axis=-1, keepdims=True))
        own = shifted / jnp.sum(shifted, axis=-1, keepdims=True)
        probs_l = probs.at[l]
        probs_l[rows_of(me), :] = own.astype(BF)
        start_gather(probs_l)
        finish_gather(probs_l)
        mixed_l = mixed.at[l]
        for p in range(PAIRS):
            out = dot(beside(probs_l, p), split_block(*halves(here, 2 * WIDTH, p)), 1, 0)
            put_halves(mixed_l, 0, p, out.astype(BF))
        pltpu.make_async_copy(wout_hbm.at[l], wo.at[l], w_sem.at[1, l]).wait()

        @pl.when(l < LAYERS - 1)
        def _():
            xs[l + 1] = x + dot(mixed_l[...], wo[l], 1, 0)

        return carry

    lax.fori_loop(0, LAYERS, forward, 0)

    pltpu.make_async_copy(og_hbm.at[sec], ogb, og_sem).wait()
    dyf[...] = ogb[...].astype(F32)

    def backward(step, carry):
        l = LAYERS - 1 - step
        here = qkv.at[l]
        probs_l = probs.at[l]
        dyb = dyf[...].astype(BF)
        dmix[...] = dot(dyb, wo[l], 1, 1).astype(BF)
        pair_scores(lambda p: halves(dmix, 0, p), lambda p: halves(here, 2 * WIDTH, p), None)
        start_reduce()

        @pl.when(step > 0)
        def _():
            pltpu.make_async_copy(gq, gq_hbm.at[l], g_sem.at[0]).wait()
            pltpu.make_async_copy(go, go_hbm.at[l], g_sem.at[1]).wait()

        go[...] = dot(mixed[l], dyb, 0, 0).astype(BF)
        pltpu.make_async_copy(go, go_hbm.at[l], g_sem.at[1]).start()
        for p in range(PAIRS):
            rows = pl.ds(2 * SEQ * p, 2 * SEQ)
            out = dot(probs_l[rows, :], split_block(*halves(dmix, 0, p)), 0, 0)
            put_halves(dqkv, 2 * WIDTH, p, out.astype(BF))
        dprobs = finish_reduce()
        own = probs_l[rows_of(me), :].astype(F32)
        inner = jnp.sum(dprobs * own, axis=-1, keepdims=True)
        dlog[rows_of(me), :] = (own * (dprobs - inner)).astype(BF)
        start_gather(dlog)

        normal, rstd = norm_parts(xs[l])
        hbuf[...] = (normal * gain_ref[l]).astype(BF)
        vcols = pl.ds(2 * WIDTH, WIDTH)
        gq[:, vcols] = dot(hbuf[...], dqkv[:, vcols], 0, 0).astype(BF)
        dhacc[...] = dot(dqkv[:, vcols], wq[l, :, vcols], 1, 1)
        finish_gather(dlog)

        for p in range(PAIRS):
            out = dot(beside(dlog, p), split_block(*halves(here, WIDTH, p)), 1, 0)
            put_halves(dqkv, 0, p, (scale * out).astype(BF))
            rows = pl.ds(2 * SEQ * p, 2 * SEQ)
            out = dot(dlog[rows, :], split_block(*halves(here, 0, p)), 0, 0)
            put_halves(dqkv, WIDTH, p, (scale * out).astype(BF))
        qk = pl.ds(0, 2 * WIDTH)

        @pl.when(l > 0)
        def _():
            dh = dhacc[...] + dot(dqkv[:, qk], wq[l, :, qk], 1, 1)
            dn = dh.astype(BF).astype(F32) * gain_ref[l]
            first = jnp.mean(dn, axis=-1, keepdims=True)
            second = jnp.mean(dn * normal, axis=-1, keepdims=True)
            dyf[...] = dyf[...] + rstd * (dn - first - normal * second)

        for n in range(2):
            cols = pl.ds(WIDTH * n, WIDTH)
            gq[:, cols] = dot(hbuf[...], dqkv[:, cols], 0, 0).astype(BF)
        pltpu.make_async_copy(gq, gq_hbm.at[l], g_sem.at[0]).start()
        return carry

    lax.fori_loop(0, LAYERS, backward, 0)
    pltpu.make_async_copy(gq, gq_hbm.at[0], g_sem.at[0]).wait()
    pltpu.make_async_copy(go, go_hbm.at[0], g_sem.at[1]).wait()


def local(tokens, embed, ln_gain, w_qkv, w_out, out_grad):
    n_row = lax.axis_size("row")
    section = lax.axis_index("section")
    row = lax.axis_index("row")
    micro, rows_here, seq = tokens.shape
    vocab, width = embed.shape
    npos = rows_here * seq
    scale = HEAD_DIM ** (-0.5) / (rows_here * n_row) ** 0.5
    tok = lax.dynamic_index_in_dim(tokens, section, 0, keepdims=False).reshape(npos, 1)
    emb = jnp.pad(embed, ((0, -vocab % 16), (0, 0)))
    gains = lax.all_gather(ln_gain, "section", axis=0, tiled=False)
    wqkv = lax.all_gather(w_qkv, "section", axis=0, tiled=True)
    wout = lax.all_gather(w_out, "section", axis=0, tiled=True)
    flat = HEADS * seq
    vm, anyspace = pl.BlockSpec(memory_space=pltpu.VMEM), pl.BlockSpec(memory_space=pl.ANY)
    gq, go = pl.pallas_call(
        functools.partial(kernel, n_row, scale),
        out_shape=(
            jax.ShapeDtypeStruct((LAYERS, width, 3 * width), BF),
            jax.ShapeDtypeStruct((LAYERS, width, width), BF),
        ),
        in_specs=[vm, vm, vm, anyspace, anyspace, anyspace],
        out_specs=(anyspace, anyspace),
        scratch_shapes=[
            pltpu.VMEM((LAYERS, width, 3 * width), BF),
            pltpu.VMEM((LAYERS, width, width), BF),
            pltpu.VMEM((LAYERS, npos, width), F32),
            pltpu.VMEM((LAYERS, npos, 3 * width), BF),
            pltpu.VMEM((LAYERS, flat, seq), BF),
            pltpu.VMEM((LAYERS, npos, width), BF),
            pltpu.VMEM((flat, seq), BF),
            pltpu.VMEM((n_row, flat // n_row, seq), BF),
            pltpu.VMEM((flat, seq), BF),
            pltpu.VMEM((npos, width), F32),
            pltpu.VMEM((npos, width), BF),
            pltpu.VMEM((npos, width), BF),
            pltpu.VMEM((npos, 3 * width), BF),
            pltpu.VMEM((npos, width), BF),
            pltpu.VMEM((npos, width), F32),
            pltpu.VMEM((width, 3 * width), BF),
            pltpu.VMEM((width, width), BF),
            pltpu.SemaphoreType.DMA((n_row,)),
            pltpu.SemaphoreType.DMA((n_row,)),
            pltpu.SemaphoreType.DMA((n_row,)),
            pltpu.SemaphoreType.DMA((n_row,)),
            pltpu.SemaphoreType.DMA((2, LAYERS)),
            pltpu.SemaphoreType.DMA,
            pltpu.SemaphoreType.DMA((2,)),
        ],
        compiler_params=pltpu.CompilerParams(
            collective_id=0, has_side_effects=True, vmem_limit_bytes=64 * 1024 * 1024 - 1024 * 1024
        ),
    )(tok, emb, gains, wqkv, wout, out_grad.reshape(micro, npos, width))

    def reduced(g):
        g = lax.psum_scatter(g, "section", scatter_dimension=0, tiled=True)
        return lax.psum_scatter(g.astype(F32), "row", scatter_dimension=1, tiled=True)

    grad_qkv = reduced(gq)
    grad_out = reduced(go)
    own_rows = width // n_row
    w_own = lax.dynamic_slice_in_dim(w_qkv[0], row * own_rows, own_rows, 0).astype(F32)
    gain_own = lax.dynamic_slice_in_dim(ln_gain[0], row * own_rows, own_rows, 0)
    grad_gain = (jnp.sum(w_own * grad_qkv[0], axis=-1) / gain_own)[None]
    return (grad_qkv, grad_out, grad_gain)


def solution(mesh):
    in_specs = (
        P(None, "row", None),
        P(),
        P("section", None),
        P("section", None, None),
        P("section", None, None),
        P(None, "row", None, None),
    )
    out_specs = (P("section", "row", None), P("section", "row", None), P("section", "row"))
    return jax.shard_map(local, mesh=mesh, in_specs=in_specs, out_specs=out_specs, check_vma=False)
```

```python
import functools

import jax
import jax.numpy as jnp
from jax import lax
from jax.experimental import pallas as pl
from jax.experimental.pallas import tpu as pltpu
from jax.sharding import PartitionSpec as P

HEADS = 12
HEAD_DIM = 64
LAYERS = 4
PAIRS = HEADS // 2
WIDTH = HEADS * HEAD_DIM
SEQ = 128
SIDE = 4
OUT, VAL, QRY, KEY = 0, 1, 2, 3
CHUNKS = 6
CHUNKS_FIRST = 2
QUARTER = WIDTH // 4
MESH = pl.DeviceIdType.MESH
BF = jnp.bfloat16
F32 = jnp.float32


def dot(a, b, ca, cb):
    return lax.dot_general(a, b, (((ca,), (cb,)), ((), ())), preferred_element_type=F32)


def norm_parts(x):
    centred = x - jnp.mean(x, axis=-1, keepdims=True)
    spread = jnp.mean(centred * centred, axis=-1, keepdims=True)
    rstd = lax.rsqrt(spread + 1e-05)
    return centred * rstd, rstd


def kernel(
    n_row,
    scale,
    tok_ref,
    emb_ref,
    gain_ref,
    wqkv_hbm,
    wout_hbm,
    og_hbm,
    gq_ref,
    go_ref,
    wcat,
    gains,
    tab,
    xs,
    qkv,
    probs,
    mixed,
    part,
    recv,
    dlog,
    dyf,
    ogb,
    dmix,
    dqkv,
    hbuf,
    dhacc,
    grad,
    pairbuf,
    line1,
    sum1,
    line2,
    xout,
    xin,
    fin,
    rs_send,
    rs_recv,
    ag_send,
    ag_recv,
    w_sem,
    og_sem,
    tab_send,
    tab_recv,
    gain_send,
    gain_recv,
    ring_send,
    ring_recv,
    twin_send,
    twin_recv,
    pair_send,
    pair_recv,
    c1_send,
    c1_recv,
    c2_send,
    c2_recv,
    x_send,
    x_recv,
):
    sec = lax.axis_index("section")
    me = lax.axis_index("row")
    piece = part.shape[0] // n_row
    core = lax.rem(me, 2)
    partner = me + 1 - 2 * core
    chip = me // 2
    zc = chip // SIDE
    yc = lax.rem(chip, SIDE)

    def row_at(z, y):
        return (z * SIDE + y) * 2 + core

    local_qkv = pltpu.make_async_copy(
        wqkv_hbm.at[0], wcat.at[sec, :, pl.ds(0, 3 * WIDTH)], w_sem.at[0]
    )
    local_out = pltpu.make_async_copy(
        wout_hbm.at[0], wcat.at[sec, :, pl.ds(3 * WIDTH, WIDTH)], w_sem.at[1]
    )
    local_qkv.start()
    local_out.start()
    pltpu.make_async_copy(og_hbm.at[sec], ogb, og_sem).start()

    barrier = pltpu.get_barrier_semaphore()

    def greet(d, carry):
        peer = lax.rem(me + d, n_row)
        pl.semaphore_signal(barrier, inc=1, device_id=(sec, peer), device_id_type=MESH)
        return carry

    lax.fori_loop(1, n_row, greet, 0)
    for d in range(1, LAYERS):
        pl.semaphore_signal(
            barrier, inc=1, device_id=(lax.rem(sec + d, LAYERS), me), device_id_type=MESH
        )

    lane = lax.broadcasted_iota(jnp.int32, (1, SEQ), 1)
    low = (lane < HEAD_DIM).astype(F32).astype(BF)
    high = (lane >= HEAD_DIM).astype(F32).astype(BF)

    gains[sec] = gain_ref[...]
    vocab = emb_ref.shape[0]
    ids = lax.broadcasted_iota(jnp.int32, (tok_ref.shape[0], vocab), 1)
    picks = (tok_ref[...] == ids).astype(F32).astype(BF)
    xs[0] = dot(picks, emb_ref[...], 1, 0)

    local_qkv.wait()

    @pl.when(sec == 0)
    def _():
        normal, _ = norm_parts(emb_ref[...].astype(F32))
        h = (normal * gain_ref[...]).astype(BF)
        for n in range(3):
            cols = pl.ds(WIDTH * n, WIDTH)
            tab[:, cols] = dot(h, wcat[0, :, cols], 1, 0).astype(BF)

    local_out.wait()
    pl.semaphore_wait(barrier, n_row - 1 + LAYERS - 1)

    def tab_copy(t):
        return pltpu.make_async_remote_copy(
            src_ref=tab,
            dst_ref=tab,
            send_sem=tab_send.at[t],
            recv_sem=tab_recv,
            device_id=(t, me),
            device_id_type=MESH,
        )

    @pl.when(sec == 0)
    def _():
        for t in range(1, LAYERS):
            tab_copy(t).start()

    def gain_copy(d):
        return pltpu.make_async_remote_copy(
            src_ref=gain_ref,
            dst_ref=gains.at[sec],
            send_sem=gain_send.at[d],
            recv_sem=gain_recv.at[d],
            device_id=(lax.rem(sec + d, LAYERS), me),
            device_id_type=MESH,
        )

    for d in range(1, LAYERS):
        gain_copy(d).start()

    def flow(l, d, k, who, first):
        rows = QUARTER // (CHUNKS_FIRST if first else CHUNKS)
        start = who * (2 * QUARTER) + d * QUARTER + k * rows
        span = pl.ds(pl.multiple_of(start, 16), rows)
        if first:
            return wcat.at[0, span, pl.ds(3 * WIDTH, WIDTH)]
        return wcat.at[l, span]

    def place(l, d):
        return lax.rem(sec - l + LAYERS, LAYERS) if d == 0 else lax.rem(l - sec + LAYERS, LAYERS)

    def ring_copy(l, d, k, first):
        step = 1 if d == 0 else LAYERS - 1
        ref = flow(l, d, k, core, first)
        return pltpu.make_async_remote_copy(
            src_ref=ref,
            dst_ref=ref,
            send_sem=ring_send.at[l, d, k],
            recv_sem=ring_recv.at[l, d, k],
            device_id=(lax.rem(sec + step, LAYERS), me),
            device_id_type=MESH,
        )

    def twin_copy(l, d, k, who, first):
        ref = flow(l, d, k, who, first)
        return pltpu.make_async_remote_copy(
            src_ref=ref,
            dst_ref=ref,
            send_sem=twin_send.at[l, d, k],
            recv_sem=twin_recv.at[l, d, k],
            device_id=(sec, partner),
            device_id_type=MESH,
        )

    def launch_flow(l, first=False):
        chunks = CHUNKS_FIRST if first else CHUNKS

        @pl.when(sec == l)
        def _():
            for k in range(chunks):
                for d in range(2):
                    ring_copy(l, d, k, first).start()

    def pump(l, slot, first=False):
        chunks = CHUNKS_FIRST if first else CHUNKS
        for d in range(2):
            at = place(l, d)
            k = slot - at

            @pl.when((at > 0) & (k >= 0) & (k < chunks))
            def _():
                ring_copy(l, d, k, first).wait_recv()

                @pl.when(at < LAYERS - 1)
                def _():
                    ring_copy(l, d, k, first).start()

                twin_copy(l, d, k, core, first).start()

    def settle(l, first=False):
        chunks = CHUNKS_FIRST if first else CHUNKS

        @pl.when(sec != l)
        def _():
            for k in range(chunks):
                for d in range(2):
                    twin_copy(l, d, k, 1 - core, first).wait_recv()

    def drain(l, first=False):
        chunks = CHUNKS_FIRST if first else CHUNKS

        def one(k, carry):
            for d in range(2):
                at = place(l, d)

                @pl.when(at < LAYERS - 1)
                def _():
                    ring_copy(l, d, k, first).wait_send()

                @pl.when(at > 0)
                def _():
                    twin_copy(l, d, k, core, first).wait_send()

            return carry

        lax.fori_loop(0, chunks, one, 0)

    def rows_of(k):
        return pl.ds(pl.multiple_of(k * piece, 16), piece)

    def split_block(a0, a1):
        top = jnp.concatenate([a0 * low, a1 * low], axis=1)
        bottom = jnp.concatenate([a0 * high, a1 * high], axis=1)
        return jnp.concatenate([top, bottom], axis=0)

    def pair_scores(left, right, factor):
        for p in range(PAIRS):
            la, ra = left(p), right(p)
            out = dot(split_block(*la), jnp.concatenate(ra, axis=1), 1, 1)
            if factor is not None:
                out = factor * out
            part[pl.ds(2 * SEQ * p, 2 * SEQ), :] = out.astype(BF)

    def rs_copy(d):
        peer = lax.rem(me + d, n_row)
        return pltpu.make_async_remote_copy(
            src_ref=part.at[rows_of(peer)],
            dst_ref=recv.at[d],
            send_sem=rs_send.at[d],
            recv_sem=rs_recv.at[d],
            device_id=(sec, peer),
            device_id_type=MESH,
        )

    def start_reduce():
        def send(d, carry):
            rs_copy(d).start()
            return carry

        lax.fori_loop(1, n_row, send, 0)

    def finish_reduce():
        def take(d, total):
            rs_copy(d).wait_recv()
            return total + recv[d].astype(F32)

        return lax.fori_loop(1, n_row, take, part[rows_of(me), :].astype(F32))

    def ag_copy(buf, d):
        peer = lax.rem(me + d, n_row)
        return pltpu.make_async_remote_copy(
            src_ref=buf.at[rows_of(me)],
            dst_ref=buf.at[rows_of(me)],
            send_sem=ag_send.at[d],
            recv_sem=ag_recv.at[d],
            device_id=(sec, peer),
            device_id_type=MESH,
        )

    def start_gather(buf):
        def send(d, carry):
            ag_copy(buf, d).start()
            return carry

        lax.fori_loop(1, n_row, send, 0)

    def finish_gather(buf):
        def take(d, carry):
            ag_copy(buf, d).wait_recv()
            rs_copy(d).wait_send()
            ag_copy(buf, d).wait_send()
            return carry

        lax.fori_loop(1, n_row, take, 0)

    def halves(ref, base, p):
        cols = pl.ds(base + SEQ * p, SEQ)
        return ref[pl.ds(0, SEQ), cols], ref[pl.ds(SEQ, SEQ), cols]

    def beside(buf, p):
        return jnp.concatenate(
            [buf[pl.ds(2 * SEQ * p, SEQ), :], buf[pl.ds(2 * SEQ * p + SEQ, SEQ), :]], axis=1
        )

    def put_halves(ref, base, p, value):
        cols = pl.ds(base + SEQ * p, SEQ)
        ref[pl.ds(0, SEQ), cols] = value[:, :SEQ]
        ref[pl.ds(SEQ, SEQ), cols] = value[:, SEQ:]

    own_rows = WIDTH // n_row

    def put_grad(u, value):
        for r in range(n_row):
            q = r // 2
            grad[u, r % 2, q // SIDE, q % SIDE] = value[own_rows * r : own_rows * (r + 1)].astype(BF)

    def pair_copy(u, par):
        return pltpu.make_async_remote_copy(
            src_ref=grad.at[u, 1 - core],
            dst_ref=pairbuf.at[par, u],
            send_sem=pair_send.at[u],
            recv_sem=pair_recv.at[par, u],
            device_id=(sec, partner),
            device_id_type=MESH,
        )

    def y_first(u):
        return u % 2 == 0

    def c1_copy(u, par, d):
        if y_first(u):
            y = lax.rem(yc + d, SIDE)
            src, peer = grad.at[u, core, :, y], row_at(zc, y)
        else:
            z = lax.rem(zc + d, SIDE)
            src, peer = grad.at[u, core, z], row_at(z, yc)
        return pltpu.make_async_remote_copy(
            src_ref=src,
            dst_ref=line1.at[par, u, d - 1],
            send_sem=c1_send.at[u, d - 1],
            recv_sem=c1_recv.at[par, u, d - 1],
            device_id=(sec, peer),
            device_id_type=MESH,
        )

    def c2_copy(u, par, d):
        if y_first(u):
            at = lax.rem(zc + d, SIDE)
            peer = row_at(at, yc)
        else:
            at = lax.rem(yc + d, SIDE)
            peer = row_at(zc, at)
        return pltpu.make_async_remote_copy(
            src_ref=sum1.at[par, u, at],
            dst_ref=line2.at[par, u, d - 1],
            send_sem=c2_send.at[u, d - 1],
            recv_sem=c2_recv.at[par, u, d - 1],
            device_id=(sec, peer),
            device_id_type=MESH,
        )

    def x_copy(u, t):
        owner = LAYERS - 1 - t
        return pltpu.make_async_remote_copy(
            src_ref=xout.at[u],
            dst_ref=xin.at[u, lax.rem(sec - owner + LAYERS - 1 + LAYERS, LAYERS)],
            send_sem=x_send.at[u],
            recv_sem=x_recv.at[u, lax.rem(sec - owner + LAYERS - 1 + LAYERS, LAYERS)],
            device_id=(owner, me),
            device_id_type=MESH,
        )

    def stage_pair(u, t):
        pair_copy(u, t % 2).start()

    def stage_one(u, t):
        par = t % 2
        pair_copy(u, par).wait_recv()
        pair_copy(u, par).wait_send()
        for z in range(SIDE):
            both = grad[u, core, z].astype(F32) + pairbuf[par, u, z].astype(F32)
            grad[u, core, z] = both.astype(BF)
        for d in range(1, SIDE):
            c1_copy(u, par, d).start()

    def stage_two(u, t):
        par = t % 2
        for d in range(1, SIDE):
            c1_copy(u, par, d).wait_recv()
            c1_copy(u, par, d).wait_send()
        for k in range(SIDE):
            own = grad[u, core, k, yc] if y_first(u) else grad[u, core, zc, k]
            total = own.astype(F32)
            for d in range(SIDE - 1):
                total = total + line1[par, u, d, k].astype(F32)
            sum1[par, u, k] = total.astype(BF)
        for d in range(1, SIDE):
            c2_copy(u, par, d).start()

    def stage_three(u, t):
        par = t % 2
        owner = LAYERS - 1 - t
        for d in range(1, SIDE):
            c2_copy(u, par, d).wait_recv()
            c2_copy(u, par, d).wait_send()
        total = sum1[par, u, zc if y_first(u) else yc].astype(F32)
        for d in range(SIDE - 1):
            total = total + line2[par, u, d].astype(F32)

        @pl.when((t > 0) & (sec != owner + 1))
        def _():
            x_copy(u, t - 1).wait_send()

        @pl.when(sec == owner)
        def _():
            fin[u] = total

        @pl.when(sec != owner)
        def _():
            xout[u] = total.astype(BF)
            x_copy(u, t).start()

    launch_flow(0, True)
    launch_flow(1)

    def forward(l, carry):
        here = qkv.at[l]

        @pl.when(l == 0)
        def _():
            @pl.when(sec > 0)
            def _():
                tab_copy(0).wait_recv()

            for d in range(1, LAYERS):
                gain_copy(d).wait_recv()
            for n in range(3):
                cols = pl.ds(WIDTH * n, WIDTH)
                here[:, cols] = dot(picks, tab[:, cols], 1, 0).astype(BF)

        @pl.when(l > 0)
        def _():
            settle(l)
            normal, _ = norm_parts(xs[l])
            h = (normal * gains[l]).astype(BF)
            for n in range(3):
                cols = pl.ds(WIDTH * n, WIDTH)
                here[:, cols] = dot(h, wcat[l, :, cols], 1, 0).astype(BF)

        pair_scores(lambda p: halves(here, 0, p), lambda p: halves(here, WIDTH, p), scale)
        start_reduce()

        @pl.when(l == 0)
        def _():
            for slot in range(1, CHUNKS_FIRST + 3):
                pump(0, slot, True)

        @pl.when((l > 0) & (l < LAYERS - 1))
        def _():
            launch_flow(l + 1)

        @pl.when(l < LAYERS - 1)
        def _():
            for slot in range(1, 5):
                pump(l + 1, slot)

        logits = finish_reduce()
        shifted = jnp.exp(logits - jnp.max(logits, axis=-1, keepdims=True))
        own = shifted / jnp.sum(shifted, axis=-1, keepdims=True)
        probs_l = probs.at[l]
        probs_l[rows_of(me), :] = own.astype(BF)
        start_gather(probs_l)

        @pl.when(l < LAYERS - 1)
        def _():
            for slot in range(5, CHUNKS + 3):
                pump(l + 1, slot)

        finish_gather(probs_l)
        mixed_l = mixed.at[l]
        for p in range(PAIRS):
            out = dot(beside(probs_l, p), split_block(*halves(here, 2 * WIDTH, p)), 1, 0)
            put_halves(mixed_l, 0, p, out.astype(BF))

        @pl.when(l == 0)
        def _():
            settle(0, True)

        @pl.when(l < LAYERS - 1)
        def _():
            xs[l + 1] = xs[l] + dot(mixed_l[...], wcat[l, :, pl.ds(3 * WIDTH, WIDTH)], 1, 0)

        return carry

    lax.fori_loop(0, LAYERS, forward, 0)

    pltpu.make_async_copy(og_hbm.at[sec], ogb, og_sem).wait()
    dyf[...] = ogb[...].astype(F32)

    def reduce_window(step):
        def previous():
            t = step - 1
            for u, n in ((QRY, 0), (KEY, 1)):
                put_grad(u, dot(hbuf[...], dqkv[:, pl.ds(WIDTH * n, WIDTH)], 0, 0))
                stage_pair(u, t)
            for u in (OUT, VAL):
                stage_one(u, t)

        def older():
            t = step - 2
            for u in (OUT, VAL):
                stage_three(u, t)
            for u in (QRY, KEY):
                stage_two(u, t)

        return older, previous

    def gather_window(step):
        def previous():
            t = step - 1
            for u in (OUT, VAL):
                stage_two(u, t)
            for u in (QRY, KEY):
                stage_one(u, t)

        def older():
            t = step - 2
            for u in (QRY, KEY):
                stage_three(u, t)

        return previous, older

    def backward(step, carry):
        l = LAYERS - 1 - step
        here = qkv.at[l]
        probs_l = probs.at[l]
        dyb = dyf[...].astype(BF)
        dmix[...] = dot(dyb, wcat[l, :, pl.ds(3 * WIDTH, WIDTH)], 1, 1).astype(BF)
        pair_scores(lambda p: halves(dmix, 0, p), lambda p: halves(here, 2 * WIDTH, p), None)
        start_reduce()

        older, previous = reduce_window(step)
        pl.when(step >= 2)(older)
        pl.when(step >= 1)(previous)
        for p in range(PAIRS):
            rows = pl.ds(2 * SEQ * p, 2 * SEQ)
            out = dot(probs_l[rows, :], split_block(*halves(dmix, 0, p)), 0, 0)
            put_halves(dqkv, 2 * WIDTH, p, out.astype(BF))
        dprobs = finish_reduce()
        own = probs_l[rows_of(me), :].astype(F32)
        inner = jnp.sum(dprobs * own, axis=-1, keepdims=True)
        dlog[rows_of(me), :] = (own * (dprobs - inner)).astype(BF)
        start_gather(dlog)

        normal, rstd = norm_parts(xs[l])
        hbuf[...] = (normal * gains[l]).astype(BF)
        vcols = pl.ds(2 * WIDTH, WIDTH)
        previous, older = gather_window(step)
        pl.when(step >= 1)(previous)
        put_grad(OUT, dot(mixed[l], dyb, 0, 0))
        put_grad(VAL, dot(hbuf[...], dqkv[:, vcols], 0, 0))
        for u in (OUT, VAL):
            stage_pair(u, step)

        @pl.when(l > 0)
        def _():
            dhacc[...] = dot(dqkv[:, vcols], wcat[l, :, vcols], 1, 1)

        pl.when(step >= 2)(older)
        finish_gather(dlog)

        for p in range(PAIRS):
            out = dot(beside(dlog, p), split_block(*halves(here, WIDTH, p)), 1, 0)
            put_halves(dqkv, 0, p, (scale * out).astype(BF))
            rows = pl.ds(2 * SEQ * p, 2 * SEQ)
            out = dot(dlog[rows, :], split_block(*halves(here, 0, p)), 0, 0)
            put_halves(dqkv, WIDTH, p, (scale * out).astype(BF))
        qk = pl.ds(0, 2 * WIDTH)

        @pl.when(l > 0)
        def _():
            dh = dhacc[...] + dot(dqkv[:, qk], wcat[l, :, qk], 1, 1)
            dn = dh.astype(BF).astype(F32) * gains[l]
            first = jnp.mean(dn, axis=-1, keepdims=True)
            second = jnp.mean(dn * normal, axis=-1, keepdims=True)
            dyf[...] = dyf[...] + rstd * (dn - first - normal * second)

        return carry

    lax.fori_loop(0, LAYERS, backward, 0)

    for work in reduce_window(LAYERS) + gather_window(LAYERS):
        work()
    reduce_window(LAYERS + 1)[0]()
    gather_window(LAYERS + 1)[1]()

    for u in range(4):

        @pl.when(sec != 0)
        def _():
            x_copy(u, LAYERS - 1).wait_send()

        total = fin[u]
        for slot in range(LAYERS - 1):
            pltpu.make_async_remote_copy(
                src_ref=xout.at[u],
                dst_ref=xin.at[u, slot],
                send_sem=x_send.at[u],
                recv_sem=x_recv.at[u, slot],
                device_id=(lax.rem(sec + 1, LAYERS), me),
                device_id_type=MESH,
            ).wait_recv()
            total = total + xin[u, slot].astype(F32)
        if u == OUT:
            go_ref[0] = total
        else:
            gq_ref[0, :, pl.ds(WIDTH * {VAL: 2, QRY: 0, KEY: 1}[u], WIDTH)] = total

    drain(0, True)
    for l in range(1, LAYERS):
        drain(l)

    @pl.when(sec == 0)
    def _():
        for t in range(1, LAYERS):
            tab_copy(t).wait_send()

    for d in range(1, LAYERS):
        gain_copy(d).wait_send()


def local(tokens, embed, ln_gain, w_qkv, w_out, out_grad):
    n_row = lax.axis_size("row")
    section = lax.axis_index("section")
    row = lax.axis_index("row")
    micro, rows_here, seq = tokens.shape
    vocab, width = embed.shape
    npos = rows_here * seq
    scale = HEAD_DIM ** (-0.5) / (rows_here * n_row) ** 0.5
    tok = lax.dynamic_index_in_dim(tokens, section, 0, keepdims=False).reshape(npos, 1)
    emb = jnp.pad(embed, ((0, -vocab % 16), (0, 0)))
    flat = HEADS * seq
    own_rows = width // n_row
    vm, anyspace = pl.BlockSpec(memory_space=pltpu.VMEM), pl.BlockSpec(memory_space=pl.ANY)
    dma = pltpu.SemaphoreType.DMA
    grad_qkv, grad_out = pl.pallas_call(
        functools.partial(kernel, n_row, scale),
        out_shape=(
            jax.ShapeDtypeStruct((1, own_rows, 3 * width), F32),
            jax.ShapeDtypeStruct((1, own_rows, width), F32),
        ),
        in_specs=[vm, vm, vm, anyspace, anyspace, anyspace],
        out_specs=(vm, vm),
        scratch_shapes=[
            pltpu.VMEM((LAYERS, width, 4 * width), BF),
            pltpu.VMEM((LAYERS, 1, width), F32),
            pltpu.VMEM((emb.shape[0], 3 * width), BF),
            pltpu.VMEM((LAYERS, npos, width), F32),
            pltpu.VMEM((LAYERS, npos, 3 * width), BF),
            pltpu.VMEM((LAYERS, flat, seq), BF),
            pltpu.VMEM((LAYERS, npos, width), BF),
            pltpu.VMEM((flat, seq), BF),
            pltpu.VMEM((n_row, flat // n_row, seq), BF),
            pltpu.VMEM((flat, seq), BF),
            pltpu.VMEM((npos, width), F32),
            pltpu.VMEM((npos, width), BF),
            pltpu.VMEM((npos, width), BF),
            pltpu.VMEM((npos, 3 * width), BF),
            pltpu.VMEM((npos, width), BF),
            pltpu.VMEM((npos, width), F32),
            pltpu.VMEM((4, 2, SIDE, SIDE, own_rows, width), BF),
            pltpu.VMEM((2, 4, SIDE, SIDE, own_rows, width), BF),
            pltpu.VMEM((2, 4, SIDE - 1, SIDE, own_rows, width), BF),
            pltpu.VMEM((2, 4, SIDE, own_rows, width), BF),
            pltpu.VMEM((2, 4, SIDE - 1, own_rows, width), BF),
            pltpu.VMEM((4, own_rows, width), BF),
            pltpu.VMEM((4, LAYERS - 1, own_rows, width), BF),
            pltpu.VMEM((4, own_rows, width), F32),
            dma((n_row,)),
            dma((n_row,)),
            dma((n_row,)),
            dma((n_row,)),
            dma((2,)),
            dma,
            dma((LAYERS,)),
            dma,
            dma((LAYERS,)),
            dma((LAYERS,)),
            dma((LAYERS, 2, CHUNKS)),
            dma((LAYERS, 2, CHUNKS)),
            dma((LAYERS, 2, CHUNKS)),
            dma((LAYERS, 2, CHUNKS)),
            dma((4,)),
            dma((2, 4)),
            dma((4, SIDE - 1)),
            dma((2, 4, SIDE - 1)),
            dma((4, SIDE - 1)),
            dma((2, 4, SIDE - 1)),
            dma((4,)),
            dma((4, LAYERS - 1)),
        ],
        compiler_params=pltpu.CompilerParams(
            collective_id=0, has_side_effects=True, vmem_limit_bytes=67043328
        ),
    )(tok, emb, ln_gain, w_qkv, w_out, out_grad.reshape(micro, npos, width))
    w_own = lax.dynamic_slice_in_dim(w_qkv[0], row * own_rows, own_rows, 0).astype(F32)
    gain_own = lax.dynamic_slice_in_dim(ln_gain[0], row * own_rows, own_rows, 0)
    grad_gain = (jnp.sum(w_own * grad_qkv[0], axis=-1) / gain_own)[None]
    return (grad_qkv, grad_out, grad_gain)


def solution(mesh):
    in_specs = (
        P(None, "row", None),
        P(),
        P("section", None),
        P("section", None, None),
        P("section", None, None),
        P(None, "row", None, None),
    )
    out_specs = (P("section", "row", None), P("section", "row", None), P("section", "row"))
    return jax.shard_map(local, mesh=mesh, in_specs=in_specs, out_specs=out_specs, check_vma=False)
```

```python
import functools

import jax
import jax.numpy as jnp
from jax import lax
from jax.experimental import pallas as pl
from jax.experimental.pallas import tpu as pltpu
from jax.sharding import PartitionSpec as P

HEADS = 12
HEAD_DIM = 64
LAYERS = 4
PAIRS = HEADS // 2
WIDTH = HEADS * HEAD_DIM
SEQ = 128
SIDE = 4
OUT, VAL, QRY, KEY = 0, 1, 2, 3
CHUNKS = 6
CHUNKS_FIRST = 2
QUARTER = WIDTH // 4
HALF = WIDTH // 2
MESH = pl.DeviceIdType.MESH
BF = jnp.bfloat16
F32 = jnp.float32


def dot(a, b, ca, cb):
    return lax.dot_general(a, b, (((ca,), (cb,)), ((), ())), preferred_element_type=F32)


def norm_parts(x):
    centred = x - jnp.mean(x, axis=-1, keepdims=True)
    spread = jnp.mean(centred * centred, axis=-1, keepdims=True)
    rstd = lax.rsqrt(spread + 1e-05)
    return centred * rstd, rstd


def kernel(
    n_row,
    scale,
    tok_ref,
    emb_ref,
    gain_ref,
    wqkv_hbm,
    wout_hbm,
    og_hbm,
    gq_ref,
    go_ref,
    wcat,
    gains,
    embp,
    tab,
    xs,
    qkv,
    probs,
    mixed,
    part,
    recv,
    dlog,
    dyf,
    ogb,
    dmix,
    dqkv,
    hbuf,
    dhacc,
    grad,
    pairbuf,
    line1,
    sum1,
    line2,
    xout,
    xin,
    fin,
    rs_send,
    rs_recv,
    ag_send,
    ag_recv,
    w_sem,
    og_sem,
    tab_send,
    tab_recv,
    gain_send,
    gain_recv,
    deal_send,
    deal_recv,
    s1_send,
    s1_recv,
    s2_send,
    s2_recv,
    join_send,
    join_recv,
    ring_send,
    ring_recv,
    twin_send,
    twin_recv,
    pair_send,
    pair_recv,
    c1_send,
    c1_recv,
    c2_send,
    c2_recv,
    x_send,
    x_recv,
):
    sec = lax.axis_index("section")
    me = lax.axis_index("row")
    piece = part.shape[0] // n_row
    core = lax.rem(me, 2)
    partner = me + 1 - 2 * core
    chip = me // 2
    zc = chip // SIDE
    yc = lax.rem(chip, SIDE)

    def row_at(z, y):
        return (z * SIDE + y) * 2 + core

    def weight(l, first, count):
        block = wcat[l, :, :, :, pl.ds(first, count)]
        return block.reshape(WIDTH, count)

    local_qkv = pltpu.make_async_copy(
        wqkv_hbm, wcat.at[sec, :, :, :, pl.ds(0, 3 * WIDTH)], w_sem.at[0]
    )
    local_out = pltpu.make_async_copy(
        wout_hbm, wcat.at[sec, :, :, :, pl.ds(3 * WIDTH, WIDTH)], w_sem.at[1]
    )
    local_qkv.start()
    local_out.start()
    pltpu.make_async_copy(og_hbm.at[sec], ogb, og_sem).start()

    barrier = pltpu.get_barrier_semaphore()

    def greet(d, carry):
        peer = lax.rem(me + d, n_row)
        pl.semaphore_signal(barrier, inc=1, device_id=(sec, peer), device_id_type=MESH)
        return carry

    lax.fori_loop(1, n_row, greet, 0)
    for d in range(1, LAYERS):
        pl.semaphore_signal(
            barrier, inc=1, device_id=(lax.rem(sec + d, LAYERS), me), device_id_type=MESH
        )

    lane = lax.broadcasted_iota(jnp.int32, (1, SEQ), 1)
    low = (lane < HEAD_DIM).astype(F32).astype(BF)
    high = (lane >= HEAD_DIM).astype(F32).astype(BF)

    gains[sec] = gain_ref[...]
    padded = embp.shape[0]
    embp[...] = jnp.zeros_like(embp)
    embp[pl.ds(0, emb_ref.shape[0]), :] = emb_ref[...]
    ids = lax.broadcasted_iota(jnp.int32, (padded, SEQ), 0)
    tok = tok_ref[sec]
    picks = jnp.concatenate([(tok[r : r + 1] == ids) for r in range(2)], axis=1)
    picks = picks.astype(F32).astype(BF)
    xs[0] = dot(picks, embp[...], 0, 0)

    local_qkv.wait()

    @pl.when(sec == 0)
    def _():
        normal, _ = norm_parts(embp[...].astype(F32))
        h = (normal * gain_ref[...]).astype(BF)
        for n in range(3):
            made = dot(h, weight(0, WIDTH * n, WIDTH), 1, 0).astype(BF)
            for half in range(2):
                cols = pl.ds(HALF * n, HALF)
                tab[half, :, cols] = made[:, HALF * half : HALF * (half + 1)]

    local_out.wait()
    pl.semaphore_wait(barrier, n_row - 1 + LAYERS - 1)

    def tab_copy(t):
        return pltpu.make_async_remote_copy(
            src_ref=tab.at[core],
            dst_ref=tab.at[core],
            send_sem=tab_send.at[t],
            recv_sem=tab_recv.at[0],
            device_id=(t, me),
            device_id_type=MESH,
        )

    def tab_twin(who):
        return pltpu.make_async_remote_copy(
            src_ref=tab.at[who],
            dst_ref=tab.at[who],
            send_sem=tab_send.at[0],
            recv_sem=tab_recv.at[1],
            device_id=(sec, partner),
            device_id_type=MESH,
        )

    @pl.when(sec == 0)
    def _():
        for t in range(1, LAYERS):
            tab_copy(t).start()

    def gain_copy(d):
        return pltpu.make_async_remote_copy(
            src_ref=gain_ref,
            dst_ref=gains.at[sec],
            send_sem=gain_send.at[d],
            recv_sem=gain_recv.at[d],
            device_id=(lax.rem(sec + d, LAYERS), me),
            device_id_type=MESH,
        )

    for d in range(1, LAYERS):
        gain_copy(d).start()

    def flow(l, d, k, who, first):
        block = who * 2 + d
        if first:
            return wcat.at[0, block, k, :, pl.ds(3 * WIDTH, WIDTH)]
        return wcat.at[l, block, k // 3, pl.ds(pl.multiple_of(lax.rem(k, 3) * 32, 16), 32)]

    def place(l, d):
        return lax.rem(sec - l + LAYERS, LAYERS) if d == 0 else lax.rem(l - sec + LAYERS, LAYERS)

    def ring_copy(l, d, k, first):
        step = 1 if d == 0 else LAYERS - 1
        ref = flow(l, d, k, core, first)
        return pltpu.make_async_remote_copy(
            src_ref=ref,
            dst_ref=ref,
            send_sem=ring_send.at[l, d, k],
            recv_sem=ring_recv.at[l, d, k],
            device_id=(lax.rem(sec + step, LAYERS), me),
            device_id_type=MESH,
        )

    def twin_copy(l, d, k, who, first):
        ref = flow(l, d, k, who, first)
        return pltpu.make_async_remote_copy(
            src_ref=ref,
            dst_ref=ref,
            send_sem=twin_send.at[l, d, k],
            recv_sem=twin_recv.at[l, d, k],
            device_id=(sec, partner),
            device_id_type=MESH,
        )

    def launch_flow(l, first=False):
        chunks = CHUNKS_FIRST if first else CHUNKS

        @pl.when(sec == l)
        def _():
            for k in range(chunks):
                for d in range(2):
                    ring_copy(l, d, k, first).start()

    def pump(l, slot, first=False):
        chunks = CHUNKS_FIRST if first else CHUNKS
        for d in range(2):
            at = place(l, d)
            k = slot - at

            @pl.when((at > 0) & (k >= 0) & (k < chunks))
            def _():
                ring_copy(l, d, k, first).wait_recv()

                @pl.when(at < LAYERS - 1)
                def _():
                    ring_copy(l, d, k, first).start()

                twin_copy(l, d, k, core, first).start()

    def settle(l, first=False):
        chunks = CHUNKS_FIRST if first else CHUNKS

        @pl.when(sec != l)
        def _():
            for k in range(chunks):
                for d in range(2):
                    twin_copy(l, d, k, 1 - core, first).wait_recv()

    def drain(l, first=False):
        chunks = CHUNKS_FIRST if first else CHUNKS

        def one(k, carry):
            for d in range(2):
                at = place(l, d)

                @pl.when(at < LAYERS - 1)
                def _():
                    ring_copy(l, d, k, first).wait_send()

                @pl.when(at > 0)
                def _():
                    twin_copy(l, d, k, core, first).wait_send()

            return carry

        lax.fori_loop(0, chunks, one, 0)

    block_cols = pl.ds(pl.multiple_of((core * SIDE + yc) * HALF, 128), HALF)

    def side_cols(who):
        return pl.ds(pl.multiple_of(who * (2 * WIDTH), 128), 2 * WIDTH)

    def deal_copy(d):
        ref = wcat.at[1, zc, :, :, block_cols]
        return pltpu.make_async_remote_copy(
            src_ref=ref,
            dst_ref=ref,
            send_sem=deal_send.at[d],
            recv_sem=deal_recv,
            device_id=(lax.rem(1 + d, LAYERS), me),
            device_id_type=MESH,
        )

    def line_copy(stage, half, d):
        along_y = (stage + half) % 2 == 0
        y = lax.rem(yc + d, SIDE) if along_y else yc
        z = zc if along_y else lax.rem(zc + d, SIDE)
        if stage == 0:
            ref = wcat.at[1, zc, half, :, block_cols]
        elif along_y:
            ref = wcat.at[1, :, half, :, block_cols]
        else:
            ref = wcat.at[1, zc, half, :, side_cols(core)]
        send, take = (s1_send, s1_recv) if stage == 0 else (s2_send, s2_recv)
        return pltpu.make_async_remote_copy(
            src_ref=ref,
            dst_ref=ref,
            send_sem=send.at[half, d - 1],
            recv_sem=take.at[half, d - 1],
            device_id=(sec, row_at(z, y)),
            device_id_type=MESH,
        )

    def join_copy(half, who):
        ref = wcat.at[1, :, half, :, side_cols(who)]
        return pltpu.make_async_remote_copy(
            src_ref=ref,
            dst_ref=ref,
            send_sem=join_send.at[half],
            recv_sem=join_recv.at[half],
            device_id=(sec, partner),
            device_id_type=MESH,
        )

    def plane_one():
        @pl.when(sec != 1)
        def _():
            deal_copy(0).wait_recv()
            for half in range(2):
                for d in range(1, SIDE):
                    line_copy(0, half, d).start()

    def plane_two():
        @pl.when(sec != 1)
        def _():
            for half in range(2):
                for d in range(1, SIDE):
                    line_copy(0, half, d).wait_recv()
                for d in range(1, SIDE):
                    line_copy(1, half, d).start()

    def plane_three():
        @pl.when(sec != 1)
        def _():
            for half in range(2):
                for d in range(1, SIDE):
                    line_copy(1, half, d).wait_recv()
                join_copy(half, core).start()

    def plane_settle():
        @pl.when(sec != 1)
        def _():
            for half in range(2):
                join_copy(half, 1 - core).wait_recv()

    def plane_drain():
        @pl.when(sec != 1)
        def _():
            for half in range(2):
                for d in range(1, SIDE):
                    line_copy(0, half, d).wait_send()
                    line_copy(1, half, d).wait_send()
                join_copy(half, core).wait_send()

        @pl.when(sec == 1)
        def _():
            for d in range(1, LAYERS):
                deal_copy(d).wait_send()

    def rows_of(k):
        return pl.ds(pl.multiple_of(k * piece, 16), piece)

    def split_block(a0, a1):
        top = jnp.concatenate([a0 * low, a1 * low], axis=1)
        bottom = jnp.concatenate([a0 * high, a1 * high], axis=1)
        return jnp.concatenate([top, bottom], axis=0)

    def pair_scores(left, right, factor):
        for p in range(PAIRS):
            la, ra = left(p), right(p)
            out = dot(split_block(*la), jnp.concatenate(ra, axis=1), 1, 1)
            if factor is not None:
                out = factor * out
            part[pl.ds(2 * SEQ * p, 2 * SEQ), :] = out.astype(BF)

    def rs_copy(d):
        peer = lax.rem(me + d, n_row)
        return pltpu.make_async_remote_copy(
            src_ref=part.at[rows_of(peer)],
            dst_ref=recv.at[d],
            send_sem=rs_send.at[d],
            recv_sem=rs_recv.at[d],
            device_id=(sec, peer),
            device_id_type=MESH,
        )

    def start_reduce():
        def send(d, carry):
            rs_copy(d).start()
            return carry

        lax.fori_loop(1, n_row, send, 0)

    def finish_reduce():
        def take(d, total):
            rs_copy(d).wait_recv()
            return total + recv[d].astype(F32)

        return lax.fori_loop(1, n_row, take, part[rows_of(me), :].astype(F32))

    def ag_copy(buf, d):
        peer = lax.rem(me + d, n_row)
        return pltpu.make_async_remote_copy(
            src_ref=buf.at[rows_of(me)],
            dst_ref=buf.at[rows_of(me)],
            send_sem=ag_send.at[d],
            recv_sem=ag_recv.at[d],
            device_id=(sec, peer),
            device_id_type=MESH,
        )

    def start_gather(buf):
        def send(d, carry):
            ag_copy(buf, d).start()
            return carry

        lax.fori_loop(1, n_row, send, 0)

    def finish_gather(buf):
        def take(d, carry):
            ag_copy(buf, d).wait_recv()
            rs_copy(d).wait_send()
            ag_copy(buf, d).wait_send()
            return carry

        lax.fori_loop(1, n_row, take, 0)

    def halves(ref, base, p):
        cols = pl.ds(base + SEQ * p, SEQ)
        return ref[pl.ds(0, SEQ), cols], ref[pl.ds(SEQ, SEQ), cols]

    def beside(buf, p):
        return jnp.concatenate(
            [buf[pl.ds(2 * SEQ * p, SEQ), :], buf[pl.ds(2 * SEQ * p + SEQ, SEQ), :]], axis=1
        )

    def put_halves(ref, base, p, value):
        cols = pl.ds(base + SEQ * p, SEQ)
        ref[pl.ds(0, SEQ), cols] = value[:, :SEQ]
        ref[pl.ds(SEQ, SEQ), cols] = value[:, SEQ:]

    own_rows = WIDTH // n_row

    def put_grad(u, value):
        for r in range(n_row):
            q = r // 2
            grad[u, r % 2, q // SIDE, q % SIDE] = value[own_rows * r : own_rows * (r + 1)].astype(BF)

    def pair_copy(u, par):
        return pltpu.make_async_remote_copy(
            src_ref=grad.at[u, 1 - core],
            dst_ref=pairbuf.at[par, u],
            send_sem=pair_send.at[u],
            recv_sem=pair_recv.at[par, u],
            device_id=(sec, partner),
            device_id_type=MESH,
        )

    def y_first(u):
        return u % 2 == 0

    def c1_copy(u, par, d):
        if y_first(u):
            y = lax.rem(yc + d, SIDE)
            src, peer = grad.at[u, core, :, y], row_at(zc, y)
        else:
            z = lax.rem(zc + d, SIDE)
            src, peer = grad.at[u, core, z], row_at(z, yc)
        return pltpu.make_async_remote_copy(
            src_ref=src,
            dst_ref=line1.at[par, u, d - 1],
            send_sem=c1_send.at[u, d - 1],
            recv_sem=c1_recv.at[par, u, d - 1],
            device_id=(sec, peer),
            device_id_type=MESH,
        )

    def c2_copy(u, par, d):
        if y_first(u):
            at = lax.rem(zc + d, SIDE)
            peer = row_at(at, yc)
        else:
            at = lax.rem(yc + d, SIDE)
            peer = row_at(zc, at)
        return pltpu.make_async_remote_copy(
            src_ref=sum1.at[par, u, at],
            dst_ref=line2.at[par, u, d - 1],
            send_sem=c2_send.at[u, d - 1],
            recv_sem=c2_recv.at[par, u, d - 1],
            device_id=(sec, peer),
            device_id_type=MESH,
        )

    def x_copy(u, t):
        owner = LAYERS - 1 - t
        return pltpu.make_async_remote_copy(
            src_ref=xout.at[u],
            dst_ref=xin.at[u, lax.rem(sec - owner + LAYERS - 1 + LAYERS, LAYERS)],
            send_sem=x_send.at[u],
            recv_sem=x_recv.at[u, lax.rem(sec - owner + LAYERS - 1 + LAYERS, LAYERS)],
            device_id=(owner, me),
            device_id_type=MESH,
        )

    def stage_pair(u, t):
        pair_copy(u, t % 2).start()

    def stage_one(u, t):
        par = t % 2
        pair_copy(u, par).wait_recv()
        pair_copy(u, par).wait_send()
        for z in range(SIDE):
            both = grad[u, core, z].astype(F32) + pairbuf[par, u, z].astype(F32)
            grad[u, core, z] = both.astype(BF)
        for d in range(1, SIDE):
            c1_copy(u, par, d).start()

    def stage_two(u, t):
        par = t % 2
        for d in range(1, SIDE):
            c1_copy(u, par, d).wait_recv()
            c1_copy(u, par, d).wait_send()
        for k in range(SIDE):
            own = grad[u, core, k, yc] if y_first(u) else grad[u, core, zc, k]
            total = own.astype(F32)
            for d in range(SIDE - 1):
                total = total + line1[par, u, d, k].astype(F32)
            sum1[par, u, k] = total.astype(BF)
        for d in range(1, SIDE):
            c2_copy(u, par, d).start()

    def stage_three(u, t):
        par = t % 2
        owner = LAYERS - 1 - t
        for d in range(1, SIDE):
            c2_copy(u, par, d).wait_recv()
            c2_copy(u, par, d).wait_send()
        total = sum1[par, u, zc if y_first(u) else yc].astype(F32)
        for d in range(SIDE - 1):
            total = total + line2[par, u, d].astype(F32)

        @pl.when((t > 0) & (sec != owner + 1))
        def _():
            x_copy(u, t - 1).wait_send()

        @pl.when(sec == owner)
        def _():
            fin[u] = total

        @pl.when(sec != owner)
        def _():
            xout[u] = total.astype(BF)
            x_copy(u, t).start()

    @pl.when(sec == 1)
    def _():
        for d in range(1, LAYERS):
            deal_copy(d).start()

    launch_flow(0, True)
    launch_flow(2)

    def forward(l, carry):
        here = qkv.at[l]

        @pl.when(l == 0)
        def _():
            @pl.when(sec > 0)
            def _():
                tab_copy(0).wait_recv()
                tab_twin(core).start()
                tab_twin(1 - core).wait_recv()

            for d in range(1, LAYERS):
                gain_copy(d).wait_recv()
            for n in range(3):
                for half in range(2):
                    made = dot(picks, tab[half, :, pl.ds(HALF * n, HALF)], 0, 0)
                    here[:, pl.ds(WIDTH * n + HALF * half, HALF)] = made.astype(BF)

        @pl.when(l > 0)
        def _():
            pl.when(l == 1)(plane_settle)
            pl.when(l > 1)(lambda: settle(l))
            normal, _ = norm_parts(xs[l])
            h = (normal * gains[l]).astype(BF)
            for n in range(3):
                cols = pl.ds(WIDTH * n, WIDTH)
                here[:, cols] = dot(h, weight(l, WIDTH * n, WIDTH), 1, 0).astype(BF)

        pair_scores(lambda p: halves(here, 0, p), lambda p: halves(here, WIDTH, p), scale)
        start_reduce()

        @pl.when(l == 0)
        def _():
            plane_one()
            for slot in range(1, CHUNKS_FIRST + 3):
                pump(0, slot, True)
            for slot in range(1, 4):
                pump(2, slot)

        @pl.when(l == 1)
        def _():
            for slot in range(7, CHUNKS + 3):
                pump(2, slot)

        @pl.when(l == 2)
        def _():
            for slot in range(4, 7):
                pump(3, slot)

        logits = finish_reduce()
        shifted = jnp.exp(logits - jnp.max(logits, axis=-1, keepdims=True))
        own = shifted / jnp.sum(shifted, axis=-1, keepdims=True)
        probs_l = probs.at[l]
        probs_l[rows_of(me), :] = own.astype(BF)
        start_gather(probs_l)

        @pl.when(l == 0)
        def _():
            plane_two()
            for slot in range(4, 7):
                pump(2, slot)
            launch_flow(3)

        @pl.when(l == 1)
        def _():
            for slot in range(1, 4):
                pump(3, slot)

        @pl.when(l == 2)
        def _():
            for slot in range(7, CHUNKS + 3):
                pump(3, slot)

        finish_gather(probs_l)
        mixed_l = mixed.at[l]
        for p in range(PAIRS):
            out = dot(beside(probs_l, p), split_block(*halves(here, 2 * WIDTH, p)), 1, 0)
            put_halves(mixed_l, 0, p, out.astype(BF))

        @pl.when(l == 0)
        def _():
            plane_three()
            settle(0, True)

        @pl.when(l < LAYERS - 1)
        def _():
            xs[l + 1] = xs[l] + dot(mixed_l[...], weight(l, 3 * WIDTH, WIDTH), 1, 0)

        return carry

    lax.fori_loop(0, LAYERS, forward, 0)

    pltpu.make_async_copy(og_hbm.at[sec], ogb, og_sem).wait()
    dyf[...] = ogb[...].astype(F32)

    def reduce_window(step):
        def previous():
            t = step - 1
            for u, n in ((QRY, 0), (KEY, 1)):
                put_grad(u, dot(hbuf[...], dqkv[:, pl.ds(WIDTH * n, WIDTH)], 0, 0))
                stage_pair(u, t)
            for u in (OUT, VAL):
                stage_one(u, t)

        def older():
            t = step - 2
            for u in (OUT, VAL):
                stage_three(u, t)
            for u in (QRY, KEY):
                stage_two(u, t)

        return older, previous

    def gather_window(step):
        def previous():
            t = step - 1
            for u in (OUT, VAL):
                stage_two(u, t)
            for u in (QRY, KEY):
                stage_one(u, t)

        def older():
            t = step - 2
            for u in (QRY, KEY):
                stage_three(u, t)

        return previous, older

    def backward(step, carry):
        l = LAYERS - 1 - step
        here = qkv.at[l]
        probs_l = probs.at[l]
        dyb = dyf[...].astype(BF)
        dmix[...] = dot(dyb, weight(l, 3 * WIDTH, WIDTH), 1, 1).astype(BF)
        pair_scores(lambda p: halves(dmix, 0, p), lambda p: halves(here, 2 * WIDTH, p), None)
        start_reduce()

        older, previous = reduce_window(step)
        pl.when(step >= 2)(older)
        pl.when(step >= 1)(previous)
        for p in range(PAIRS):
            rows = pl.ds(2 * SEQ * p, 2 * SEQ)
            out = dot(probs_l[rows, :], split_block(*halves(dmix, 0, p)), 0, 0)
            put_halves(dqkv, 2 * WIDTH, p, out.astype(BF))
        dprobs = finish_reduce()
        own = probs_l[rows_of(me), :].astype(F32)
        inner = jnp.sum(dprobs * own, axis=-1, keepdims=True)
        dlog[rows_of(me), :] = (own * (dprobs - inner)).astype(BF)
        start_gather(dlog)

        normal, rstd = norm_parts(xs[l])
        hbuf[...] = (normal * gains[l]).astype(BF)
        vcols = pl.ds(2 * WIDTH, WIDTH)
        previous, older = gather_window(step)
        pl.when(step >= 1)(previous)
        put_grad(OUT, dot(mixed[l], dyb, 0, 0))
        put_grad(VAL, dot(hbuf[...], dqkv[:, vcols], 0, 0))
        for u in (OUT, VAL):
            stage_pair(u, step)

        @pl.when(l > 0)
        def _():
            dhacc[...] = dot(dqkv[:, vcols], weight(l, 2 * WIDTH, WIDTH), 1, 1)

        pl.when(step >= 2)(older)
        finish_gather(dlog)

        for p in range(PAIRS):
            out = dot(beside(dlog, p), split_block(*halves(here, WIDTH, p)), 1, 0)
            put_halves(dqkv, 0, p, (scale * out).astype(BF))
            rows = pl.ds(2 * SEQ * p, 2 * SEQ)
            out = dot(dlog[rows, :], split_block(*halves(here, 0, p)), 0, 0)
            put_halves(dqkv, WIDTH, p, (scale * out).astype(BF))
        qk = pl.ds(0, 2 * WIDTH)

        @pl.when(l > 0)
        def _():
            dh = dhacc[...] + dot(dqkv[:, qk], weight(l, 0, 2 * WIDTH), 1, 1)
            dn = dh.astype(BF).astype(F32) * gains[l]
            first = jnp.mean(dn, axis=-1, keepdims=True)
            second = jnp.mean(dn * normal, axis=-1, keepdims=True)
            dyf[...] = dyf[...] + rstd * (dn - first - normal * second)

        return carry

    lax.fori_loop(0, LAYERS, backward, 0)

    for work in reduce_window(LAYERS) + gather_window(LAYERS):
        work()
    reduce_window(LAYERS + 1)[0]()
    gather_window(LAYERS + 1)[1]()

    for u in range(4):

        @pl.when(sec != 0)
        def _():
            x_copy(u, LAYERS - 1).wait_send()

        total = fin[u]
        for slot in range(LAYERS - 1):
            pltpu.make_async_remote_copy(
                src_ref=xout.at[u],
                dst_ref=xin.at[u, slot],
                send_sem=x_send.at[u],
                recv_sem=x_recv.at[u, slot],
                device_id=(lax.rem(sec + 1, LAYERS), me),
                device_id_type=MESH,
            ).wait_recv()
            total = total + xin[u, slot].astype(F32)
        if u == OUT:
            go_ref[0] = total
        else:
            gq_ref[0, :, pl.ds(WIDTH * {VAL: 2, QRY: 0, KEY: 1}[u], WIDTH)] = total

    drain(0, True)
    for l in range(2, LAYERS):
        drain(l)
    plane_drain()

    @pl.when(sec == 0)
    def _():
        for t in range(1, LAYERS):
            tab_copy(t).wait_send()

    @pl.when(sec > 0)
    def _():
        tab_twin(core).wait_send()

    for d in range(1, LAYERS):
        gain_copy(d).wait_send()


def local(tokens, embed, ln_gain, w_qkv, w_out, out_grad):
    n_row = lax.axis_size("row")
    row = lax.axis_index("row")
    micro, rows_here, seq = tokens.shape
    vocab, width = embed.shape
    npos = rows_here * seq
    scale = HEAD_DIM ** (-0.5) / (rows_here * n_row) ** 0.5
    padded = vocab + -vocab % 16
    flat = HEADS * seq
    own_rows = width // n_row
    vm, anyspace = pl.BlockSpec(memory_space=pltpu.VMEM), pl.BlockSpec(memory_space=pl.ANY)
    dma = pltpu.SemaphoreType.DMA
    grad_qkv, grad_out = pl.pallas_call(
        functools.partial(kernel, n_row, scale),
        out_shape=(
            jax.ShapeDtypeStruct((1, own_rows, 3 * width), F32),
            jax.ShapeDtypeStruct((1, own_rows, width), F32),
        ),
        in_specs=[vm, vm, vm, anyspace, anyspace, anyspace],
        out_specs=(vm, vm),
        scratch_shapes=[
            pltpu.VMEM((LAYERS, SIDE, 2, width // 8, 4 * width), BF),
            pltpu.VMEM((LAYERS, 1, width), F32),
            pltpu.VMEM((padded, width), BF),
            pltpu.VMEM((2, padded, 3 * width // 2), BF),
            pltpu.VMEM((LAYERS, npos, width), F32),
            pltpu.VMEM((LAYERS, npos, 3 * width), BF),
            pltpu.VMEM((LAYERS, flat, seq), BF),
            pltpu.VMEM((LAYERS, npos, width), BF),
            pltpu.VMEM((flat, seq), BF),
            pltpu.VMEM((n_row, flat // n_row, seq), BF),
            pltpu.VMEM((flat, seq), BF),
            pltpu.VMEM((npos, width), F32),
            pltpu.VMEM((npos, width), BF),
            pltpu.VMEM((npos, width), BF),
            pltpu.VMEM((npos, 3 * width), BF),
            pltpu.VMEM((npos, width), BF),
            pltpu.VMEM((npos, width), F32),
            pltpu.VMEM((4, 2, SIDE, SIDE, own_rows, width), BF),
            pltpu.VMEM((2, 4, SIDE, SIDE, own_rows, width), BF),
            pltpu.VMEM((2, 4, SIDE - 1, SIDE, own_rows, width), BF),
            pltpu.VMEM((2, 4, SIDE, own_rows, width), BF),
            pltpu.VMEM((2, 4, SIDE - 1, own_rows, width), BF),
            pltpu.VMEM((4, own_rows, width), BF),
            pltpu.VMEM((4, LAYERS - 1, own_rows, width), BF),
            pltpu.VMEM((4, own_rows, width), F32),
            dma((n_row,)),
            dma((n_row,)),
            dma((n_row,)),
            dma((n_row,)),
            dma((2,)),
            dma,
            dma((LAYERS,)),
            dma((2,)),
            dma((LAYERS,)),
            dma((LAYERS,)),
            dma((LAYERS,)),
            dma,
            dma((2, SIDE - 1)),
            dma((2, SIDE - 1)),
            dma((2, SIDE - 1)),
            dma((2, SIDE - 1)),
            dma((2,)),
            dma((2,)),
            dma((LAYERS, 2, CHUNKS)),
            dma((LAYERS, 2, CHUNKS)),
            dma((LAYERS, 2, CHUNKS)),
            dma((LAYERS, 2, CHUNKS)),
            dma((4,)),
            dma((2, 4)),
            dma((4, SIDE - 1)),
            dma((2, 4, SIDE - 1)),
            dma((4, SIDE - 1)),
            dma((2, 4, SIDE - 1)),
            dma((4,)),
            dma((4, LAYERS - 1)),
        ],
        compiler_params=pltpu.CompilerParams(
            collective_id=0, has_side_effects=True, vmem_limit_bytes=67043328
        ),
    )(
        tokens,
        embed,
        ln_gain,
        w_qkv.reshape(SIDE, 2, width // 8, 3 * width),
        w_out.reshape(SIDE, 2, width // 8, width),
        out_grad.reshape(micro, npos, width),
    )
    w_own = lax.dynamic_slice_in_dim(w_qkv[0], row * own_rows, own_rows, 0).astype(F32)
    gain_own = lax.dynamic_slice_in_dim(ln_gain[0], row * own_rows, own_rows, 0)
    grad_gain = (jnp.sum(w_own * grad_qkv[0], axis=-1) / gain_own)[None]
    return (grad_qkv, grad_out, grad_gain)


def solution(mesh):
    in_specs = (
        P(None, "row", None),
        P(),
        P("section", None),
        P("section", None, None),
        P("section", None, None),
        P(None, "row", None, None),
    )
    out_specs = (P("section", "row", None), P("section", "row", None), P("section", "row"))
    return jax.shard_map(local, mesh=mesh, in_specs=in_specs, out_specs=out_specs, check_vma=False)
```

```python
import functools

import jax
import jax.numpy as jnp
from jax import lax
from jax.experimental import pallas as pl
from jax.experimental.pallas import tpu as pltpu
from jax.sharding import PartitionSpec as P

HEADS = 12
HEAD_DIM = 64
LAYERS = 4
PAIRS = HEADS // 2
WIDTH = HEADS * HEAD_DIM
SEQ = 128
SIDE = 4
OUT, VAL, QRY, KEY = 0, 1, 2, 3
CHUNKS = 3
CHUNK = 4 * WIDTH // CHUNKS
HALF = WIDTH // 2
MESH = pl.DeviceIdType.MESH
BF = jnp.bfloat16
F32 = jnp.float32


def dot(a, b, ca, cb):
    return lax.dot_general(a, b, (((ca,), (cb,)), ((), ())), preferred_element_type=F32)


def norm_parts(x):
    centred = x - jnp.mean(x, axis=-1, keepdims=True)
    spread = jnp.mean(centred * centred, axis=-1, keepdims=True)
    rstd = lax.rsqrt(spread + 1e-05)
    return centred * rstd, rstd


def kernel(
    n_row,
    scale,
    tok_ref,
    emb_ref,
    gain_ref,
    wqkv_hbm,
    wout_hbm,
    og_hbm,
    gq_ref,
    go_ref,
    wcat,
    gains,
    embp,
    tab,
    xs,
    qkv,
    probs,
    mixed,
    part,
    other,
    both,
    recv,
    dlog,
    dyf,
    ogb,
    dmix,
    dqkv,
    hbuf,
    dhacc,
    grad,
    pairbuf,
    line1,
    sum1,
    line2,
    xout,
    xin,
    fin,
    level_sem,
    rs_send,
    rs_recv,
    ag_send,
    ag_recv,
    hand_send,
    hand_recv,
    w_sem,
    og_sem,
    tab_send,
    tab_recv,
    gain_send,
    gain_recv,
    deal_send,
    deal_recv,
    s1_send,
    s1_recv,
    s2_send,
    s2_recv,
    join_send,
    join_recv,
    ring_send,
    ring_recv,
    twin_send,
    twin_recv,
    first_send,
    first_recv,
    pair_send,
    pair_recv,
    c1_send,
    c1_recv,
    c2_send,
    c2_recv,
    x_send,
    x_recv,
):
    sec = lax.axis_index("section")
    me = lax.axis_index("row")
    piece = part.shape[0] // n_row
    n_chip = n_row // 2
    core = lax.rem(me, 2)
    partner = me + 1 - 2 * core
    chip = me // 2
    zc = chip // SIDE
    yc = lax.rem(chip, SIDE)

    def row_at(z, y):
        return (z * SIDE + y) * 2 + core

    def weight(l, first, count):
        block = wcat[l, :, :, :, pl.ds(first, count)]
        return block.reshape(WIDTH, count)

    local_qkv = pltpu.make_async_copy(
        wqkv_hbm, wcat.at[sec, :, :, :, pl.ds(0, 3 * WIDTH)], w_sem.at[0]
    )
    local_out = pltpu.make_async_copy(
        wout_hbm, wcat.at[sec, :, :, :, pl.ds(3 * WIDTH, WIDTH)], w_sem.at[1]
    )
    local_qkv.start()
    local_out.start()
    pltpu.make_async_copy(og_hbm.at[sec], ogb, og_sem).start()

    barrier = pltpu.get_barrier_semaphore()

    def greet(d, carry):
        peer = 2 * lax.rem(chip + d, n_chip) + core
        pl.semaphore_signal(barrier, inc=1, device_id=(sec, peer), device_id_type=MESH)
        return carry

    lax.fori_loop(1, n_chip, greet, 0)
    pl.semaphore_signal(barrier, inc=1, device_id=(sec, partner), device_id_type=MESH)
    for d in range(1, LAYERS):
        pl.semaphore_signal(
            barrier, inc=1, device_id=(lax.rem(sec + d, LAYERS), me), device_id_type=MESH
        )

    lane = lax.broadcasted_iota(jnp.int32, (1, SEQ), 1)
    low = (lane < HEAD_DIM).astype(F32).astype(BF)
    high = (lane >= HEAD_DIM).astype(F32).astype(BF)

    gains[sec] = gain_ref[...]
    padded = embp.shape[0]
    embp[...] = jnp.zeros_like(embp)
    embp[pl.ds(0, emb_ref.shape[0]), :] = emb_ref[...]
    ids = lax.broadcasted_iota(jnp.int32, (padded, SEQ), 0)
    tok = tok_ref[sec]
    picks = jnp.concatenate([(tok[r : r + 1] == ids) for r in range(2)], axis=1)
    picks = picks.astype(F32).astype(BF)
    xs[0] = dot(picks, embp[...], 0, 0)

    local_qkv.wait()

    @pl.when(sec == 0)
    def _():
        normal, _ = norm_parts(embp[...].astype(F32))
        h = (normal * gain_ref[...]).astype(BF)
        for n in range(3):
            made = dot(h, weight(0, WIDTH * n, WIDTH), 1, 0).astype(BF)
            for half in range(2):
                cols = pl.ds(HALF * n, HALF)
                tab[half, :, cols] = made[:, HALF * half : HALF * (half + 1)]

    local_out.wait()
    pl.semaphore_wait(barrier, n_chip + LAYERS - 1)

    def tab_copy(t):
        return pltpu.make_async_remote_copy(
            src_ref=tab.at[core],
            dst_ref=tab.at[core],
            send_sem=tab_send.at[t],
            recv_sem=tab_recv.at[0],
            device_id=(t, me),
            device_id_type=MESH,
        )

    def tab_twin(who):
        return pltpu.make_async_remote_copy(
            src_ref=tab.at[who],
            dst_ref=tab.at[who],
            send_sem=tab_send.at[0],
            recv_sem=tab_recv.at[1],
            device_id=(sec, partner),
            device_id_type=MESH,
        )

    @pl.when(sec == 0)
    def _():
        for t in range(1, LAYERS):
            tab_copy(t).start()

    def gain_copy(d):
        return pltpu.make_async_remote_copy(
            src_ref=gain_ref,
            dst_ref=gains.at[sec],
            send_sem=gain_send.at[d],
            recv_sem=gain_recv.at[d],
            device_id=(lax.rem(sec + d, LAYERS), me),
            device_id_type=MESH,
        )

    for d in range(1, LAYERS):
        gain_copy(d).start()

    RING = LAYERS - 1

    def flow(d, k, who):
        cols = pl.ds(pl.multiple_of(k * CHUNK, 128), CHUNK)
        return wcat.at[RING, who * 2 + d, :, :, cols]

    def place(d):
        return lax.rem(sec - RING + LAYERS, LAYERS) if d == 0 else lax.rem(RING - sec, LAYERS)

    def ring_copy(d, k):
        step = 1 if d == 0 else LAYERS - 1
        ref = flow(d, k, core)
        return pltpu.make_async_remote_copy(
            src_ref=ref,
            dst_ref=ref,
            send_sem=ring_send.at[d, k],
            recv_sem=ring_recv.at[d, k],
            device_id=(lax.rem(sec + step, LAYERS), me),
            device_id_type=MESH,
        )

    def twin_copy(d, k, who):
        ref = flow(d, k, who)
        return pltpu.make_async_remote_copy(
            src_ref=ref,
            dst_ref=ref,
            send_sem=twin_send.at[d, k],
            recv_sem=twin_recv.at[d, k],
            device_id=(sec, partner),
            device_id_type=MESH,
        )

    def launch_flow():
        @pl.when(sec == RING)
        def _():
            for k in range(CHUNKS):
                for d in range(2):
                    ring_copy(d, k).start()

    def pump(slot):
        for d in range(2):
            at = place(d)
            k = slot - at

            @pl.when((at > 0) & (k >= 0) & (k < CHUNKS))
            def _():
                ring_copy(d, k).wait_recv()

                @pl.when(at < LAYERS - 1)
                def _():
                    ring_copy(d, k).start()

                twin_copy(d, k, core).start()

    def settle():
        @pl.when(sec != RING)
        def _():
            for k in range(CHUNKS):
                for d in range(2):
                    twin_copy(d, k, 1 - core).wait_recv()

    def drain():
        def one(k, carry):
            for d in range(2):
                at = place(d)

                @pl.when(at < LAYERS - 1)
                def _():
                    ring_copy(d, k).wait_send()

                @pl.when(at > 0)
                def _():
                    twin_copy(d, k, core).wait_send()

            return carry

        lax.fori_loop(0, CHUNKS, one, 0)

    def first_ref(who):
        return wcat.at[0, pl.ds(2 * who, 2), :, :, pl.ds(3 * WIDTH, WIDTH)]

    def first_copy(t):
        return pltpu.make_async_remote_copy(
            src_ref=first_ref(core),
            dst_ref=first_ref(core),
            send_sem=first_send.at[t],
            recv_sem=first_recv.at[0],
            device_id=(t, me),
            device_id_type=MESH,
        )

    def first_twin(who):
        return pltpu.make_async_remote_copy(
            src_ref=first_ref(who),
            dst_ref=first_ref(who),
            send_sem=first_send.at[0],
            recv_sem=first_recv.at[1],
            device_id=(sec, partner),
            device_id_type=MESH,
        )

    block_cols = pl.ds(pl.multiple_of((core * SIDE + yc) * HALF, 128), HALF)

    def side_cols(who):
        return pl.ds(pl.multiple_of(who * (2 * WIDTH), 128), 2 * WIDTH)

    def deal_copy(w, d):
        ref = wcat.at[w, zc, :, :, block_cols]
        return pltpu.make_async_remote_copy(
            src_ref=ref,
            dst_ref=ref,
            send_sem=deal_send.at[w - 1, d],
            recv_sem=deal_recv.at[w - 1],
            device_id=((w + d) % LAYERS, me),
            device_id_type=MESH,
        )

    def line_copy(w, stage, half, d):
        along_y = (stage + half) % 2 == 0
        y = lax.rem(yc + d, SIDE) if along_y else yc
        z = zc if along_y else lax.rem(zc + d, SIDE)
        if stage == 0:
            ref = wcat.at[w, zc, half, :, block_cols]
        elif along_y:
            ref = wcat.at[w, :, half, :, block_cols]
        else:
            ref = wcat.at[w, zc, half, :, side_cols(core)]
        send, take = (s1_send, s1_recv) if stage == 0 else (s2_send, s2_recv)
        return pltpu.make_async_remote_copy(
            src_ref=ref,
            dst_ref=ref,
            send_sem=send.at[w - 1, half, d - 1],
            recv_sem=take.at[w - 1, half, d - 1],
            device_id=(sec, row_at(z, y)),
            device_id_type=MESH,
        )

    def join_copy(w, half, who):
        ref = wcat.at[w, :, half, :, side_cols(who)]
        return pltpu.make_async_remote_copy(
            src_ref=ref,
            dst_ref=ref,
            send_sem=join_send.at[w - 1, half],
            recv_sem=join_recv.at[w - 1, half],
            device_id=(sec, partner),
            device_id_type=MESH,
        )

    def plane_one(w):
        @pl.when(sec != w)
        def _():
            deal_copy(w, 0).wait_recv()
            for half in range(2):
                for d in range(1, SIDE):
                    line_copy(w, 0, half, d).start()

    def plane_two(w, half):
        @pl.when(sec != w)
        def _():
            for d in range(1, SIDE):
                line_copy(w, 0, half, d).wait_recv()
            for d in range(1, SIDE):
                line_copy(w, 1, half, d).start()

    def plane_three(w, half):
        @pl.when(sec != w)
        def _():
            for d in range(1, SIDE):
                line_copy(w, 1, half, d).wait_recv()
            join_copy(w, half, core).start()

    def plane_settle(w):
        @pl.when(sec != w)
        def _():
            for half in range(2):
                join_copy(w, half, 1 - core).wait_recv()

    def plane_drain(w):
        @pl.when(sec != w)
        def _():
            for half in range(2):
                for d in range(1, SIDE):
                    line_copy(w, 0, half, d).wait_send()
                    line_copy(w, 1, half, d).wait_send()
                join_copy(w, half, core).wait_send()

        @pl.when(sec == w)
        def _():
            for d in range(1, LAYERS):
                deal_copy(w, d).wait_send()

    def rows_of(k):
        return pl.ds(pl.multiple_of(k * piece, 16), piece)

    def half_rows(who):
        return pl.ds(pl.multiple_of(who * (n_chip * piece), 16), n_chip * piece)

    own_block = rows_of(core * n_chip + chip)

    def split_block(a0, a1):
        top = jnp.concatenate([a0 * low, a1 * low], axis=1)
        bottom = jnp.concatenate([a0 * high, a1 * high], axis=1)
        return jnp.concatenate([top, bottom], axis=0)

    def pair_scores(left, right, factor):
        for p in range(PAIRS):
            la, ra = left(p), right(p)
            out = dot(split_block(*la), jnp.concatenate(ra, axis=1), 1, 1)
            if factor is not None:
                out = factor * out
            part[pl.ds(2 * SEQ * p, 2 * SEQ), :] = out.astype(BF)

    def level_copy():
        return pltpu.make_async_remote_copy(
            src_ref=part.at[half_rows(1 - core)],
            dst_ref=other,
            send_sem=level_sem.at[0],
            recv_sem=level_sem.at[1],
            device_id=(sec, partner),
            device_id_type=MESH,
        )

    def rs_copy(d):
        to = lax.rem(chip + d, n_chip)
        return pltpu.make_async_remote_copy(
            src_ref=both.at[rows_of(to)],
            dst_ref=recv.at[d],
            send_sem=rs_send.at[d],
            recv_sem=rs_recv.at[d],
            device_id=(sec, 2 * to + core),
            device_id_type=MESH,
        )

    def start_reduce():
        level_copy().start()
        mine = part[half_rows(core), :].astype(F32)
        level_copy().wait_recv()
        both[...] = (mine + other[...].astype(F32)).astype(BF)

        def send(d, carry):
            rs_copy(d).start()
            return carry

        lax.fori_loop(1, n_chip, send, 0)

    def finish_reduce():
        def take(d, total):
            rs_copy(d).wait_recv()
            return total + recv[d].astype(F32)

        return lax.fori_loop(1, n_chip, take, both[rows_of(chip), :].astype(F32))

    def ag_copy(buf, d):
        to = lax.rem(chip + d, n_chip)
        return pltpu.make_async_remote_copy(
            src_ref=buf.at[own_block],
            dst_ref=buf.at[own_block],
            send_sem=ag_send.at[d],
            recv_sem=ag_recv.at[d],
            device_id=(sec, 2 * to + core),
            device_id_type=MESH,
        )

    def hand_copy(buf, d):
        block = rows_of(core * n_chip + lax.rem(chip + n_chip - d, n_chip))
        return pltpu.make_async_remote_copy(
            src_ref=buf.at[block],
            dst_ref=buf.at[block],
            send_sem=hand_send.at[d],
            recv_sem=hand_recv.at[d],
            device_id=(sec, partner),
            device_id_type=MESH,
        )

    def start_gather(buf):
        def send(d, carry):
            ag_copy(buf, d).start()
            return carry

        lax.fori_loop(1, n_chip, send, 0)
        hand_copy(buf, 0).start()

    def finish_gather(buf):
        def take(d, carry):
            ag_copy(buf, d).wait_recv()
            hand_copy(buf, d).start()
            return carry

        lax.fori_loop(1, n_chip, take, 0)

        def settle_one(d, carry):
            hand_copy(buf, d).wait_recv()
            hand_copy(buf, d).wait_send()
            return carry

        lax.fori_loop(0, n_chip, settle_one, 0)

        def sent(d, carry):
            rs_copy(d).wait_send()
            ag_copy(buf, d).wait_send()
            return carry

        lax.fori_loop(1, n_chip, sent, 0)
        level_copy().wait_send()

    def halves(ref, base, p):
        cols = pl.ds(base + SEQ * p, SEQ)
        return ref[pl.ds(0, SEQ), cols], ref[pl.ds(SEQ, SEQ), cols]

    def beside(buf, p):
        return jnp.concatenate(
            [buf[pl.ds(2 * SEQ * p, SEQ), :], buf[pl.ds(2 * SEQ * p + SEQ, SEQ), :]], axis=1
        )

    def put_halves(ref, base, p, value):
        cols = pl.ds(base + SEQ * p, SEQ)
        ref[pl.ds(0, SEQ), cols] = value[:, :SEQ]
        ref[pl.ds(SEQ, SEQ), cols] = value[:, SEQ:]

    own_rows = WIDTH // n_row

    def put_grad(u, value):
        for r in range(n_row):
            q = r // 2
            grad[u, r % 2, q // SIDE, q % SIDE] = value[own_rows * r : own_rows * (r + 1)].astype(BF)

    def pair_copy(u, par):
        return pltpu.make_async_remote_copy(
            src_ref=grad.at[u, 1 - core],
            dst_ref=pairbuf.at[par, u],
            send_sem=pair_send.at[u],
            recv_sem=pair_recv.at[par, u],
            device_id=(sec, partner),
            device_id_type=MESH,
        )

    def y_first(u):
        return u % 2 == 0

    def c1_copy(u, par, d):
        if y_first(u):
            y = lax.rem(yc + d, SIDE)
            src, peer = grad.at[u, core, :, y], row_at(zc, y)
        else:
            z = lax.rem(zc + d, SIDE)
            src, peer = grad.at[u, core, z], row_at(z, yc)
        return pltpu.make_async_remote_copy(
            src_ref=src,
            dst_ref=line1.at[par, u, d - 1],
            send_sem=c1_send.at[u, d - 1],
            recv_sem=c1_recv.at[par, u, d - 1],
            device_id=(sec, peer),
            device_id_type=MESH,
        )

    def c2_copy(u, par, d):
        if y_first(u):
            at = lax.rem(zc + d, SIDE)
            peer = row_at(at, yc)
        else:
            at = lax.rem(yc + d, SIDE)
            peer = row_at(zc, at)
        return pltpu.make_async_remote_copy(
            src_ref=sum1.at[par, u, at],
            dst_ref=line2.at[par, u, d - 1],
            send_sem=c2_send.at[u, d - 1],
            recv_sem=c2_recv.at[par, u, d - 1],
            device_id=(sec, peer),
            device_id_type=MESH,
        )

    def x_copy(u, t):
        owner = LAYERS - 1 - t
        return pltpu.make_async_remote_copy(
            src_ref=xout.at[u],
            dst_ref=xin.at[u, lax.rem(sec - owner + LAYERS - 1 + LAYERS, LAYERS)],
            send_sem=x_send.at[u],
            recv_sem=x_recv.at[u, lax.rem(sec - owner + LAYERS - 1 + LAYERS, LAYERS)],
            device_id=(owner, me),
            device_id_type=MESH,
        )

    def stage_pair(u, t):
        pair_copy(u, t % 2).start()

    def stage_one(u, t):
        par = t % 2
        pair_copy(u, par).wait_recv()
        pair_copy(u, par).wait_send()
        for z in range(SIDE):
            total = grad[u, core, z].astype(F32) + pairbuf[par, u, z].astype(F32)
            grad[u, core, z] = total.astype(BF)
        for d in range(1, SIDE):
            c1_copy(u, par, d).start()

    def stage_two(u, t):
        par = t % 2
        for d in range(1, SIDE):
            c1_copy(u, par, d).wait_recv()
            c1_copy(u, par, d).wait_send()
        for k in range(SIDE):
            own = grad[u, core, k, yc] if y_first(u) else grad[u, core, zc, k]
            total = own.astype(F32)
            for d in range(SIDE - 1):
                total = total + line1[par, u, d, k].astype(F32)
            sum1[par, u, k] = total.astype(BF)
        for d in range(1, SIDE):
            c2_copy(u, par, d).start()

    def stage_three(u, t):
        par = t % 2
        owner = LAYERS - 1 - t
        for d in range(1, SIDE):
            c2_copy(u, par, d).wait_recv()
            c2_copy(u, par, d).wait_send()
        total = sum1[par, u, zc if y_first(u) else yc].astype(F32)
        for d in range(SIDE - 1):
            total = total + line2[par, u, d].astype(F32)

        @pl.when((t > 0) & (sec != owner + 1))
        def _():
            x_copy(u, t - 1).wait_send()

        @pl.when(sec == owner)
        def _():
            fin[u] = total

        @pl.when(sec != owner)
        def _():
            xout[u] = total.astype(BF)
            x_copy(u, t).start()

    for w in (1, 2):

        @pl.when(sec == w)
        def _():
            for d in range(1, LAYERS):
                deal_copy(w, d).start()

    @pl.when(sec == 0)
    def _():
        for t in (1, 3, 2):
            first_copy(t).start()

    launch_flow()

    def forward(l, carry):
        here = qkv.at[l]

        @pl.when(l == 0)
        def _():
            @pl.when(sec > 0)
            def _():
                tab_copy(0).wait_recv()
                tab_twin(core).start()
                tab_twin(1 - core).wait_recv()

            for d in range(1, LAYERS):
                gain_copy(d).wait_recv()
            for n in range(3):
                for half in range(2):
                    made = dot(picks, tab[half, :, pl.ds(HALF * n, HALF)], 0, 0)
                    here[:, pl.ds(WIDTH * n + HALF * half, HALF)] = made.astype(BF)

        @pl.when(l > 0)
        def _():
            for w in (1, 2):
                pl.when(l == w)(functools.partial(plane_settle, w))
            pl.when(l == RING)(settle)
            normal, _ = norm_parts(xs[l])
            h = (normal * gains[l]).astype(BF)
            for n in range(3):
                cols = pl.ds(WIDTH * n, WIDTH)
                here[:, cols] = dot(h, weight(l, WIDTH * n, WIDTH), 1, 0).astype(BF)

        pair_scores(lambda p: halves(here, 0, p), lambda p: halves(here, WIDTH, p), scale)
        start_reduce()

        @pl.when(l == 0)
        def _():
            plane_one(1)
            plane_two(1, 0)

        @pl.when(l == 1)
        def _():
            plane_two(2, 0)

        for turn in range(3):
            pl.when(l == turn)(functools.partial(pump, 2 * turn + 1))

        logits = finish_reduce()
        shifted = jnp.exp(logits - jnp.max(logits, axis=-1, keepdims=True))
        own = shifted / jnp.sum(shifted, axis=-1, keepdims=True)
        probs_l = probs.at[l]
        probs_l[own_block, :] = own.astype(BF)
        start_gather(probs_l)

        @pl.when(l == 0)
        def _():
            plane_two(1, 1)

        @pl.when(l == 1)
        def _():
            plane_two(2, 1)

        for turn in range(2):
            pl.when(l == turn)(functools.partial(pump, 2 * turn + 2))

        finish_gather(probs_l)
        mixed_l = mixed.at[l]
        for p in range(PAIRS):
            out = dot(beside(probs_l, p), split_block(*halves(here, 2 * WIDTH, p)), 1, 0)
            put_halves(mixed_l, 0, p, out.astype(BF))

        @pl.when(l == 0)
        def _():
            @pl.when(sec > 0)
            def _():
                first_copy(0).wait_recv()
                first_twin(core).start()

            plane_three(1, 0)

            @pl.when(sec > 0)
            def _():
                first_twin(1 - core).wait_recv()

        @pl.when(l == 1)
        def _():
            plane_three(2, 0)

        @pl.when(l < LAYERS - 1)
        def _():
            xs[l + 1] = xs[l] + dot(mixed_l[...], weight(l, 3 * WIDTH, WIDTH), 1, 0)

        @pl.when(l == 0)
        def _():
            plane_three(1, 1)
            plane_one(2)

        @pl.when(l == 1)
        def _():
            plane_three(2, 1)

        return carry

    lax.fori_loop(0, LAYERS, forward, 0)

    pltpu.make_async_copy(og_hbm.at[sec], ogb, og_sem).wait()
    dyf[...] = ogb[...].astype(F32)

    def reduce_window(step):
        def previous():
            t = step - 1
            for u, n in ((QRY, 0), (KEY, 1)):
                put_grad(u, dot(hbuf[...], dqkv[:, pl.ds(WIDTH * n, WIDTH)], 0, 0))
                stage_pair(u, t)
            for u in (OUT, VAL):
                stage_one(u, t)

        def older():
            t = step - 2
            for u in (OUT, VAL):
                stage_three(u, t)
            for u in (QRY, KEY):
                stage_two(u, t)

        return older, previous

    def gather_window(step):
        def previous():
            t = step - 1
            for u in (OUT, VAL):
                stage_two(u, t)
            for u in (QRY, KEY):
                stage_one(u, t)

        def older():
            t = step - 2
            for u in (QRY, KEY):
                stage_three(u, t)

        return previous, older

    def backward(step, carry):
        l = LAYERS - 1 - step
        here = qkv.at[l]
        probs_l = probs.at[l]
        dyb = dyf[...].astype(BF)
        dmix[...] = dot(dyb, weight(l, 3 * WIDTH, WIDTH), 1, 1).astype(BF)
        pair_scores(lambda p: halves(dmix, 0, p), lambda p: halves(here, 2 * WIDTH, p), None)
        start_reduce()

        older, previous = reduce_window(step)
        pl.when(step >= 2)(older)
        pl.when(step >= 1)(previous)
        for p in range(PAIRS):
            rows = pl.ds(2 * SEQ * p, 2 * SEQ)
            out = dot(probs_l[rows, :], split_block(*halves(dmix, 0, p)), 0, 0)
            put_halves(dqkv, 2 * WIDTH, p, out.astype(BF))
        dprobs = finish_reduce()
        own = probs_l[own_block, :].astype(F32)
        inner = jnp.sum(dprobs * own, axis=-1, keepdims=True)
        dlog[own_block, :] = (own * (dprobs - inner)).astype(BF)
        start_gather(dlog)

        normal, rstd = norm_parts(xs[l])
        hbuf[...] = (normal * gains[l]).astype(BF)
        vcols = pl.ds(2 * WIDTH, WIDTH)
        previous, older = gather_window(step)
        pl.when(step >= 1)(previous)
        put_grad(OUT, dot(mixed[l], dyb, 0, 0))
        put_grad(VAL, dot(hbuf[...], dqkv[:, vcols], 0, 0))
        for u in (OUT, VAL):
            stage_pair(u, step)

        @pl.when(l > 0)
        def _():
            dhacc[...] = dot(dqkv[:, vcols], weight(l, 2 * WIDTH, WIDTH), 1, 1)

        pl.when(step >= 2)(older)
        finish_gather(dlog)

        for p in range(PAIRS):
            out = dot(beside(dlog, p), split_block(*halves(here, WIDTH, p)), 1, 0)
            put_halves(dqkv, 0, p, (scale * out).astype(BF))
            rows = pl.ds(2 * SEQ * p, 2 * SEQ)
            out = dot(dlog[rows, :], split_block(*halves(here, 0, p)), 0, 0)
            put_halves(dqkv, WIDTH, p, (scale * out).astype(BF))
        qk = pl.ds(0, 2 * WIDTH)

        @pl.when(l > 0)
        def _():
            dh = dhacc[...] + dot(dqkv[:, qk], weight(l, 0, 2 * WIDTH), 1, 1)
            dn = dh.astype(BF).astype(F32) * gains[l]
            first = jnp.mean(dn, axis=-1, keepdims=True)
            second = jnp.mean(dn * normal, axis=-1, keepdims=True)
            dyf[...] = dyf[...] + rstd * (dn - first - normal * second)

        return carry

    lax.fori_loop(0, LAYERS, backward, 0)

    for work in reduce_window(LAYERS) + gather_window(LAYERS):
        work()
    reduce_window(LAYERS + 1)[0]()
    gather_window(LAYERS + 1)[1]()

    for u in range(4):

        @pl.when(sec != 0)
        def _():
            x_copy(u, LAYERS - 1).wait_send()

        total = fin[u]
        for slot in range(LAYERS - 1):
            pltpu.make_async_remote_copy(
                src_ref=xout.at[u],
                dst_ref=xin.at[u, slot],
                send_sem=x_send.at[u],
                recv_sem=x_recv.at[u, slot],
                device_id=(lax.rem(sec + 1, LAYERS), me),
                device_id_type=MESH,
            ).wait_recv()
            total = total + xin[u, slot].astype(F32)
        if u == OUT:
            go_ref[0] = total
        else:
            gq_ref[0, :, pl.ds(WIDTH * {VAL: 2, QRY: 0, KEY: 1}[u], WIDTH)] = total

    drain()
    for w in (1, 2):
        plane_drain(w)

    @pl.when(sec == 0)
    def _():
        for t in range(1, LAYERS):
            tab_copy(t).wait_send()
            first_copy(t).wait_send()

    @pl.when(sec > 0)
    def _():
        tab_twin(core).wait_send()
        first_twin(core).wait_send()

    for d in range(1, LAYERS):
        gain_copy(d).wait_send()


def local(tokens, embed, ln_gain, w_qkv, w_out, out_grad):
    n_row = lax.axis_size("row")
    row = lax.axis_index("row")
    micro, rows_here, seq = tokens.shape
    vocab, width = embed.shape
    npos = rows_here * seq
    scale = HEAD_DIM ** (-0.5) / (rows_here * n_row) ** 0.5
    padded = vocab + -vocab % 16
    flat = HEADS * seq
    own_rows = width // n_row
    vm, anyspace = pl.BlockSpec(memory_space=pltpu.VMEM), pl.BlockSpec(memory_space=pl.ANY)
    dma = pltpu.SemaphoreType.DMA
    grad_qkv, grad_out = pl.pallas_call(
        functools.partial(kernel, n_row, scale),
        out_shape=(
            jax.ShapeDtypeStruct((1, own_rows, 3 * width), F32),
            jax.ShapeDtypeStruct((1, own_rows, width), F32),
        ),
        in_specs=[vm, vm, vm, anyspace, anyspace, anyspace],
        out_specs=(vm, vm),
        scratch_shapes=[
            pltpu.VMEM((LAYERS, SIDE, 2, width // 8, 4 * width), BF),
            pltpu.VMEM((LAYERS, 1, width), F32),
            pltpu.VMEM((padded, width), BF),
            pltpu.VMEM((2, padded, 3 * width // 2), BF),
            pltpu.VMEM((LAYERS, npos, width), F32),
            pltpu.VMEM((LAYERS, npos, 3 * width), BF),
            pltpu.VMEM((LAYERS, flat, seq), BF),
            pltpu.VMEM((LAYERS, npos, width), BF),
            pltpu.VMEM((flat, seq), BF),
            pltpu.VMEM((flat // 2, seq), BF),
            pltpu.VMEM((flat // 2, seq), BF),
            pltpu.VMEM((n_row // 2, flat // n_row, seq), BF),
            pltpu.VMEM((flat, seq), BF),
            pltpu.VMEM((npos, width), F32),
            pltpu.VMEM((npos, width), BF),
            pltpu.VMEM((npos, width), BF),
            pltpu.VMEM((npos, 3 * width), BF),
            pltpu.VMEM((npos, width), BF),
            pltpu.VMEM((npos, width), F32),
            pltpu.VMEM((4, 2, SIDE, SIDE, own_rows, width), BF),
            pltpu.VMEM((2, 4, SIDE, SIDE, own_rows, width), BF),
            pltpu.VMEM((2, 4, SIDE - 1, SIDE, own_rows, width), BF),
            pltpu.VMEM((2, 4, SIDE, own_rows, width), BF),
            pltpu.VMEM((2, 4, SIDE - 1, own_rows, width), BF),
            pltpu.VMEM((4, own_rows, width), BF),
            pltpu.VMEM((4, LAYERS - 1, own_rows, width), BF),
            pltpu.VMEM((4, own_rows, width), F32),
            dma((2,)),
            dma((n_row // 2,)),
            dma((n_row // 2,)),
            dma((n_row // 2,)),
            dma((n_row // 2,)),
            dma((n_row // 2,)),
            dma((n_row // 2,)),
            dma((2,)),
            dma,
            dma((LAYERS,)),
            dma((2,)),
            dma((LAYERS,)),
            dma((LAYERS,)),
            dma((2, LAYERS)),
            dma((2,)),
            dma((2, 2, SIDE - 1)),
            dma((2, 2, SIDE - 1)),
            dma((2, 2, SIDE - 1)),
            dma((2, 2, SIDE - 1)),
            dma((2, 2)),
            dma((2, 2)),
            dma((2, CHUNKS)),
            dma((2, CHUNKS)),
            dma((2, CHUNKS)),
            dma((2, CHUNKS)),
            dma((LAYERS,)),
            dma((2,)),
            dma((4,)),
            dma((2, 4)),
            dma((4, SIDE - 1)),
            dma((2, 4, SIDE - 1)),
            dma((4, SIDE - 1)),
            dma((2, 4, SIDE - 1)),
            dma((4,)),
            dma((4, LAYERS - 1)),
        ],
        compiler_params=pltpu.CompilerParams(
            collective_id=0, has_side_effects=True, vmem_limit_bytes=67043328
        ),
    )(
        tokens,
        embed,
        ln_gain,
        w_qkv.reshape(SIDE, 2, width // 8, 3 * width),
        w_out.reshape(SIDE, 2, width // 8, width),
        out_grad.reshape(micro, npos, width),
    )
    w_own = lax.dynamic_slice_in_dim(w_qkv[0], row * own_rows, own_rows, 0).astype(F32)
    gain_own = lax.dynamic_slice_in_dim(ln_gain[0], row * own_rows, own_rows, 0)
    grad_gain = (jnp.sum(w_own * grad_qkv[0], axis=-1) / gain_own)[None]
    return (grad_qkv, grad_out, grad_gain)


def solution(mesh):
    in_specs = (
        P(None, "row", None),
        P(),
        P("section", None),
        P("section", None, None),
        P("section", None, None),
        P(None, "row", None, None),
    )
    out_specs = (P("section", "row", None), P("section", "row", None), P("section", "row"))
    return jax.shard_map(local, mesh=mesh, in_specs=in_specs, out_specs=out_specs, check_vma=False)
```

```python
import functools

import jax
import jax.numpy as jnp
from jax import lax
from jax.experimental import pallas as pl
from jax.experimental.pallas import tpu as pltpu
from jax.sharding import PartitionSpec as P

HEADS = 12
HEAD_DIM = 64
LAYERS = 4
PAIRS = HEADS // 2
WIDTH = HEADS * HEAD_DIM
SEQ = 128
SIDE = 4
OUT, VAL, QRY, KEY = 0, 1, 2, 3
CHUNKS = 3
CHUNK = 4 * WIDTH // CHUNKS
HALF = WIDTH // 2
MESH = pl.DeviceIdType.MESH
BF = jnp.bfloat16
F32 = jnp.float32


def dot(a, b, ca, cb):
    return lax.dot_general(a, b, (((ca,), (cb,)), ((), ())), preferred_element_type=F32)


def norm_parts(x):
    centred = x - jnp.mean(x, axis=-1, keepdims=True)
    spread = jnp.mean(centred * centred, axis=-1, keepdims=True)
    rstd = lax.rsqrt(spread + 1e-05)
    return centred * rstd, rstd


def kernel(
    n_row,
    scale,
    tok_ref,
    emb_ref,
    gain_ref,
    wqkv_hbm,
    wout_hbm,
    og_hbm,
    gq_ref,
    go_ref,
    gg_ref,
    wcat,
    gains,
    embp,
    tab,
    xs,
    qkv,
    probs,
    mixed,
    part,
    other,
    both,
    recv,
    dlog,
    dyf,
    ogb,
    dmix,
    dqkv,
    hbuf,
    dhacc,
    grad,
    pairbuf,
    line1,
    sum1,
    line2,
    xout,
    xin,
    fin,
    level_sem,
    rs_send,
    rs_recv,
    ag_send,
    ag_recv,
    hand_send,
    hand_recv,
    w_sem,
    og_sem,
    tab_send,
    tab_recv,
    gain_send,
    gain_recv,
    deal_send,
    deal_recv,
    bulk_send,
    bulk_recv,
    s1_send,
    s1_recv,
    s2_send,
    s2_recv,
    join_send,
    join_recv,
    ring_send,
    ring_recv,
    twin_send,
    twin_recv,
    first_send,
    first_recv,
    pair_send,
    pair_recv,
    c1_send,
    c1_recv,
    c2_send,
    c2_recv,
    x_send,
    x_recv,
):
    sec = lax.axis_index("section")
    me = lax.axis_index("row")
    piece = part.shape[0] // n_row
    n_chip = n_row // 2
    core = lax.rem(me, 2)
    partner = me + 1 - 2 * core
    chip = me // 2
    zc = chip // SIDE
    yc = lax.rem(chip, SIDE)

    def row_at(z, y):
        return (z * SIDE + y) * 2 + core

    def weight(l, first, count):
        block = wcat[l, :, :, :, pl.ds(first, count)]
        return block.reshape(WIDTH, count)

    local_qkv = pltpu.make_async_copy(
        wqkv_hbm, wcat.at[sec, :, :, :, pl.ds(0, 3 * WIDTH)], w_sem.at[0]
    )
    local_out = pltpu.make_async_copy(
        wout_hbm, wcat.at[sec, :, :, :, pl.ds(3 * WIDTH, WIDTH)], w_sem.at[1]
    )
    local_qkv.start()
    local_out.start()
    pltpu.make_async_copy(og_hbm.at[sec], ogb, og_sem).start()

    barrier = pltpu.get_barrier_semaphore()

    def greet(d, carry):
        peer = 2 * lax.rem(chip + d, n_chip) + core
        pl.semaphore_signal(barrier, inc=1, device_id=(sec, peer), device_id_type=MESH)
        return carry

    lax.fori_loop(1, n_chip, greet, 0)
    pl.semaphore_signal(barrier, inc=1, device_id=(sec, partner), device_id_type=MESH)
    for d in range(1, LAYERS):
        pl.semaphore_signal(
            barrier, inc=1, device_id=(lax.rem(sec + d, LAYERS), me), device_id_type=MESH
        )

    lane = lax.broadcasted_iota(jnp.int32, (1, SEQ), 1)
    low = (lane < HEAD_DIM).astype(F32).astype(BF)
    high = (lane >= HEAD_DIM).astype(F32).astype(BF)

    gains[sec] = gain_ref[...]
    padded = embp.shape[0]
    embp[...] = jnp.zeros_like(embp)
    embp[pl.ds(0, emb_ref.shape[0]), :] = emb_ref[...]
    ids = lax.broadcasted_iota(jnp.int32, (padded, SEQ), 0)
    tok = tok_ref[sec]
    picks = jnp.concatenate([(tok[r : r + 1] == ids) for r in range(2)], axis=1)
    picks = picks.astype(F32).astype(BF)
    xs[0] = dot(picks, embp[...], 0, 0)

    local_qkv.wait()

    @pl.when(sec == 0)
    def _():
        normal, _ = norm_parts(embp[...].astype(F32))
        h = (normal * gain_ref[...]).astype(BF)
        for n in range(3):
            made = dot(h, weight(0, WIDTH * n, WIDTH), 1, 0).astype(BF)
            for half in range(2):
                cols = pl.ds(HALF * n, HALF)
                tab[half, :, cols] = made[:, HALF * half : HALF * (half + 1)]

    local_out.wait()
    pl.semaphore_wait(barrier, n_chip + LAYERS - 1)

    def tab_copy(t):
        return pltpu.make_async_remote_copy(
            src_ref=tab.at[core],
            dst_ref=tab.at[core],
            send_sem=tab_send.at[t],
            recv_sem=tab_recv.at[0],
            device_id=(t, me),
            device_id_type=MESH,
        )

    def tab_twin(who):
        return pltpu.make_async_remote_copy(
            src_ref=tab.at[who],
            dst_ref=tab.at[who],
            send_sem=tab_send.at[0],
            recv_sem=tab_recv.at[1],
            device_id=(sec, partner),
            device_id_type=MESH,
        )

    @pl.when(sec == 0)
    def _():
        for t in range(1, LAYERS):
            tab_copy(t).start()

    def gain_copy(d):
        return pltpu.make_async_remote_copy(
            src_ref=gain_ref,
            dst_ref=gains.at[sec],
            send_sem=gain_send.at[d],
            recv_sem=gain_recv.at[d],
            device_id=(lax.rem(sec + d, LAYERS), me),
            device_id_type=MESH,
        )

    for d in range(1, LAYERS):
        gain_copy(d).start()

    RING = LAYERS - 1

    def flow(d, k, who):
        cols = pl.ds(pl.multiple_of(k * CHUNK, 128), CHUNK)
        return wcat.at[RING, who * 2 + d, :, :, cols]

    def place(d):
        return lax.rem(sec - RING + LAYERS, LAYERS) if d == 0 else lax.rem(RING - sec, LAYERS)

    def ring_copy(d, k):
        step = 1 if d == 0 else LAYERS - 1
        ref = flow(d, k, core)
        return pltpu.make_async_remote_copy(
            src_ref=ref,
            dst_ref=ref,
            send_sem=ring_send.at[d, k],
            recv_sem=ring_recv.at[d, k],
            device_id=(lax.rem(sec + step, LAYERS), me),
            device_id_type=MESH,
        )

    def twin_copy(d, k, who):
        ref = flow(d, k, who)
        return pltpu.make_async_remote_copy(
            src_ref=ref,
            dst_ref=ref,
            send_sem=twin_send.at[d, k],
            recv_sem=twin_recv.at[d, k],
            device_id=(sec, partner),
            device_id_type=MESH,
        )

    def launch_flow():
        @pl.when(sec == RING)
        def _():
            for k in range(CHUNKS):
                for d in range(2):
                    ring_copy(d, k).start()

    def pump(slot):
        for d in range(2):
            at = place(d)
            k = slot - at

            @pl.when((at > 0) & (k >= 0) & (k < CHUNKS))
            def _():
                ring_copy(d, k).wait_recv()

                @pl.when(at < LAYERS - 1)
                def _():
                    ring_copy(d, k).start()

                twin_copy(d, k, core).start()

    def settle():
        @pl.when(sec != RING)
        def _():
            for k in range(CHUNKS):
                for d in range(2):
                    twin_copy(d, k, 1 - core).wait_recv()

    def drain():
        def one(k, carry):
            for d in range(2):
                at = place(d)

                @pl.when(at < LAYERS - 1)
                def _():
                    ring_copy(d, k).wait_send()

                @pl.when(at > 0)
                def _():
                    twin_copy(d, k, core).wait_send()

            return carry

        lax.fori_loop(0, CHUNKS, one, 0)

    def first_ref(who):
        return wcat.at[0, pl.ds(2 * who, 2), :, :, pl.ds(3 * WIDTH, WIDTH)]

    def first_copy(t):
        return pltpu.make_async_remote_copy(
            src_ref=first_ref(core),
            dst_ref=first_ref(core),
            send_sem=first_send.at[t],
            recv_sem=first_recv.at[0],
            device_id=(t, me),
            device_id_type=MESH,
        )

    def first_twin(who):
        return pltpu.make_async_remote_copy(
            src_ref=first_ref(who),
            dst_ref=first_ref(who),
            send_sem=first_send.at[0],
            recv_sem=first_recv.at[1],
            device_id=(sec, partner),
            device_id_type=MESH,
        )

    block_cols = pl.ds(pl.multiple_of((core * SIDE + yc) * HALF, 128), HALF)

    def side_cols(who):
        return pl.ds(pl.multiple_of(who * (2 * WIDTH), 128), 2 * WIDTH)

    def deal_copy(w, d):
        halves_sent = 2 if w == 1 else 1
        ref = wcat.at[w, zc, pl.ds(0, halves_sent), :, block_cols]
        return pltpu.make_async_remote_copy(
            src_ref=ref,
            dst_ref=ref,
            send_sem=deal_send.at[w - 1, d],
            recv_sem=deal_recv.at[w - 1],
            device_id=((w + d) % LAYERS, me),
            device_id_type=MESH,
        )

    def bulk_copy(d):
        ref = wcat.at[2, :, 1, :, side_cols(core)]
        return pltpu.make_async_remote_copy(
            src_ref=ref,
            dst_ref=ref,
            send_sem=bulk_send.at[d],
            recv_sem=bulk_recv,
            device_id=((2 + d) % LAYERS, me),
            device_id_type=MESH,
        )

    def line_copy(w, stage, half, d):
        along_y = (stage + half) % 2 == 0
        y = lax.rem(yc + d, SIDE) if along_y else yc
        z = zc if along_y else lax.rem(zc + d, SIDE)
        if stage == 0:
            ref = wcat.at[w, zc, half, :, block_cols]
        elif along_y:
            ref = wcat.at[w, :, half, :, block_cols]
        else:
            ref = wcat.at[w, zc, half, :, side_cols(core)]
        send, take = (s1_send, s1_recv) if stage == 0 else (s2_send, s2_recv)
        return pltpu.make_async_remote_copy(
            src_ref=ref,
            dst_ref=ref,
            send_sem=send.at[w - 1, half, d - 1],
            recv_sem=take.at[w - 1, half, d - 1],
            device_id=(sec, row_at(z, y)),
            device_id_type=MESH,
        )

    def join_copy(w, half, who):
        ref = wcat.at[w, :, half, :, side_cols(who)]
        return pltpu.make_async_remote_copy(
            src_ref=ref,
            dst_ref=ref,
            send_sem=join_send.at[w - 1, half],
            recv_sem=join_recv.at[w - 1, half],
            device_id=(sec, partner),
            device_id_type=MESH,
        )

    def plane_one(w):
        @pl.when(sec != w)
        def _():
            deal_copy(w, 0).wait_recv()
            for half in range(2 if w == 1 else 1):
                for d in range(1, SIDE):
                    line_copy(w, 0, half, d).start()

    def plane_two(w, half):
        @pl.when(sec != w)
        def _():
            for d in range(1, SIDE):
                line_copy(w, 0, half, d).wait_recv()
            for d in range(1, SIDE):
                line_copy(w, 1, half, d).start()

    def plane_three(w, half):
        @pl.when(sec != w)
        def _():
            if w == 2 and half == 1:
                bulk_copy(0).wait_recv()
            else:
                for d in range(1, SIDE):
                    line_copy(w, 1, half, d).wait_recv()
            join_copy(w, half, core).start()

    def plane_settle(w):
        @pl.when(sec != w)
        def _():
            for half in range(2):
                join_copy(w, half, 1 - core).wait_recv()

    def plane_drain(w):
        @pl.when(sec != w)
        def _():
            for half in range(2):
                for d in range(1, SIDE):
                    if w == 1 or half == 0:
                        line_copy(w, 0, half, d).wait_send()
                        line_copy(w, 1, half, d).wait_send()
                join_copy(w, half, core).wait_send()

        @pl.when(sec == w)
        def _():
            for d in range(1, LAYERS):
                deal_copy(w, d).wait_send()
                if w == 2:
                    bulk_copy(d).wait_send()

    def rows_of(k):
        return pl.ds(pl.multiple_of(k * piece, 16), piece)

    def half_rows(who):
        return pl.ds(pl.multiple_of(who * (n_chip * piece), 16), n_chip * piece)

    own_block = rows_of(core * n_chip + chip)

    def split_block(a0, a1):
        top = jnp.concatenate([a0 * low, a1 * low], axis=1)
        bottom = jnp.concatenate([a0 * high, a1 * high], axis=1)
        return jnp.concatenate([top, bottom], axis=0)

    def pair_scores(left, right, factor):
        for p in range(PAIRS):
            la, ra = left(p), right(p)
            out = dot(split_block(*la), jnp.concatenate(ra, axis=1), 1, 1)
            if factor is not None:
                out = factor * out
            part[pl.ds(2 * SEQ * p, 2 * SEQ), :] = out.astype(BF)

    def level_copy():
        return pltpu.make_async_remote_copy(
            src_ref=part.at[half_rows(1 - core)],
            dst_ref=other,
            send_sem=level_sem.at[0],
            recv_sem=level_sem.at[1],
            device_id=(sec, partner),
            device_id_type=MESH,
        )

    def rs_copy(d):
        to = lax.rem(chip + d, n_chip)
        return pltpu.make_async_remote_copy(
            src_ref=both.at[rows_of(to)],
            dst_ref=recv.at[d],
            send_sem=rs_send.at[d],
            recv_sem=rs_recv.at[d],
            device_id=(sec, 2 * to + core),
            device_id_type=MESH,
        )

    def start_reduce():
        level_copy().start()
        mine = part[half_rows(core), :].astype(F32)
        level_copy().wait_recv()
        both[...] = (mine + other[...].astype(F32)).astype(BF)

        def send(d, carry):
            rs_copy(d).start()
            return carry

        lax.fori_loop(1, n_chip, send, 0)

    def finish_reduce():
        def take(d, total):
            rs_copy(d).wait_recv()
            return total + recv[d].astype(F32)

        return lax.fori_loop(1, n_chip, take, both[rows_of(chip), :].astype(F32))

    def ag_copy(buf, d):
        to = lax.rem(chip + d, n_chip)
        return pltpu.make_async_remote_copy(
            src_ref=buf.at[own_block],
            dst_ref=buf.at[own_block],
            send_sem=ag_send.at[d],
            recv_sem=ag_recv.at[d],
            device_id=(sec, 2 * to + core),
            device_id_type=MESH,
        )

    def hand_copy(buf, d):
        block = rows_of(core * n_chip + lax.rem(chip + n_chip - d, n_chip))
        return pltpu.make_async_remote_copy(
            src_ref=buf.at[block],
            dst_ref=buf.at[block],
            send_sem=hand_send.at[d],
            recv_sem=hand_recv.at[d],
            device_id=(sec, partner),
            device_id_type=MESH,
        )

    def start_gather(buf):
        def send(d, carry):
            ag_copy(buf, d).start()
            return carry

        lax.fori_loop(1, n_chip, send, 0)
        hand_copy(buf, 0).start()

    def finish_gather(buf):
        def take(d, carry):
            ag_copy(buf, d).wait_recv()
            hand_copy(buf, d).start()
            return carry

        lax.fori_loop(1, n_chip, take, 0)

        def settle_one(d, carry):
            hand_copy(buf, d).wait_recv()
            hand_copy(buf, d).wait_send()
            return carry

        lax.fori_loop(0, n_chip, settle_one, 0)

        def sent(d, carry):
            rs_copy(d).wait_send()
            ag_copy(buf, d).wait_send()
            return carry

        lax.fori_loop(1, n_chip, sent, 0)
        level_copy().wait_send()

    def halves(ref, base, p):
        cols = pl.ds(base + SEQ * p, SEQ)
        return ref[pl.ds(0, SEQ), cols], ref[pl.ds(SEQ, SEQ), cols]

    def beside(buf, p):
        return jnp.concatenate(
            [buf[pl.ds(2 * SEQ * p, SEQ), :], buf[pl.ds(2 * SEQ * p + SEQ, SEQ), :]], axis=1
        )

    def put_halves(ref, base, p, value):
        cols = pl.ds(base + SEQ * p, SEQ)
        ref[pl.ds(0, SEQ), cols] = value[:, :SEQ]
        ref[pl.ds(SEQ, SEQ), cols] = value[:, SEQ:]

    own_rows = WIDTH // n_row

    def put_grad(u, value):
        for r in range(n_row):
            q = r // 2
            grad[u, r % 2, q // SIDE, q % SIDE] = value[own_rows * r : own_rows * (r + 1)].astype(BF)

    def pair_copy(u, par):
        return pltpu.make_async_remote_copy(
            src_ref=grad.at[u, 1 - core],
            dst_ref=pairbuf.at[par, u],
            send_sem=pair_send.at[u],
            recv_sem=pair_recv.at[par, u],
            device_id=(sec, partner),
            device_id_type=MESH,
        )

    def y_first(u):
        return u % 2 == 0

    def c1_copy(u, par, d):
        if y_first(u):
            y = lax.rem(yc + d, SIDE)
            src, peer = grad.at[u, core, :, y], row_at(zc, y)
        else:
            z = lax.rem(zc + d, SIDE)
            src, peer = grad.at[u, core, z], row_at(z, yc)
        return pltpu.make_async_remote_copy(
            src_ref=src,
            dst_ref=line1.at[par, u, d - 1],
            send_sem=c1_send.at[u, d - 1],
            recv_sem=c1_recv.at[par, u, d - 1],
            device_id=(sec, peer),
            device_id_type=MESH,
        )

    def c2_copy(u, par, d):
        if y_first(u):
            at = lax.rem(zc + d, SIDE)
            peer = row_at(at, yc)
        else:
            at = lax.rem(yc + d, SIDE)
            peer = row_at(zc, at)
        return pltpu.make_async_remote_copy(
            src_ref=sum1.at[par, u, at],
            dst_ref=line2.at[par, u, d - 1],
            send_sem=c2_send.at[u, d - 1],
            recv_sem=c2_recv.at[par, u, d - 1],
            device_id=(sec, peer),
            device_id_type=MESH,
        )

    def x_copy(u, t):
        owner = LAYERS - 1 - t
        return pltpu.make_async_remote_copy(
            src_ref=xout.at[u],
            dst_ref=xin.at[u, lax.rem(sec - owner + LAYERS - 1 + LAYERS, LAYERS)],
            send_sem=x_send.at[u],
            recv_sem=x_recv.at[u, lax.rem(sec - owner + LAYERS - 1 + LAYERS, LAYERS)],
            device_id=(owner, me),
            device_id_type=MESH,
        )

    def stage_pair(u, t):
        pair_copy(u, t % 2).start()

    def stage_one(u, t):
        par = t % 2
        pair_copy(u, par).wait_recv()
        pair_copy(u, par).wait_send()
        for z in range(SIDE):
            total = grad[u, core, z].astype(F32) + pairbuf[par, u, z].astype(F32)
            grad[u, core, z] = total.astype(BF)
        for d in range(1, SIDE):
            c1_copy(u, par, d).start()

    def stage_two(u, t):
        par = t % 2
        for d in range(1, SIDE):
            c1_copy(u, par, d).wait_recv()
            c1_copy(u, par, d).wait_send()
        for k in range(SIDE):
            own = grad[u, core, k, yc] if y_first(u) else grad[u, core, zc, k]
            total = own.astype(F32)
            for d in range(SIDE - 1):
                total = total + line1[par, u, d, k].astype(F32)
            sum1[par, u, k] = total.astype(BF)
        for d in range(1, SIDE):
            c2_copy(u, par, d).start()

    def stage_three(u, t):
        par = t % 2
        owner = LAYERS - 1 - t
        for d in range(1, SIDE):
            c2_copy(u, par, d).wait_recv()
            c2_copy(u, par, d).wait_send()
        total = sum1[par, u, zc if y_first(u) else yc].astype(F32)
        for d in range(SIDE - 1):
            total = total + line2[par, u, d].astype(F32)

        @pl.when((t > 0) & (sec != owner + 1))
        def _():
            x_copy(u, t - 1).wait_send()

        @pl.when(sec == owner)
        def _():
            fin[u] = total

        @pl.when(sec != owner)
        def _():
            xout[u] = total.astype(BF)
            x_copy(u, t).start()

    for w in (1, 2):

        @pl.when(sec == w)
        def _():
            for d in range(1, LAYERS):
                deal_copy(w, d).start()
            if w == 2:
                for d in (1, 3, 2):
                    bulk_copy(d).start()

    @pl.when(sec == 0)
    def _():
        for t in (1, 3, 2):
            first_copy(t).start()

    launch_flow()

    def forward(l, carry):
        here = qkv.at[l]

        @pl.when(l == 0)
        def _():
            @pl.when(sec > 0)
            def _():
                tab_copy(0).wait_recv()
                tab_twin(core).start()
                tab_twin(1 - core).wait_recv()

            for d in range(1, LAYERS):
                gain_copy(d).wait_recv()
            for n in range(3):
                for half in range(2):
                    made = dot(picks, tab[half, :, pl.ds(HALF * n, HALF)], 0, 0)
                    here[:, pl.ds(WIDTH * n + HALF * half, HALF)] = made.astype(BF)

        @pl.when(l > 0)
        def _():
            for w in (1, 2):
                pl.when(l == w)(functools.partial(plane_settle, w))
            pl.when(l == RING)(settle)
            normal, _ = norm_parts(xs[l])
            h = (normal * gains[l]).astype(BF)
            for n in range(3):
                cols = pl.ds(WIDTH * n, WIDTH)
                here[:, cols] = dot(h, weight(l, WIDTH * n, WIDTH), 1, 0).astype(BF)

        pair_scores(lambda p: halves(here, 0, p), lambda p: halves(here, WIDTH, p), scale)
        start_reduce()

        @pl.when(l == 0)
        def _():
            plane_one(1)
            plane_two(1, 0)

        @pl.when(l == 1)
        def _():
            plane_two(2, 0)

        for turn in range(3):
            pl.when(l == turn)(functools.partial(pump, 2 * turn + 1))

        logits = finish_reduce()
        shifted = jnp.exp(logits - jnp.max(logits, axis=-1, keepdims=True))
        own = shifted / jnp.sum(shifted, axis=-1, keepdims=True)
        probs_l = probs.at[l]
        probs_l[own_block, :] = own.astype(BF)
        start_gather(probs_l)

        @pl.when(l == 0)
        def _():
            plane_two(1, 1)
            plane_one(2)

        for turn in range(2):
            pl.when(l == turn)(functools.partial(pump, 2 * turn + 2))

        finish_gather(probs_l)
        mixed_l = mixed.at[l]
        for p in range(PAIRS):
            out = dot(beside(probs_l, p), split_block(*halves(here, 2 * WIDTH, p)), 1, 0)
            put_halves(mixed_l, 0, p, out.astype(BF))

        @pl.when(l == 0)
        def _():
            @pl.when(sec > 0)
            def _():
                first_copy(0).wait_recv()
                first_twin(core).start()

            plane_three(1, 0)

            @pl.when(sec > 0)
            def _():
                first_twin(1 - core).wait_recv()

        @pl.when(l == 1)
        def _():
            plane_three(2, 0)

        @pl.when(l < LAYERS - 1)
        def _():
            xs[l + 1] = xs[l] + dot(mixed_l[...], weight(l, 3 * WIDTH, WIDTH), 1, 0)

        @pl.when(l == 0)
        def _():
            plane_three(1, 1)

        @pl.when(l == 1)
        def _():
            plane_three(2, 1)

        return carry

    lax.fori_loop(0, LAYERS, forward, 0)

    pltpu.make_async_copy(og_hbm.at[sec], ogb, og_sem).wait()
    dyf[...] = ogb[...].astype(F32)

    def reduce_window(step):
        def previous():
            t = step - 1
            for u, n in ((QRY, 0), (KEY, 1)):
                put_grad(u, dot(hbuf[...], dqkv[:, pl.ds(WIDTH * n, WIDTH)], 0, 0))
                stage_pair(u, t)
            for u in (OUT, VAL):
                stage_one(u, t)

        def older():
            t = step - 2
            for u in (OUT, VAL):
                stage_three(u, t)
            for u in (QRY, KEY):
                stage_two(u, t)

        return older, previous

    def gather_window(step):
        def previous():
            t = step - 1
            for u in (OUT, VAL):
                stage_two(u, t)
            for u in (QRY, KEY):
                stage_one(u, t)

        def older():
            t = step - 2
            for u in (QRY, KEY):
                stage_three(u, t)

        return previous, older

    def backward(step, carry):
        l = LAYERS - 1 - step
        here = qkv.at[l]
        probs_l = probs.at[l]
        dyb = dyf[...].astype(BF)
        dmix[...] = dot(dyb, weight(l, 3 * WIDTH, WIDTH), 1, 1).astype(BF)
        pair_scores(lambda p: halves(dmix, 0, p), lambda p: halves(here, 2 * WIDTH, p), None)
        start_reduce()

        older, previous = reduce_window(step)
        pl.when(step >= 2)(older)
        pl.when(step >= 1)(previous)
        for p in range(PAIRS):
            rows = pl.ds(2 * SEQ * p, 2 * SEQ)
            out = dot(probs_l[rows, :], split_block(*halves(dmix, 0, p)), 0, 0)
            put_halves(dqkv, 2 * WIDTH, p, out.astype(BF))
        dprobs = finish_reduce()
        own = probs_l[own_block, :].astype(F32)
        inner = jnp.sum(dprobs * own, axis=-1, keepdims=True)
        dlog[own_block, :] = (own * (dprobs - inner)).astype(BF)
        start_gather(dlog)

        normal, rstd = norm_parts(xs[l])
        hbuf[...] = (normal * gains[l]).astype(BF)
        vcols = pl.ds(2 * WIDTH, WIDTH)
        previous, older = gather_window(step)
        pl.when(step >= 1)(previous)
        put_grad(OUT, dot(mixed[l], dyb, 0, 0))
        put_grad(VAL, dot(hbuf[...], dqkv[:, vcols], 0, 0))
        for u in (OUT, VAL):
            stage_pair(u, step)

        @pl.when(l > 0)
        def _():
            dhacc[...] = dot(dqkv[:, vcols], weight(l, 2 * WIDTH, WIDTH), 1, 1)

        pl.when(step >= 2)(older)
        finish_gather(dlog)

        for p in range(PAIRS):
            out = dot(beside(dlog, p), split_block(*halves(here, WIDTH, p)), 1, 0)
            put_halves(dqkv, 0, p, (scale * out).astype(BF))
            rows = pl.ds(2 * SEQ * p, 2 * SEQ)
            out = dot(dlog[rows, :], split_block(*halves(here, 0, p)), 0, 0)
            put_halves(dqkv, WIDTH, p, (scale * out).astype(BF))
        qk = pl.ds(0, 2 * WIDTH)

        @pl.when(l > 0)
        def _():
            dh = dhacc[...] + dot(dqkv[:, qk], weight(l, 0, 2 * WIDTH), 1, 1)
            dn = dh.astype(BF).astype(F32) * gains[l]
            first = jnp.mean(dn, axis=-1, keepdims=True)
            second = jnp.mean(dn * normal, axis=-1, keepdims=True)
            dyf[...] = dyf[...] + rstd * (dn - first - normal * second)

        return carry

    lax.fori_loop(0, LAYERS, backward, 0)

    for work in reduce_window(LAYERS) + gather_window(LAYERS):
        work()
    reduce_window(LAYERS + 1)[0]()
    gather_window(LAYERS + 1)[1]()

    for u in range(4):

        @pl.when(sec != 0)
        def _():
            x_copy(u, LAYERS - 1).wait_send()

        total = fin[u]
        for slot in range(LAYERS - 1):
            pltpu.make_async_remote_copy(
                src_ref=xout.at[u],
                dst_ref=xin.at[u, slot],
                send_sem=x_send.at[u],
                recv_sem=x_recv.at[u, slot],
                device_id=(lax.rem(sec + 1, LAYERS), me),
                device_id_type=MESH,
            ).wait_recv()
            total = total + xin[u, slot].astype(F32)
        if u == OUT:
            go_ref[0] = total
        else:
            gq_ref[0, :, pl.ds(WIDTH * {VAL: 2, QRY: 0, KEY: 1}[u], WIDTH)] = total

    tall = wcat[sec, zc, yc // 2, pl.ds(pl.multiple_of(2 * own_rows * lax.rem(yc, 2), 16), 2 * own_rows), :]
    tall = tall[:, : 3 * WIDTH].astype(F32)
    w_own = jnp.where(core == 0, tall[:own_rows], tall[own_rows:])
    dotted = jnp.sum(w_own * gq_ref[0], axis=-1, keepdims=True)
    lanes = lax.broadcasted_iota(jnp.int32, (own_rows, WIDTH), 1)
    subs = lax.broadcasted_iota(jnp.int32, (own_rows, WIDTH), 0)
    gain_own = jnp.sum(
        jnp.where(lanes == subs + own_rows * me, gain_ref[...], 0.0), axis=-1, keepdims=True
    )
    spread = jnp.where(lanes == subs, dotted / gain_own, 0.0)
    gg_ref[...] = jnp.sum(spread, axis=0, keepdims=True)[:, :own_rows]

    drain()
    for w in (1, 2):
        plane_drain(w)

    @pl.when(sec == 0)
    def _():
        for t in range(1, LAYERS):
            tab_copy(t).wait_send()
            first_copy(t).wait_send()

    @pl.when(sec > 0)
    def _():
        tab_twin(core).wait_send()
        first_twin(core).wait_send()

    for d in range(1, LAYERS):
        gain_copy(d).wait_send()


def hand_over(qkv_in, out_in, gain_in, qkv_out, out_out, gain_out):
    qkv_out[...] = qkv_in[...]
    out_out[...] = out_in[...]
    gain_out[...] = gain_in[...]


def local(tokens, embed, ln_gain, w_qkv, w_out, out_grad):
    n_row = lax.axis_size("row")
    micro, rows_here, seq = tokens.shape
    vocab, width = embed.shape
    npos = rows_here * seq
    scale = HEAD_DIM ** (-0.5) / (rows_here * n_row) ** 0.5
    padded = vocab + -vocab % 16
    flat = HEADS * seq
    own_rows = width // n_row
    vm, anyspace = pl.BlockSpec(memory_space=pltpu.VMEM), pl.BlockSpec(memory_space=pl.ANY)
    dma = pltpu.SemaphoreType.DMA
    sums = pl.pallas_call(
        functools.partial(kernel, n_row, scale),
        out_shape=(
            jax.ShapeDtypeStruct((1, own_rows, 3 * width), F32),
            jax.ShapeDtypeStruct((1, own_rows, width), F32),
            jax.ShapeDtypeStruct((1, own_rows), F32),
        ),
        in_specs=[vm, vm, vm, anyspace, anyspace, anyspace],
        out_specs=(vm, vm, vm),
        scratch_shapes=[
            pltpu.VMEM((LAYERS, SIDE, 2, width // 8, 4 * width), BF),
            pltpu.VMEM((LAYERS, 1, width), F32),
            pltpu.VMEM((padded, width), BF),
            pltpu.VMEM((2, padded, 3 * width // 2), BF),
            pltpu.VMEM((LAYERS, npos, width), F32),
            pltpu.VMEM((LAYERS, npos, 3 * width), BF),
            pltpu.VMEM((LAYERS, flat, seq), BF),
            pltpu.VMEM((LAYERS, npos, width), BF),
            pltpu.VMEM((flat, seq), BF),
            pltpu.VMEM((flat // 2, seq), BF),
            pltpu.VMEM((flat // 2, seq), BF),
            pltpu.VMEM((n_row // 2, flat // n_row, seq), BF),
            pltpu.VMEM((flat, seq), BF),
            pltpu.VMEM((npos, width), F32),
            pltpu.VMEM((npos, width), BF),
            pltpu.VMEM((npos, width), BF),
            pltpu.VMEM((npos, 3 * width), BF),
            pltpu.VMEM((npos, width), BF),
            pltpu.VMEM((npos, width), F32),
            pltpu.VMEM((4, 2, SIDE, SIDE, own_rows, width), BF),
            pltpu.VMEM((2, 4, SIDE, SIDE, own_rows, width), BF),
            pltpu.VMEM((2, 4, SIDE - 1, SIDE, own_rows, width), BF),
            pltpu.VMEM((2, 4, SIDE, own_rows, width), BF),
            pltpu.VMEM((2, 4, SIDE - 1, own_rows, width), BF),
            pltpu.VMEM((4, own_rows, width), BF),
            pltpu.VMEM((4, LAYERS - 1, own_rows, width), BF),
            pltpu.VMEM((4, own_rows, width), F32),
            dma((2,)),
            dma((n_row // 2,)),
            dma((n_row // 2,)),
            dma((n_row // 2,)),
            dma((n_row // 2,)),
            dma((n_row // 2,)),
            dma((n_row // 2,)),
            dma((2,)),
            dma,
            dma((LAYERS,)),
            dma((2,)),
            dma((LAYERS,)),
            dma((LAYERS,)),
            dma((2, LAYERS)),
            dma((2,)),
            dma((LAYERS,)),
            dma,
            dma((2, 2, SIDE - 1)),
            dma((2, 2, SIDE - 1)),
            dma((2, 2, SIDE - 1)),
            dma((2, 2, SIDE - 1)),
            dma((2, 2)),
            dma((2, 2)),
            dma((2, CHUNKS)),
            dma((2, CHUNKS)),
            dma((2, CHUNKS)),
            dma((2, CHUNKS)),
            dma((LAYERS,)),
            dma((2,)),
            dma((4,)),
            dma((2, 4)),
            dma((4, SIDE - 1)),
            dma((2, 4, SIDE - 1)),
            dma((4, SIDE - 1)),
            dma((2, 4, SIDE - 1)),
            dma((4,)),
            dma((4, LAYERS - 1)),
        ],
        compiler_params=pltpu.CompilerParams(
            collective_id=0, has_side_effects=True, vmem_limit_bytes=67043328
        ),
    )(
        tokens,
        embed,
        ln_gain,
        w_qkv.reshape(SIDE, 2, width // 8, 3 * width),
        w_out.reshape(SIDE, 2, width // 8, width),
        out_grad.reshape(micro, npos, width),
    )
    grad_qkv, grad_out, grad_gain = pl.pallas_call(
        hand_over,
        out_shape=tuple(jax.ShapeDtypeStruct(g.shape, F32) for g in sums),
        in_specs=[vm, vm, vm],
        out_specs=(vm, vm, vm),
    )(*sums)
    return (grad_qkv, grad_out, grad_gain)


def solution(mesh):
    in_specs = (
        P(None, "row", None),
        P(),
        P("section", None),
        P("section", None, None),
        P("section", None, None),
        P(None, "row", None, None),
    )
    out_specs = (P("section", "row", None), P("section", "row", None), P("section", "row"))
    return jax.shard_map(local, mesh=mesh, in_specs=in_specs, out_specs=out_specs, check_vma=False)
```

```python
import functools

import jax
import jax.numpy as jnp
from jax import lax
from jax.experimental import pallas as pl
from jax.experimental.pallas import tpu as pltpu
from jax.sharding import PartitionSpec as P

HEADS = 12
HEAD_DIM = 64
LAYERS = 4
PAIRS = HEADS // 2
WIDTH = HEADS * HEAD_DIM
SEQ = 128
SIDE = 4
OUT, VAL, QRY, KEY = 0, 1, 2, 3
CHUNKS = 3
NEAR = sorted(
    ((z, y) for z in range(SIDE) for y in range(SIDE) if z or y),
    key=lambda step: sum(min(n, SIDE - n) for n in step),
)
CHUNK = 4 * WIDTH // CHUNKS
HALF = WIDTH // 2
MESH = pl.DeviceIdType.MESH
BF = jnp.bfloat16
F32 = jnp.float32


def dot(a, b, ca, cb):
    return lax.dot_general(a, b, (((ca,), (cb,)), ((), ())), preferred_element_type=F32)


def norm_parts(x):
    centred = x - jnp.mean(x, axis=-1, keepdims=True)
    spread = jnp.mean(centred * centred, axis=-1, keepdims=True)
    rstd = lax.rsqrt(spread + 1e-05)
    return centred * rstd, rstd


def kernel(
    n_row,
    scale,
    tok_ref,
    emb_ref,
    gain_ref,
    wqkv_hbm,
    wout_hbm,
    og_hbm,
    gq_ref,
    go_ref,
    gg_ref,
    wcat,
    gains,
    embp,
    tab,
    xs,
    qkv,
    probs,
    mixed,
    part,
    other,
    both,
    recv,
    dlog,
    dyf,
    ogb,
    dmix,
    dqkv,
    hbuf,
    dhacc,
    grad,
    pairbuf,
    line1,
    sum1,
    line2,
    xout,
    xin,
    fin,
    level_sem,
    rs_send,
    rs_recv,
    ag_send,
    ag_recv,
    hand_send,
    hand_recv,
    w_sem,
    og_sem,
    tab_send,
    tab_recv,
    gain_send,
    gain_recv,
    deal_send,
    deal_recv,
    bulk_send,
    bulk_recv,
    s1_send,
    s1_recv,
    s2_send,
    s2_recv,
    join_send,
    join_recv,
    ring_send,
    ring_recv,
    twin_send,
    twin_recv,
    first_send,
    first_recv,
    pair_send,
    pair_recv,
    c1_send,
    c1_recv,
    c2_send,
    c2_recv,
    x_send,
    x_recv,
):
    sec = lax.axis_index("section")
    me = lax.axis_index("row")
    piece = part.shape[0] // n_row
    n_chip = n_row // 2
    core = lax.rem(me, 2)
    partner = me + 1 - 2 * core
    chip = me // 2
    zc = chip // SIDE
    yc = lax.rem(chip, SIDE)

    def row_at(z, y):
        return (z * SIDE + y) * 2 + core

    def weight(l, first, count):
        block = wcat[l, :, :, :, pl.ds(first, count)]
        return block.reshape(WIDTH, count)

    local_qkv = pltpu.make_async_copy(
        wqkv_hbm, wcat.at[sec, :, :, :, pl.ds(0, 3 * WIDTH)], w_sem.at[0]
    )
    local_out = pltpu.make_async_copy(
        wout_hbm, wcat.at[sec, :, :, :, pl.ds(3 * WIDTH, WIDTH)], w_sem.at[1]
    )
    local_qkv.start()
    local_out.start()
    pltpu.make_async_copy(og_hbm.at[sec], ogb, og_sem).start()

    barrier = pltpu.get_barrier_semaphore()

    def greet(d, carry):
        peer = 2 * lax.rem(chip + d, n_chip) + core
        pl.semaphore_signal(barrier, inc=1, device_id=(sec, peer), device_id_type=MESH)
        return carry

    lax.fori_loop(1, n_chip, greet, 0)
    pl.semaphore_signal(barrier, inc=1, device_id=(sec, partner), device_id_type=MESH)
    for d in range(1, LAYERS):
        pl.semaphore_signal(
            barrier, inc=1, device_id=(lax.rem(sec + d, LAYERS), me), device_id_type=MESH
        )

    lane = lax.broadcasted_iota(jnp.int32, (1, SEQ), 1)
    low = (lane < HEAD_DIM).astype(F32).astype(BF)
    high = (lane >= HEAD_DIM).astype(F32).astype(BF)

    gains[sec] = gain_ref[...]
    padded = embp.shape[0]
    embp[...] = jnp.zeros_like(embp)
    embp[pl.ds(0, emb_ref.shape[0]), :] = emb_ref[...]
    ids = lax.broadcasted_iota(jnp.int32, (padded, SEQ), 0)
    tok = tok_ref[sec]
    picks = jnp.concatenate([(tok[r : r + 1] == ids) for r in range(2)], axis=1)
    picks = picks.astype(F32).astype(BF)
    xs[0] = dot(picks, embp[...], 0, 0)

    local_qkv.wait()

    @pl.when(sec == 0)
    def _():
        normal, _ = norm_parts(embp[...].astype(F32))
        h = (normal * gain_ref[...]).astype(BF)
        for n in range(3):
            made = dot(h, weight(0, WIDTH * n, WIDTH), 1, 0).astype(BF)
            for half in range(2):
                cols = pl.ds(HALF * n, HALF)
                tab[half, :, cols] = made[:, HALF * half : HALF * (half + 1)]

    local_out.wait()
    pl.semaphore_wait(barrier, n_chip + LAYERS - 1)

    def tab_copy(t):
        return pltpu.make_async_remote_copy(
            src_ref=tab.at[core],
            dst_ref=tab.at[core],
            send_sem=tab_send.at[t],
            recv_sem=tab_recv.at[0],
            device_id=(t, me),
            device_id_type=MESH,
        )

    def tab_twin(who):
        return pltpu.make_async_remote_copy(
            src_ref=tab.at[who],
            dst_ref=tab.at[who],
            send_sem=tab_send.at[0],
            recv_sem=tab_recv.at[1],
            device_id=(sec, partner),
            device_id_type=MESH,
        )

    @pl.when(sec == 0)
    def _():
        for t in range(1, LAYERS):
            tab_copy(t).start()

    def gain_copy(d):
        return pltpu.make_async_remote_copy(
            src_ref=gain_ref,
            dst_ref=gains.at[sec],
            send_sem=gain_send.at[d],
            recv_sem=gain_recv.at[d],
            device_id=(lax.rem(sec + d, LAYERS), me),
            device_id_type=MESH,
        )

    for d in range(1, LAYERS):
        gain_copy(d).start()

    RING = LAYERS - 1

    def flow(d, k, who):
        cols = pl.ds(pl.multiple_of(k * CHUNK, 128), CHUNK)
        return wcat.at[RING, who * 2 + d, :, :, cols]

    def place(d):
        return lax.rem(sec - RING + LAYERS, LAYERS) if d == 0 else lax.rem(RING - sec, LAYERS)

    def ring_copy(d, k):
        step = 1 if d == 0 else LAYERS - 1
        ref = flow(d, k, core)
        return pltpu.make_async_remote_copy(
            src_ref=ref,
            dst_ref=ref,
            send_sem=ring_send.at[d, k],
            recv_sem=ring_recv.at[d, k],
            device_id=(lax.rem(sec + step, LAYERS), me),
            device_id_type=MESH,
        )

    def twin_copy(d, k, who):
        ref = flow(d, k, who)
        return pltpu.make_async_remote_copy(
            src_ref=ref,
            dst_ref=ref,
            send_sem=twin_send.at[d, k],
            recv_sem=twin_recv.at[d, k],
            device_id=(sec, partner),
            device_id_type=MESH,
        )

    def launch_flow():
        @pl.when(sec == RING)
        def _():
            for k in range(CHUNKS):
                for d in range(2):
                    ring_copy(d, k).start()

    def pump(slot):
        for d in range(2):
            at = place(d)
            k = slot - at

            @pl.when((at > 0) & (k >= 0) & (k < CHUNKS))
            def _():
                ring_copy(d, k).wait_recv()

                @pl.when(at < LAYERS - 1)
                def _():
                    ring_copy(d, k).start()

                twin_copy(d, k, core).start()

    def settle():
        @pl.when(sec != RING)
        def _():
            for k in range(CHUNKS):
                for d in range(2):
                    twin_copy(d, k, 1 - core).wait_recv()

    def drain():
        def one(k, carry):
            for d in range(2):
                at = place(d)

                @pl.when(at < LAYERS - 1)
                def _():
                    ring_copy(d, k).wait_send()

                @pl.when(at > 0)
                def _():
                    twin_copy(d, k, core).wait_send()

            return carry

        lax.fori_loop(0, CHUNKS, one, 0)

    def first_ref(who):
        return wcat.at[0, pl.ds(2 * who, 2), :, :, pl.ds(3 * WIDTH, WIDTH)]

    def first_copy(t):
        return pltpu.make_async_remote_copy(
            src_ref=first_ref(core),
            dst_ref=first_ref(core),
            send_sem=first_send.at[t],
            recv_sem=first_recv.at[0],
            device_id=(t, me),
            device_id_type=MESH,
        )

    def first_twin(who):
        return pltpu.make_async_remote_copy(
            src_ref=first_ref(who),
            dst_ref=first_ref(who),
            send_sem=first_send.at[0],
            recv_sem=first_recv.at[1],
            device_id=(sec, partner),
            device_id_type=MESH,
        )

    block_cols = pl.ds(pl.multiple_of((core * SIDE + yc) * HALF, 128), HALF)

    def side_cols(who):
        return pl.ds(pl.multiple_of(who * (2 * WIDTH), 128), 2 * WIDTH)

    def deal_copy(w, d):
        halves_sent = 2 if w == 1 else 1
        ref = wcat.at[w, zc, pl.ds(0, halves_sent), :, block_cols]
        return pltpu.make_async_remote_copy(
            src_ref=ref,
            dst_ref=ref,
            send_sem=deal_send.at[w - 1, d],
            recv_sem=deal_recv.at[w - 1],
            device_id=((w + d) % LAYERS, me),
            device_id_type=MESH,
        )

    def bulk_copy(d):
        ref = wcat.at[2, :, 1, :, side_cols(core)]
        return pltpu.make_async_remote_copy(
            src_ref=ref,
            dst_ref=ref,
            send_sem=bulk_send.at[d],
            recv_sem=bulk_recv,
            device_id=((2 + d) % LAYERS, me),
            device_id_type=MESH,
        )

    def line_copy(w, stage, half, d):
        along_y = (stage + half) % 2 == 0
        y = lax.rem(yc + d, SIDE) if along_y else yc
        z = zc if along_y else lax.rem(zc + d, SIDE)
        if stage == 0:
            ref = wcat.at[w, zc, half, :, block_cols]
        elif along_y:
            ref = wcat.at[w, :, half, :, block_cols]
        else:
            ref = wcat.at[w, zc, half, :, side_cols(core)]
        send, take = (s1_send, s1_recv) if stage == 0 else (s2_send, s2_recv)
        return pltpu.make_async_remote_copy(
            src_ref=ref,
            dst_ref=ref,
            send_sem=send.at[w - 1, half, d - 1],
            recv_sem=take.at[w - 1, half, d - 1],
            device_id=(sec, row_at(z, y)),
            device_id_type=MESH,
        )

    def join_copy(w, half, who):
        ref = wcat.at[w, :, half, :, side_cols(who)]
        return pltpu.make_async_remote_copy(
            src_ref=ref,
            dst_ref=ref,
            send_sem=join_send.at[w - 1, half],
            recv_sem=join_recv.at[w - 1, half],
            device_id=(sec, partner),
            device_id_type=MESH,
        )

    def plane_one(w):
        @pl.when(sec != w)
        def _():
            deal_copy(w, 0).wait_recv()
            for half in range(2 if w == 1 else 1):
                for d in range(1, SIDE):
                    line_copy(w, 0, half, d).start()

    def plane_two(w, half):
        @pl.when(sec != w)
        def _():
            for d in range(1, SIDE):
                line_copy(w, 0, half, d).wait_recv()
            for d in range(1, SIDE):
                line_copy(w, 1, half, d).start()

    def plane_three(w, half):
        @pl.when(sec != w)
        def _():
            if w == 2 and half == 1:
                bulk_copy(0).wait_recv()
            else:
                for d in range(1, SIDE):
                    line_copy(w, 1, half, d).wait_recv()
            join_copy(w, half, core).start()

    def plane_settle(w):
        @pl.when(sec != w)
        def _():
            for half in range(2):
                join_copy(w, half, 1 - core).wait_recv()

    def plane_drain(w):
        @pl.when(sec != w)
        def _():
            for half in range(2):
                for d in range(1, SIDE):
                    if w == 1 or half == 0:
                        line_copy(w, 0, half, d).wait_send()
                        line_copy(w, 1, half, d).wait_send()
                join_copy(w, half, core).wait_send()

        @pl.when(sec == w)
        def _():
            for d in range(1, LAYERS):
                deal_copy(w, d).wait_send()
                if w == 2:
                    bulk_copy(d).wait_send()

    def rows_of(k):
        return pl.ds(pl.multiple_of(k * piece, 16), piece)

    def half_rows(who):
        return pl.ds(pl.multiple_of(who * (n_chip * piece), 16), n_chip * piece)

    own_block = rows_of(core * n_chip + chip)

    def split_block(a0, a1):
        top = jnp.concatenate([a0 * low, a1 * low], axis=1)
        bottom = jnp.concatenate([a0 * high, a1 * high], axis=1)
        return jnp.concatenate([top, bottom], axis=0)

    def pair_scores(left, right, factor):
        for p in range(PAIRS):
            la, ra = left(p), right(p)
            out = dot(split_block(*la), jnp.concatenate(ra, axis=1), 1, 1)
            if factor is not None:
                out = factor * out
            part[pl.ds(2 * SEQ * p, 2 * SEQ), :] = out.astype(BF)

    def level_copy():
        return pltpu.make_async_remote_copy(
            src_ref=part.at[half_rows(1 - core)],
            dst_ref=other,
            send_sem=level_sem.at[0],
            recv_sem=level_sem.at[1],
            device_id=(sec, partner),
            device_id_type=MESH,
        )

    def chip_at(step, sign):
        z, y = ((sign * n) % SIDE for n in step)
        return lax.rem(zc + z, SIDE) * SIDE + lax.rem(yc + y, SIDE)

    def rs_copy(d):
        to = chip_at(NEAR[d - 1], 1)
        return pltpu.make_async_remote_copy(
            src_ref=both.at[rows_of(to)],
            dst_ref=recv.at[d],
            send_sem=rs_send.at[d],
            recv_sem=rs_recv.at[d],
            device_id=(sec, 2 * to + core),
            device_id_type=MESH,
        )

    def start_reduce():
        level_copy().start()
        mine = part[half_rows(core), :].astype(F32)
        level_copy().wait_recv()
        both[...] = (mine + other[...].astype(F32)).astype(BF)
        for d in reversed(range(1, n_chip)):
            rs_copy(d).start()

    def finish_reduce():
        total = both[rows_of(chip), :].astype(F32)
        for d in range(1, n_chip):
            rs_copy(d).wait_recv()
            total = total + recv[d].astype(F32)
        return total

    def ag_copy(buf, d):
        to = chip_at(NEAR[d - 1], 1)
        return pltpu.make_async_remote_copy(
            src_ref=buf.at[own_block],
            dst_ref=buf.at[own_block],
            send_sem=ag_send.at[d],
            recv_sem=ag_recv.at[d],
            device_id=(sec, 2 * to + core),
            device_id_type=MESH,
        )

    def hand_copy(buf, d):
        source = chip_at(NEAR[d - 1], -1) if d else chip
        block = rows_of(core * n_chip + source)
        return pltpu.make_async_remote_copy(
            src_ref=buf.at[block],
            dst_ref=buf.at[block],
            send_sem=hand_send.at[d],
            recv_sem=hand_recv.at[d],
            device_id=(sec, partner),
            device_id_type=MESH,
        )

    def start_gather(buf):
        for d in reversed(range(1, n_chip)):
            ag_copy(buf, d).start()
        hand_copy(buf, 0).start()

    def finish_gather(buf):
        for d in range(1, n_chip):
            ag_copy(buf, d).wait_recv()
            hand_copy(buf, d).start()
        for d in range(n_chip):
            hand_copy(buf, d).wait_recv()

    def clear_exchange(buf):
        for d in range(n_chip):
            hand_copy(buf, d).wait_send()
        for d in range(1, n_chip):
            rs_copy(d).wait_send()
            ag_copy(buf, d).wait_send()
        level_copy().wait_send()

    def halves(ref, base, p):
        cols = pl.ds(base + SEQ * p, SEQ)
        return ref[pl.ds(0, SEQ), cols], ref[pl.ds(SEQ, SEQ), cols]

    def beside(buf, p):
        return jnp.concatenate(
            [buf[pl.ds(2 * SEQ * p, SEQ), :], buf[pl.ds(2 * SEQ * p + SEQ, SEQ), :]], axis=1
        )

    def put_halves(ref, base, p, value):
        cols = pl.ds(base + SEQ * p, SEQ)
        ref[pl.ds(0, SEQ), cols] = value[:, :SEQ]
        ref[pl.ds(SEQ, SEQ), cols] = value[:, SEQ:]

    own_rows = WIDTH // n_row

    def put_grad(u, value):
        for r in range(n_row):
            q = r // 2
            grad[u, r % 2, q // SIDE, q % SIDE] = value[own_rows * r : own_rows * (r + 1)].astype(BF)

    def pair_copy(u, par):
        return pltpu.make_async_remote_copy(
            src_ref=grad.at[u, 1 - core],
            dst_ref=pairbuf.at[par, u],
            send_sem=pair_send.at[u],
            recv_sem=pair_recv.at[par, u],
            device_id=(sec, partner),
            device_id_type=MESH,
        )

    def y_first(u):
        return u % 2 == 0

    def c1_copy(u, par, d):
        if y_first(u):
            y = lax.rem(yc + d, SIDE)
            src, peer = grad.at[u, core, :, y], row_at(zc, y)
        else:
            z = lax.rem(zc + d, SIDE)
            src, peer = grad.at[u, core, z], row_at(z, yc)
        return pltpu.make_async_remote_copy(
            src_ref=src,
            dst_ref=line1.at[par, u, d - 1],
            send_sem=c1_send.at[u, d - 1],
            recv_sem=c1_recv.at[par, u, d - 1],
            device_id=(sec, peer),
            device_id_type=MESH,
        )

    def c2_copy(u, par, d):
        if y_first(u):
            at = lax.rem(zc + d, SIDE)
            peer = row_at(at, yc)
        else:
            at = lax.rem(yc + d, SIDE)
            peer = row_at(zc, at)
        return pltpu.make_async_remote_copy(
            src_ref=sum1.at[par, u, at],
            dst_ref=line2.at[par, u, d - 1],
            send_sem=c2_send.at[u, d - 1],
            recv_sem=c2_recv.at[par, u, d - 1],
            device_id=(sec, peer),
            device_id_type=MESH,
        )

    def x_copy(u, t):
        owner = LAYERS - 1 - t
        return pltpu.make_async_remote_copy(
            src_ref=xout.at[u],
            dst_ref=xin.at[u, lax.rem(sec - owner + LAYERS - 1 + LAYERS, LAYERS)],
            send_sem=x_send.at[u],
            recv_sem=x_recv.at[u, lax.rem(sec - owner + LAYERS - 1 + LAYERS, LAYERS)],
            device_id=(owner, me),
            device_id_type=MESH,
        )

    def stage_pair(u, t):
        pair_copy(u, t % 2).start()

    def stage_one(u, t):
        par = t % 2
        pair_copy(u, par).wait_recv()
        pair_copy(u, par).wait_send()
        for z in range(SIDE):
            total = grad[u, core, z].astype(F32) + pairbuf[par, u, z].astype(F32)
            grad[u, core, z] = total.astype(BF)
        for d in range(1, SIDE):
            c1_copy(u, par, d).start()

    def stage_two(u, t):
        par = t % 2
        for d in range(1, SIDE):
            c1_copy(u, par, d).wait_recv()
            c1_copy(u, par, d).wait_send()
        for k in range(SIDE):
            own = grad[u, core, k, yc] if y_first(u) else grad[u, core, zc, k]
            total = own.astype(F32)
            for d in range(SIDE - 1):
                total = total + line1[par, u, d, k].astype(F32)
            sum1[par, u, k] = total.astype(BF)
        for d in range(1, SIDE):
            c2_copy(u, par, d).start()

    def stage_three(u, t):
        par = t % 2
        owner = LAYERS - 1 - t
        for d in range(1, SIDE):
            c2_copy(u, par, d).wait_recv()
            c2_copy(u, par, d).wait_send()
        total = sum1[par, u, zc if y_first(u) else yc].astype(F32)
        for d in range(SIDE - 1):
            total = total + line2[par, u, d].astype(F32)

        @pl.when((t > 0) & (sec != owner + 1))
        def _():
            x_copy(u, t - 1).wait_send()

        @pl.when(sec == owner)
        def _():
            fin[u] = total

        @pl.when(sec != owner)
        def _():
            xout[u] = total.astype(BF)
            x_copy(u, t).start()

    for w in (1, 2):

        @pl.when(sec == w)
        def _():
            for d in range(1, LAYERS):
                deal_copy(w, d).start()
            if w == 2:
                for d in (1, 3, 2):
                    bulk_copy(d).start()

    @pl.when(sec == 0)
    def _():
        for t in (1, 3, 2):
            first_copy(t).start()

    def forward(l, carry):
        here = qkv.at[l]

        @pl.when(l == 0)
        def _():
            @pl.when(sec > 0)
            def _():
                tab_copy(0).wait_recv()
                tab_twin(core).start()
                tab_twin(1 - core).wait_recv()

            for d in range(1, LAYERS):
                gain_copy(d).wait_recv()
            for n in range(3):
                for half in range(2):
                    made = dot(picks, tab[half, :, pl.ds(HALF * n, HALF)], 0, 0)
                    here[:, pl.ds(WIDTH * n + HALF * half, HALF)] = made.astype(BF)

        @pl.when(l > 0)
        def _():
            for w in (1, 2):
                pl.when(l == w)(functools.partial(plane_settle, w))

            @pl.when(l == RING)
            def _():
                pump(5)
                settle()

            normal, _ = norm_parts(xs[l])
            h = (normal * gains[l]).astype(BF)
            for n in range(3):
                cols = pl.ds(WIDTH * n, WIDTH)
                here[:, cols] = dot(h, weight(l, WIDTH * n, WIDTH), 1, 0).astype(BF)

        pair_scores(lambda p: halves(here, 0, p), lambda p: halves(here, WIDTH, p), scale)
        start_reduce()

        @pl.when(l == 0)
        def _():
            plane_one(1)
            plane_two(1, 0)

        @pl.when(l == 1)
        def _():
            plane_two(2, 0)

        for turn in (1, 2):
            pl.when(l == turn)(functools.partial(pump, 2 * turn - 1))

        logits = finish_reduce()
        shifted = jnp.exp(logits - jnp.max(logits, axis=-1, keepdims=True))
        own = shifted / jnp.sum(shifted, axis=-1, keepdims=True)
        probs_l = probs.at[l]
        probs_l[own_block, :] = own.astype(BF)
        start_gather(probs_l)

        @pl.when(l == 0)
        def _():
            plane_two(1, 1)
            plane_one(2)
            launch_flow()

        for turn in (1, 2):
            pl.when(l == turn)(functools.partial(pump, 2 * turn))

        finish_gather(probs_l)
        clear_exchange(probs_l)
        mixed_l = mixed.at[l]
        for p in range(PAIRS):
            out = dot(beside(probs_l, p), split_block(*halves(here, 2 * WIDTH, p)), 1, 0)
            put_halves(mixed_l, 0, p, out.astype(BF))

        @pl.when(l == 0)
        def _():
            @pl.when(sec > 0)
            def _():
                first_copy(0).wait_recv()
                first_twin(core).start()

            plane_three(1, 0)

            @pl.when(sec > 0)
            def _():
                first_twin(1 - core).wait_recv()

        @pl.when(l == 1)
        def _():
            plane_three(2, 0)

        @pl.when(l < LAYERS - 1)
        def _():
            xs[l + 1] = xs[l] + dot(mixed_l[...], weight(l, 3 * WIDTH, WIDTH), 1, 0)

        @pl.when(l == 0)
        def _():
            plane_three(1, 1)

        @pl.when(l == 1)
        def _():
            plane_three(2, 1)

        return carry

    lax.fori_loop(0, LAYERS, forward, 0)

    pltpu.make_async_copy(og_hbm.at[sec], ogb, og_sem).wait()
    dyf[...] = ogb[...].astype(F32)

    def reduce_window(step):
        def previous():
            t = step - 1
            for u, n in ((QRY, 0), (KEY, 1)):
                put_grad(u, dot(hbuf[...], dqkv[:, pl.ds(WIDTH * n, WIDTH)], 0, 0))
                stage_pair(u, t)
            for u in (OUT, VAL):
                stage_one(u, t)

        def older():
            t = step - 2
            for u in (OUT, VAL):
                stage_three(u, t)
            for u in (QRY, KEY):
                stage_two(u, t)

        return older, previous

    def gather_window(step):
        def previous():
            t = step - 1
            for u in (OUT, VAL):
                stage_two(u, t)
            for u in (QRY, KEY):
                stage_one(u, t)

        def older():
            t = step - 2
            for u in (QRY, KEY):
                stage_three(u, t)

        return previous, older

    def backward(step, carry):
        l = LAYERS - 1 - step
        here = qkv.at[l]
        probs_l = probs.at[l]
        dyb = dyf[...].astype(BF)
        dmix[...] = dot(dyb, weight(l, 3 * WIDTH, WIDTH), 1, 1).astype(BF)
        pair_scores(lambda p: halves(dmix, 0, p), lambda p: halves(here, 2 * WIDTH, p), None)
        start_reduce()

        older, previous = reduce_window(step)
        pl.when(step >= 2)(older)
        pl.when(step >= 1)(previous)
        for p in range(PAIRS):
            rows = pl.ds(2 * SEQ * p, 2 * SEQ)
            out = dot(probs_l[rows, :], split_block(*halves(dmix, 0, p)), 0, 0)
            put_halves(dqkv, 2 * WIDTH, p, out.astype(BF))
        dprobs = finish_reduce()
        own = probs_l[own_block, :].astype(F32)
        inner = jnp.sum(dprobs * own, axis=-1, keepdims=True)
        dlog[own_block, :] = (own * (dprobs - inner)).astype(BF)
        start_gather(dlog)

        normal, rstd = norm_parts(xs[l])
        hbuf[...] = (normal * gains[l]).astype(BF)
        vcols = pl.ds(2 * WIDTH, WIDTH)
        previous, older = gather_window(step)
        pl.when(step >= 1)(previous)
        put_grad(OUT, dot(mixed[l], dyb, 0, 0))
        put_grad(VAL, dot(hbuf[...], dqkv[:, vcols], 0, 0))
        for u in (OUT, VAL):
            stage_pair(u, step)

        @pl.when(l > 0)
        def _():
            dhacc[...] = dot(dqkv[:, vcols], weight(l, 2 * WIDTH, WIDTH), 1, 1)

        pl.when(step >= 2)(older)
        finish_gather(dlog)
        clear_exchange(dlog)

        for p in range(PAIRS):
            out = dot(beside(dlog, p), split_block(*halves(here, WIDTH, p)), 1, 0)
            put_halves(dqkv, 0, p, (scale * out).astype(BF))
            rows = pl.ds(2 * SEQ * p, 2 * SEQ)
            out = dot(dlog[rows, :], split_block(*halves(here, 0, p)), 0, 0)
            put_halves(dqkv, WIDTH, p, (scale * out).astype(BF))
        qk = pl.ds(0, 2 * WIDTH)

        @pl.when(l > 0)
        def _():
            dh = dhacc[...] + dot(dqkv[:, qk], weight(l, 0, 2 * WIDTH), 1, 1)
            dn = dh.astype(BF).astype(F32) * gains[l]
            first = jnp.mean(dn, axis=-1, keepdims=True)
            second = jnp.mean(dn * normal, axis=-1, keepdims=True)
            dyf[...] = dyf[...] + rstd * (dn - first - normal * second)

        return carry

    lax.fori_loop(0, LAYERS, backward, 0)

    for work in reduce_window(LAYERS) + gather_window(LAYERS):
        work()
    reduce_window(LAYERS + 1)[0]()
    gather_window(LAYERS + 1)[1]()

    for u in range(4):

        @pl.when(sec != 0)
        def _():
            x_copy(u, LAYERS - 1).wait_send()

        total = fin[u]
        for slot in range(LAYERS - 1):
            pltpu.make_async_remote_copy(
                src_ref=xout.at[u],
                dst_ref=xin.at[u, slot],
                send_sem=x_send.at[u],
                recv_sem=x_recv.at[u, slot],
                device_id=(lax.rem(sec + 1, LAYERS), me),
                device_id_type=MESH,
            ).wait_recv()
            total = total + xin[u, slot].astype(F32)
        if u == OUT:
            go_ref[0] = total
        else:
            gq_ref[0, :, pl.ds(WIDTH * {VAL: 2, QRY: 0, KEY: 1}[u], WIDTH)] = total

    tall = wcat[sec, zc, yc // 2, pl.ds(pl.multiple_of(2 * own_rows * lax.rem(yc, 2), 16), 2 * own_rows), :]
    tall = tall[:, : 3 * WIDTH].astype(F32)
    w_own = jnp.where(core == 0, tall[:own_rows], tall[own_rows:])
    dotted = jnp.sum(w_own * gq_ref[0], axis=-1, keepdims=True)
    lanes = lax.broadcasted_iota(jnp.int32, (own_rows, WIDTH), 1)
    subs = lax.broadcasted_iota(jnp.int32, (own_rows, WIDTH), 0)
    gain_own = jnp.sum(
        jnp.where(lanes == subs + own_rows * me, gain_ref[...], 0.0), axis=-1, keepdims=True
    )
    spread = jnp.where(lanes == subs, dotted / gain_own, 0.0)
    gg_ref[...] = jnp.sum(spread, axis=0, keepdims=True)[:, :own_rows]

    drain()
    for w in (1, 2):
        plane_drain(w)

    @pl.when(sec == 0)
    def _():
        for t in range(1, LAYERS):
            tab_copy(t).wait_send()
            first_copy(t).wait_send()

    @pl.when(sec > 0)
    def _():
        tab_twin(core).wait_send()
        first_twin(core).wait_send()

    for d in range(1, LAYERS):
        gain_copy(d).wait_send()


def hand_over(qkv_in, out_in, gain_in, qkv_out, out_out, gain_out):
    qkv_out[...] = qkv_in[...]
    out_out[...] = out_in[...]
    gain_out[...] = gain_in[...]


def local(tokens, embed, ln_gain, w_qkv, w_out, out_grad):
    n_row = lax.axis_size("row")
    micro, rows_here, seq = tokens.shape
    vocab, width = embed.shape
    npos = rows_here * seq
    scale = HEAD_DIM ** (-0.5) / (rows_here * n_row) ** 0.5
    padded = vocab + -vocab % 16
    flat = HEADS * seq
    own_rows = width // n_row
    vm, anyspace = pl.BlockSpec(memory_space=pltpu.VMEM), pl.BlockSpec(memory_space=pl.ANY)
    dma = pltpu.SemaphoreType.DMA
    sums = pl.pallas_call(
        functools.partial(kernel, n_row, scale),
        out_shape=(
            jax.ShapeDtypeStruct((1, own_rows, 3 * width), F32),
            jax.ShapeDtypeStruct((1, own_rows, width), F32),
            jax.ShapeDtypeStruct((1, own_rows), F32),
        ),
        in_specs=[vm, vm, vm, anyspace, anyspace, anyspace],
        out_specs=(vm, vm, vm),
        scratch_shapes=[
            pltpu.VMEM((LAYERS, SIDE, 2, width // 8, 4 * width), BF),
            pltpu.VMEM((LAYERS, 1, width), F32),
            pltpu.VMEM((padded, width), BF),
            pltpu.VMEM((2, padded, 3 * width // 2), BF),
            pltpu.VMEM((LAYERS, npos, width), F32),
            pltpu.VMEM((LAYERS, npos, 3 * width), BF),
            pltpu.VMEM((LAYERS, flat, seq), BF),
            pltpu.VMEM((LAYERS, npos, width), BF),
            pltpu.VMEM((flat, seq), BF),
            pltpu.VMEM((flat // 2, seq), BF),
            pltpu.VMEM((flat // 2, seq), BF),
            pltpu.VMEM((n_row // 2, flat // n_row, seq), BF),
            pltpu.VMEM((flat, seq), BF),
            pltpu.VMEM((npos, width), F32),
            pltpu.VMEM((npos, width), BF),
            pltpu.VMEM((npos, width), BF),
            pltpu.VMEM((npos, 3 * width), BF),
            pltpu.VMEM((npos, width), BF),
            pltpu.VMEM((npos, width), F32),
            pltpu.VMEM((4, 2, SIDE, SIDE, own_rows, width), BF),
            pltpu.VMEM((2, 4, SIDE, SIDE, own_rows, width), BF),
            pltpu.VMEM((2, 4, SIDE - 1, SIDE, own_rows, width), BF),
            pltpu.VMEM((2, 4, SIDE, own_rows, width), BF),
            pltpu.VMEM((2, 4, SIDE - 1, own_rows, width), BF),
            pltpu.VMEM((4, own_rows, width), BF),
            pltpu.VMEM((4, LAYERS - 1, own_rows, width), BF),
            pltpu.VMEM((4, own_rows, width), F32),
            dma((2,)),
            dma((n_row // 2,)),
            dma((n_row // 2,)),
            dma((n_row // 2,)),
            dma((n_row // 2,)),
            dma((n_row // 2,)),
            dma((n_row // 2,)),
            dma((2,)),
            dma,
            dma((LAYERS,)),
            dma((2,)),
            dma((LAYERS,)),
            dma((LAYERS,)),
            dma((2, LAYERS)),
            dma((2,)),
            dma((LAYERS,)),
            dma,
            dma((2, 2, SIDE - 1)),
            dma((2, 2, SIDE - 1)),
            dma((2, 2, SIDE - 1)),
            dma((2, 2, SIDE - 1)),
            dma((2, 2)),
            dma((2, 2)),
            dma((2, CHUNKS)),
            dma((2, CHUNKS)),
            dma((2, CHUNKS)),
            dma((2, CHUNKS)),
            dma((LAYERS,)),
            dma((2,)),
            dma((4,)),
            dma((2, 4)),
            dma((4, SIDE - 1)),
            dma((2, 4, SIDE - 1)),
            dma((4, SIDE - 1)),
            dma((2, 4, SIDE - 1)),
            dma((4,)),
            dma((4, LAYERS - 1)),
        ],
        compiler_params=pltpu.CompilerParams(
            collective_id=0, has_side_effects=True, vmem_limit_bytes=67043328
        ),
    )(
        tokens,
        embed,
        ln_gain,
        w_qkv.reshape(SIDE, 2, width // 8, 3 * width),
        w_out.reshape(SIDE, 2, width // 8, width),
        out_grad.reshape(micro, npos, width),
    )
    grad_qkv, grad_out, grad_gain = pl.pallas_call(
        hand_over,
        out_shape=tuple(jax.ShapeDtypeStruct(g.shape, F32) for g in sums),
        in_specs=[vm, vm, vm],
        out_specs=(vm, vm, vm),
    )(*sums)
    return (grad_qkv, grad_out, grad_gain)


def solution(mesh):
    in_specs = (
        P(None, "row", None),
        P(),
        P("section", None),
        P("section", None, None),
        P("section", None, None),
        P(None, "row", None, None),
    )
    out_specs = (P("section", "row", None), P("section", "row", None), P("section", "row"))
    return jax.shard_map(local, mesh=mesh, in_specs=in_specs, out_specs=out_specs, check_vma=False)
```

```python
import functools

import jax
import jax.numpy as jnp
from jax import lax
from jax.experimental import pallas as pl
from jax.experimental.pallas import tpu as pltpu
from jax.sharding import PartitionSpec as P

HEADS = 12
HEAD_DIM = 64
LAYERS = 4
PAIRS = HEADS // 2
WIDTH = HEADS * HEAD_DIM
SEQ = 128
SIDE = 4
OUT, VAL, QRY, KEY = 0, 1, 2, 3
CHUNKS = 3
NEAR = sorted(
    ((z, y) for z in range(SIDE) for y in range(SIDE) if z or y),
    key=lambda step: sum(min(n, SIDE - n) for n in step),
)
CHUNK = 4 * WIDTH // CHUNKS
HALF = WIDTH // 2
MESH = pl.DeviceIdType.MESH
BF = jnp.bfloat16
F32 = jnp.float32


def dot(a, b, ca, cb):
    return lax.dot_general(a, b, (((ca,), (cb,)), ((), ())), preferred_element_type=F32)


def norm_parts(x):
    centred = x - jnp.mean(x, axis=-1, keepdims=True)
    spread = jnp.mean(centred * centred, axis=-1, keepdims=True)
    rstd = lax.rsqrt(spread + 1e-05)
    return centred * rstd, rstd


def kernel(
    n_row,
    scale,
    tok_ref,
    emb_ref,
    gain_ref,
    wqkv_hbm,
    wout_hbm,
    og_hbm,
    gq_ref,
    go_ref,
    gg_ref,
    wcat,
    gains,
    embp,
    tab,
    xs,
    qkv,
    probs,
    mixed,
    part,
    other,
    both,
    recv,
    dlog,
    dyf,
    ogb,
    dmix,
    dqkv,
    hbuf,
    dhacc,
    grad,
    pairbuf,
    line1,
    sum1,
    line2,
    xout,
    xin,
    fin,
    level_sem,
    rs_send,
    rs_recv,
    ag_send,
    ag_recv,
    hand_send,
    hand_recv,
    w_sem,
    og_sem,
    tab_send,
    tab_recv,
    gain_send,
    gain_recv,
    deal_send,
    deal_recv,
    s1_send,
    s1_recv,
    s2_send,
    s2_recv,
    join_send,
    join_recv,
    ring_send,
    ring_recv,
    twin_send,
    twin_recv,
    first_send,
    first_recv,
    pair_send,
    pair_recv,
    c1_send,
    c1_recv,
    c2_send,
    c2_recv,
    x_send,
    x_recv,
):
    sec = lax.axis_index("section")
    me = lax.axis_index("row")
    piece = part.shape[0] // n_row
    n_chip = n_row // 2
    core = lax.rem(me, 2)
    partner = me + 1 - 2 * core
    chip = me // 2
    zc = chip // SIDE
    yc = lax.rem(chip, SIDE)

    def row_at(z, y):
        return (z * SIDE + y) * 2 + core

    def weight(l, first, count):
        block = wcat[l, :, :, :, pl.ds(first, count)]
        return block.reshape(WIDTH, count)

    local_qkv = pltpu.make_async_copy(
        wqkv_hbm, wcat.at[sec, :, :, :, pl.ds(0, 3 * WIDTH)], w_sem.at[0]
    )
    local_out = pltpu.make_async_copy(
        wout_hbm, wcat.at[sec, :, :, :, pl.ds(3 * WIDTH, WIDTH)], w_sem.at[1]
    )
    local_qkv.start()
    local_out.start()
    pltpu.make_async_copy(og_hbm.at[sec], ogb, og_sem).start()

    barrier = pltpu.get_barrier_semaphore()

    def greet(d, carry):
        peer = 2 * lax.rem(chip + d, n_chip) + core
        pl.semaphore_signal(barrier, inc=1, device_id=(sec, peer), device_id_type=MESH)
        return carry

    lax.fori_loop(1, n_chip, greet, 0)
    pl.semaphore_signal(barrier, inc=1, device_id=(sec, partner), device_id_type=MESH)
    for d in range(1, LAYERS):
        pl.semaphore_signal(
            barrier, inc=1, device_id=(lax.rem(sec + d, LAYERS), me), device_id_type=MESH
        )

    lane = lax.broadcasted_iota(jnp.int32, (1, SEQ), 1)
    low = (lane < HEAD_DIM).astype(F32).astype(BF)
    high = (lane >= HEAD_DIM).astype(F32).astype(BF)

    gains[sec] = gain_ref[...]
    padded = embp.shape[0]
    embp[...] = jnp.zeros_like(embp)
    embp[pl.ds(0, emb_ref.shape[0]), :] = emb_ref[...]
    ids = lax.broadcasted_iota(jnp.int32, (padded, SEQ), 0)
    tok = tok_ref[sec]
    picks = jnp.concatenate([(tok[r : r + 1] == ids) for r in range(2)], axis=1)
    picks = picks.astype(F32).astype(BF)
    xs[0] = dot(picks, embp[...], 0, 0)

    local_qkv.wait()

    @pl.when(sec == 0)
    def _():
        normal, _ = norm_parts(embp[...].astype(F32))
        h = (normal * gain_ref[...]).astype(BF)
        for n in range(3):
            made = dot(h, weight(0, WIDTH * n, WIDTH), 1, 0).astype(BF)
            for half in range(2):
                cols = pl.ds(HALF * n, HALF)
                tab[half, :, cols] = made[:, HALF * half : HALF * (half + 1)]

    local_out.wait()
    pl.semaphore_wait(barrier, n_chip + LAYERS - 1)

    def tab_copy(t):
        return pltpu.make_async_remote_copy(
            src_ref=tab.at[core],
            dst_ref=tab.at[core],
            send_sem=tab_send.at[t],
            recv_sem=tab_recv.at[0],
            device_id=(t, me),
            device_id_type=MESH,
        )

    def tab_twin(who):
        return pltpu.make_async_remote_copy(
            src_ref=tab.at[who],
            dst_ref=tab.at[who],
            send_sem=tab_send.at[0],
            recv_sem=tab_recv.at[1],
            device_id=(sec, partner),
            device_id_type=MESH,
        )

    @pl.when(sec == 0)
    def _():
        for t in range(1, LAYERS):
            tab_copy(t).start()

    def gain_copy(d):
        return pltpu.make_async_remote_copy(
            src_ref=gain_ref,
            dst_ref=gains.at[sec],
            send_sem=gain_send.at[d],
            recv_sem=gain_recv.at[d],
            device_id=(lax.rem(sec + d, LAYERS), me),
            device_id_type=MESH,
        )

    for d in range(1, LAYERS):
        gain_copy(d).start()

    RING = LAYERS - 1

    def flow(d, k, who):
        cols = pl.ds(pl.multiple_of(k * CHUNK, 128), CHUNK)
        return wcat.at[RING, who * 2 + d, 1, :, cols]

    def place(d):
        return lax.rem(sec - RING + LAYERS, LAYERS) if d == 0 else lax.rem(RING - sec, LAYERS)

    def ring_copy(d, k):
        step = 1 if d == 0 else LAYERS - 1
        ref = flow(d, k, core)
        return pltpu.make_async_remote_copy(
            src_ref=ref,
            dst_ref=ref,
            send_sem=ring_send.at[d, k],
            recv_sem=ring_recv.at[d, k],
            device_id=(lax.rem(sec + step, LAYERS), me),
            device_id_type=MESH,
        )

    def twin_copy(d, k, who):
        ref = flow(d, k, who)
        return pltpu.make_async_remote_copy(
            src_ref=ref,
            dst_ref=ref,
            send_sem=twin_send.at[d, k],
            recv_sem=twin_recv.at[d, k],
            device_id=(sec, partner),
            device_id_type=MESH,
        )

    def launch_flow():
        @pl.when(sec == RING)
        def _():
            for k in range(CHUNKS):
                for d in range(2):
                    ring_copy(d, k).start()

    def pump(slot):
        for d in range(2):
            at = place(d)
            k = slot - at

            @pl.when((at > 0) & (k >= 0) & (k < CHUNKS))
            def _():
                ring_copy(d, k).wait_recv()

                @pl.when(at < LAYERS - 1)
                def _():
                    ring_copy(d, k).start()

                twin_copy(d, k, core).start()

    def settle():
        @pl.when(sec != RING)
        def _():
            for k in range(CHUNKS):
                for d in range(2):
                    twin_copy(d, k, 1 - core).wait_recv()

    def drain():
        def one(k, carry):
            for d in range(2):
                at = place(d)

                @pl.when(at < LAYERS - 1)
                def _():
                    ring_copy(d, k).wait_send()

                @pl.when(at > 0)
                def _():
                    twin_copy(d, k, core).wait_send()

            return carry

        lax.fori_loop(0, CHUNKS, one, 0)

    def first_ref(who):
        return wcat.at[0, pl.ds(2 * who, 2), :, :, pl.ds(3 * WIDTH, WIDTH)]

    def first_copy(t):
        return pltpu.make_async_remote_copy(
            src_ref=first_ref(core),
            dst_ref=first_ref(core),
            send_sem=first_send.at[t],
            recv_sem=first_recv.at[0],
            device_id=(t, me),
            device_id_type=MESH,
        )

    def first_twin(who):
        return pltpu.make_async_remote_copy(
            src_ref=first_ref(who),
            dst_ref=first_ref(who),
            send_sem=first_send.at[0],
            recv_sem=first_recv.at[1],
            device_id=(sec, partner),
            device_id_type=MESH,
        )

    block_cols = pl.ds(pl.multiple_of((core * SIDE + yc) * HALF, 128), HALF)

    def side_cols(who):
        return pl.ds(pl.multiple_of(who * (2 * WIDTH), 128), 2 * WIDTH)

    def parts_of(w):
        return 1 if w == RING else 2

    def deal_copy(w, d):
        ref = wcat.at[w, zc, pl.ds(0, parts_of(w)), :, block_cols]
        return pltpu.make_async_remote_copy(
            src_ref=ref,
            dst_ref=ref,
            send_sem=deal_send.at[w - 1, d],
            recv_sem=deal_recv.at[w - 1],
            device_id=((w + d) % LAYERS, me),
            device_id_type=MESH,
        )

    def line_copy(w, stage, half, d):
        along_y = (stage + half) % 2 == 0
        y = lax.rem(yc + d, SIDE) if along_y else yc
        z = zc if along_y else lax.rem(zc + d, SIDE)
        if stage == 0:
            ref = wcat.at[w, zc, half, :, block_cols]
        elif along_y:
            ref = wcat.at[w, :, half, :, block_cols]
        else:
            ref = wcat.at[w, zc, half, :, side_cols(core)]
        send, take = (s1_send, s1_recv) if stage == 0 else (s2_send, s2_recv)
        return pltpu.make_async_remote_copy(
            src_ref=ref,
            dst_ref=ref,
            send_sem=send.at[w - 1, half, d - 1],
            recv_sem=take.at[w - 1, half, d - 1],
            device_id=(sec, row_at(z, y)),
            device_id_type=MESH,
        )

    def join_copy(w, half, who):
        ref = wcat.at[w, :, half, :, side_cols(who)]
        return pltpu.make_async_remote_copy(
            src_ref=ref,
            dst_ref=ref,
            send_sem=join_send.at[w - 1, half],
            recv_sem=join_recv.at[w - 1, half],
            device_id=(sec, partner),
            device_id_type=MESH,
        )

    def plane_one(w):
        @pl.when(sec != w)
        def _():
            deal_copy(w, 0).wait_recv()
            for half in range(parts_of(w)):
                for d in range(1, SIDE):
                    line_copy(w, 0, half, d).start()

    def plane_two(w, half):
        @pl.when(sec != w)
        def _():
            for d in range(1, SIDE):
                line_copy(w, 0, half, d).wait_recv()
            for d in range(1, SIDE):
                line_copy(w, 1, half, d).start()

    def plane_three(w, half):
        @pl.when(sec != w)
        def _():
            for d in range(1, SIDE):
                line_copy(w, 1, half, d).wait_recv()
            join_copy(w, half, core).start()

    def plane_settle(w):
        @pl.when(sec != w)
        def _():
            for half in range(parts_of(w)):
                join_copy(w, half, 1 - core).wait_recv()

    def plane_drain(w):
        @pl.when(sec != w)
        def _():
            for half in range(parts_of(w)):
                for d in range(1, SIDE):
                    line_copy(w, 0, half, d).wait_send()
                    line_copy(w, 1, half, d).wait_send()
                join_copy(w, half, core).wait_send()

        @pl.when(sec == w)
        def _():
            for d in range(1, LAYERS):
                deal_copy(w, d).wait_send()

    def rows_of(k):
        return pl.ds(pl.multiple_of(k * piece, 16), piece)

    def half_rows(who):
        return pl.ds(pl.multiple_of(who * (n_chip * piece), 16), n_chip * piece)

    own_block = rows_of(core * n_chip + chip)

    def split_block(a0, a1):
        top = jnp.concatenate([a0 * low, a1 * low], axis=1)
        bottom = jnp.concatenate([a0 * high, a1 * high], axis=1)
        return jnp.concatenate([top, bottom], axis=0)

    def pair_scores(left, right, factor):
        for p in range(PAIRS):
            la, ra = left(p), right(p)
            out = dot(split_block(*la), jnp.concatenate(ra, axis=1), 1, 1)
            if factor is not None:
                out = factor * out
            part[pl.ds(2 * SEQ * p, 2 * SEQ), :] = out.astype(BF)

    def level_copy():
        return pltpu.make_async_remote_copy(
            src_ref=part.at[half_rows(1 - core)],
            dst_ref=other,
            send_sem=level_sem.at[0],
            recv_sem=level_sem.at[1],
            device_id=(sec, partner),
            device_id_type=MESH,
        )

    def chip_at(step, sign):
        z, y = ((sign * n) % SIDE for n in step)
        return lax.rem(zc + z, SIDE) * SIDE + lax.rem(yc + y, SIDE)

    def rs_copy(d):
        to = chip_at(NEAR[d - 1], 1)
        return pltpu.make_async_remote_copy(
            src_ref=both.at[rows_of(to)],
            dst_ref=recv.at[d],
            send_sem=rs_send.at[d],
            recv_sem=rs_recv.at[d],
            device_id=(sec, 2 * to + core),
            device_id_type=MESH,
        )

    def start_reduce():
        level_copy().start()
        mine = part[half_rows(core), :].astype(F32)
        level_copy().wait_recv()
        both[...] = (mine + other[...].astype(F32)).astype(BF)
        for d in reversed(range(1, n_chip)):
            rs_copy(d).start()

    def finish_reduce():
        total = both[rows_of(chip), :].astype(F32)
        for d in range(1, n_chip):
            rs_copy(d).wait_recv()
            total = total + recv[d].astype(F32)
        return total

    def ag_copy(buf, d):
        to = chip_at(NEAR[d - 1], 1)
        return pltpu.make_async_remote_copy(
            src_ref=buf.at[own_block],
            dst_ref=buf.at[own_block],
            send_sem=ag_send.at[d],
            recv_sem=ag_recv.at[d],
            device_id=(sec, 2 * to + core),
            device_id_type=MESH,
        )

    def hand_copy(buf, d):
        source = chip_at(NEAR[d - 1], -1) if d else chip
        block = rows_of(core * n_chip + source)
        return pltpu.make_async_remote_copy(
            src_ref=buf.at[block],
            dst_ref=buf.at[block],
            send_sem=hand_send.at[d],
            recv_sem=hand_recv.at[d],
            device_id=(sec, partner),
            device_id_type=MESH,
        )

    def start_gather(buf):
        for d in reversed(range(1, n_chip)):
            ag_copy(buf, d).start()
        hand_copy(buf, 0).start()

    def finish_gather(buf):
        for d in range(1, n_chip):
            ag_copy(buf, d).wait_recv()
            hand_copy(buf, d).start()
        for d in range(n_chip):
            hand_copy(buf, d).wait_recv()

    def clear_exchange(buf):
        for d in range(n_chip):
            hand_copy(buf, d).wait_send()
        for d in range(1, n_chip):
            rs_copy(d).wait_send()
            ag_copy(buf, d).wait_send()
        level_copy().wait_send()

    def halves(ref, base, p):
        cols = pl.ds(base + SEQ * p, SEQ)
        return ref[pl.ds(0, SEQ), cols], ref[pl.ds(SEQ, SEQ), cols]

    def beside(buf, p):
        return jnp.concatenate(
            [buf[pl.ds(2 * SEQ * p, SEQ), :], buf[pl.ds(2 * SEQ * p + SEQ, SEQ), :]], axis=1
        )

    def put_halves(ref, base, p, value):
        cols = pl.ds(base + SEQ * p, SEQ)
        ref[pl.ds(0, SEQ), cols] = value[:, :SEQ]
        ref[pl.ds(SEQ, SEQ), cols] = value[:, SEQ:]

    own_rows = WIDTH // n_row

    def put_grad(u, value):
        for r in range(n_row):
            q = r // 2
            grad[u, r % 2, q // SIDE, q % SIDE] = value[own_rows * r : own_rows * (r + 1)].astype(BF)

    def pair_copy(u, par):
        return pltpu.make_async_remote_copy(
            src_ref=grad.at[u, 1 - core],
            dst_ref=pairbuf.at[par, u],
            send_sem=pair_send.at[u],
            recv_sem=pair_recv.at[par, u],
            device_id=(sec, partner),
            device_id_type=MESH,
        )

    def y_first(u):
        return u % 2 == 0

    def c1_copy(u, par, d):
        if y_first(u):
            y = lax.rem(yc + d, SIDE)
            src, peer = grad.at[u, core, :, y], row_at(zc, y)
        else:
            z = lax.rem(zc + d, SIDE)
            src, peer = grad.at[u, core, z], row_at(z, yc)
        return pltpu.make_async_remote_copy(
            src_ref=src,
            dst_ref=line1.at[par, u, d - 1],
            send_sem=c1_send.at[u, d - 1],
            recv_sem=c1_recv.at[par, u, d - 1],
            device_id=(sec, peer),
            device_id_type=MESH,
        )

    def c2_copy(u, par, d):
        if y_first(u):
            at = lax.rem(zc + d, SIDE)
            peer = row_at(at, yc)
        else:
            at = lax.rem(yc + d, SIDE)
            peer = row_at(zc, at)
        return pltpu.make_async_remote_copy(
            src_ref=sum1.at[par, u, at],
            dst_ref=line2.at[par, u, d - 1],
            send_sem=c2_send.at[u, d - 1],
            recv_sem=c2_recv.at[par, u, d - 1],
            device_id=(sec, peer),
            device_id_type=MESH,
        )

    def x_copy(u, t):
        owner = LAYERS - 1 - t
        return pltpu.make_async_remote_copy(
            src_ref=xout.at[u],
            dst_ref=xin.at[u, lax.rem(sec - owner + LAYERS - 1 + LAYERS, LAYERS)],
            send_sem=x_send.at[u],
            recv_sem=x_recv.at[u, lax.rem(sec - owner + LAYERS - 1 + LAYERS, LAYERS)],
            device_id=(owner, me),
            device_id_type=MESH,
        )

    def stage_pair(u, t):
        pair_copy(u, t % 2).start()

    def stage_one(u, t):
        par = t % 2
        pair_copy(u, par).wait_recv()
        pair_copy(u, par).wait_send()
        for z in range(SIDE):
            total = grad[u, core, z].astype(F32) + pairbuf[par, u, z].astype(F32)
            grad[u, core, z] = total.astype(BF)
        for d in range(1, SIDE):
            c1_copy(u, par, d).start()

    def stage_two(u, t):
        par = t % 2
        for d in range(1, SIDE):
            c1_copy(u, par, d).wait_recv()
            c1_copy(u, par, d).wait_send()
        for k in range(SIDE):
            own = grad[u, core, k, yc] if y_first(u) else grad[u, core, zc, k]
            total = own.astype(F32)
            for d in range(SIDE - 1):
                total = total + line1[par, u, d, k].astype(F32)
            sum1[par, u, k] = total.astype(BF)
        for d in range(1, SIDE):
            c2_copy(u, par, d).start()

    def stage_three(u, t):
        par = t % 2
        owner = LAYERS - 1 - t
        for d in range(1, SIDE):
            c2_copy(u, par, d).wait_recv()
            c2_copy(u, par, d).wait_send()
        total = sum1[par, u, zc if y_first(u) else yc].astype(F32)
        for d in range(SIDE - 1):
            total = total + line2[par, u, d].astype(F32)

        @pl.when((t > 0) & (sec != owner + 1))
        def _():
            x_copy(u, t - 1).wait_send()

        @pl.when(sec == owner)
        def _():
            fin[u] = total

        @pl.when(sec != owner)
        def _():
            xout[u] = total.astype(BF)
            x_copy(u, t).start()

    for w in (1, 2, 3):

        @pl.when(sec == w)
        def _():
            for d in range(1, LAYERS):
                deal_copy(w, d).start()

    @pl.when(sec == 0)
    def _():
        for t in (1, 3, 2):
            first_copy(t).start()

    launch_flow()

    def forward(l, carry):
        here = qkv.at[l]

        @pl.when(l == 0)
        def _():
            @pl.when(sec > 0)
            def _():
                tab_copy(0).wait_recv()
                tab_twin(core).start()
                tab_twin(1 - core).wait_recv()

            for d in range(1, LAYERS):
                gain_copy(d).wait_recv()
            for n in range(3):
                for half in range(2):
                    made = dot(picks, tab[half, :, pl.ds(HALF * n, HALF)], 0, 0)
                    here[:, pl.ds(WIDTH * n + HALF * half, HALF)] = made.astype(BF)

        @pl.when(l > 0)
        def _():
            for w in (1, 2, 3):
                pl.when(l == w)(functools.partial(plane_settle, w))

            @pl.when(l == RING)
            def _():
                settle()

            normal, _ = norm_parts(xs[l])
            h = (normal * gains[l]).astype(BF)
            for n in range(3):
                cols = pl.ds(WIDTH * n, WIDTH)
                here[:, cols] = dot(h, weight(l, WIDTH * n, WIDTH), 1, 0).astype(BF)

        pair_scores(lambda p: halves(here, 0, p), lambda p: halves(here, WIDTH, p), scale)
        start_reduce()

        @pl.when(l == 0)
        def _():
            plane_one(1)
            plane_two(1, 0)

        @pl.when(l == 1)
        def _():
            plane_two(2, 0)

        @pl.when(l == 2)
        def _():
            plane_two(3, 0)

        for turn in range(3):
            pl.when(l == turn)(functools.partial(pump, 2 * turn + 1))

        logits = finish_reduce()
        shifted = jnp.exp(logits - jnp.max(logits, axis=-1, keepdims=True))
        own = shifted / jnp.sum(shifted, axis=-1, keepdims=True)
        probs_l = probs.at[l]
        probs_l[own_block, :] = own.astype(BF)
        start_gather(probs_l)

        @pl.when(l == 0)
        def _():
            plane_two(1, 1)
            plane_one(2)

        @pl.when(l == 1)
        def _():
            plane_two(2, 1)
            plane_one(3)

        for turn in range(2):
            pl.when(l == turn)(functools.partial(pump, 2 * turn + 2))

        finish_gather(probs_l)
        clear_exchange(probs_l)
        mixed_l = mixed.at[l]
        for p in range(PAIRS):
            out = dot(beside(probs_l, p), split_block(*halves(here, 2 * WIDTH, p)), 1, 0)
            put_halves(mixed_l, 0, p, out.astype(BF))

        @pl.when(l == 0)
        def _():
            @pl.when(sec > 0)
            def _():
                first_copy(0).wait_recv()
                first_twin(core).start()

            plane_three(1, 0)

            @pl.when(sec > 0)
            def _():
                first_twin(1 - core).wait_recv()

        @pl.when(l == 1)
        def _():
            plane_three(2, 0)

        @pl.when(l < LAYERS - 1)
        def _():
            xs[l + 1] = xs[l] + dot(mixed_l[...], weight(l, 3 * WIDTH, WIDTH), 1, 0)

        @pl.when(l == 0)
        def _():
            plane_three(1, 1)

        @pl.when(l == 1)
        def _():
            plane_three(2, 1)

        @pl.when(l == 2)
        def _():
            plane_three(3, 0)

        return carry

    lax.fori_loop(0, LAYERS, forward, 0)

    pltpu.make_async_copy(og_hbm.at[sec], ogb, og_sem).wait()
    dyf[...] = ogb[...].astype(F32)

    def reduce_window(step):
        def previous():
            t = step - 1
            for u, n in ((QRY, 0), (KEY, 1)):
                put_grad(u, dot(hbuf[...], dqkv[:, pl.ds(WIDTH * n, WIDTH)], 0, 0))
                stage_pair(u, t)
            for u in (OUT, VAL):
                stage_one(u, t)

        def older():
            t = step - 2
            for u in (OUT, VAL):
                stage_three(u, t)
            for u in (QRY, KEY):
                stage_two(u, t)

        return older, previous

    def gather_window(step):
        def previous():
            t = step - 1
            for u in (OUT, VAL):
                stage_two(u, t)
            for u in (QRY, KEY):
                stage_one(u, t)

        def older():
            t = step - 2
            for u in (QRY, KEY):
                stage_three(u, t)

        return previous, older

    def backward(step, carry):
        l = LAYERS - 1 - step
        here = qkv.at[l]
        probs_l = probs.at[l]
        dyb = dyf[...].astype(BF)
        dmix[...] = dot(dyb, weight(l, 3 * WIDTH, WIDTH), 1, 1).astype(BF)
        pair_scores(lambda p: halves(dmix, 0, p), lambda p: halves(here, 2 * WIDTH, p), None)
        start_reduce()

        older, previous = reduce_window(step)
        pl.when(step >= 2)(older)
        pl.when(step >= 1)(previous)
        for p in range(PAIRS):
            rows = pl.ds(2 * SEQ * p, 2 * SEQ)
            out = dot(probs_l[rows, :], split_block(*halves(dmix, 0, p)), 0, 0)
            put_halves(dqkv, 2 * WIDTH, p, out.astype(BF))
        dprobs = finish_reduce()
        own = probs_l[own_block, :].astype(F32)
        inner = jnp.sum(dprobs * own, axis=-1, keepdims=True)
        dlog[own_block, :] = (own * (dprobs - inner)).astype(BF)
        start_gather(dlog)

        normal, rstd = norm_parts(xs[l])
        hbuf[...] = (normal * gains[l]).astype(BF)
        vcols = pl.ds(2 * WIDTH, WIDTH)
        previous, older = gather_window(step)
        pl.when(step >= 1)(previous)
        put_grad(OUT, dot(mixed[l], dyb, 0, 0))
        put_grad(VAL, dot(hbuf[...], dqkv[:, vcols], 0, 0))
        for u in (OUT, VAL):
            stage_pair(u, step)

        @pl.when(l > 0)
        def _():
            dhacc[...] = dot(dqkv[:, vcols], weight(l, 2 * WIDTH, WIDTH), 1, 1)

        pl.when(step >= 2)(older)
        finish_gather(dlog)
        clear_exchange(dlog)

        for p in range(PAIRS):
            out = dot(beside(dlog, p), split_block(*halves(here, WIDTH, p)), 1, 0)
            put_halves(dqkv, 0, p, (scale * out).astype(BF))
            rows = pl.ds(2 * SEQ * p, 2 * SEQ)
            out = dot(dlog[rows, :], split_block(*halves(here, 0, p)), 0, 0)
            put_halves(dqkv, WIDTH, p, (scale * out).astype(BF))
        qk = pl.ds(0, 2 * WIDTH)

        @pl.when(l > 0)
        def _():
            dh = dhacc[...] + dot(dqkv[:, qk], weight(l, 0, 2 * WIDTH), 1, 1)
            dn = dh.astype(BF).astype(F32) * gains[l]
            first = jnp.mean(dn, axis=-1, keepdims=True)
            second = jnp.mean(dn * normal, axis=-1, keepdims=True)
            dyf[...] = dyf[...] + rstd * (dn - first - normal * second)

        return carry

    lax.fori_loop(0, LAYERS, backward, 0)

    for work in reduce_window(LAYERS) + gather_window(LAYERS):
        work()
    reduce_window(LAYERS + 1)[0]()
    gather_window(LAYERS + 1)[1]()

    for u in range(4):

        @pl.when(sec != 0)
        def _():
            x_copy(u, LAYERS - 1).wait_send()

        total = fin[u]
        for slot in range(LAYERS - 1):
            pltpu.make_async_remote_copy(
                src_ref=xout.at[u],
                dst_ref=xin.at[u, slot],
                send_sem=x_send.at[u],
                recv_sem=x_recv.at[u, slot],
                device_id=(lax.rem(sec + 1, LAYERS), me),
                device_id_type=MESH,
            ).wait_recv()
            total = total + xin[u, slot].astype(F32)
        if u == OUT:
            go_ref[0] = total
        else:
            gq_ref[0, :, pl.ds(WIDTH * {VAL: 2, QRY: 0, KEY: 1}[u], WIDTH)] = total

    tall = wcat[sec, zc, yc // 2, pl.ds(pl.multiple_of(2 * own_rows * lax.rem(yc, 2), 16), 2 * own_rows), :]
    tall = tall[:, : 3 * WIDTH].astype(F32)
    w_own = jnp.where(core == 0, tall[:own_rows], tall[own_rows:])
    dotted = jnp.sum(w_own * gq_ref[0], axis=-1, keepdims=True)
    lanes = lax.broadcasted_iota(jnp.int32, (own_rows, WIDTH), 1)
    subs = lax.broadcasted_iota(jnp.int32, (own_rows, WIDTH), 0)
    gain_own = jnp.sum(
        jnp.where(lanes == subs + own_rows * me, gain_ref[...], 0.0), axis=-1, keepdims=True
    )
    spread = jnp.where(lanes == subs, dotted / gain_own, 0.0)
    gg_ref[...] = jnp.sum(spread, axis=0, keepdims=True)[:, :own_rows]

    drain()
    for w in (1, 2, 3):
        plane_drain(w)

    @pl.when(sec == 0)
    def _():
        for t in range(1, LAYERS):
            tab_copy(t).wait_send()
            first_copy(t).wait_send()

    @pl.when(sec > 0)
    def _():
        tab_twin(core).wait_send()
        first_twin(core).wait_send()

    for d in range(1, LAYERS):
        gain_copy(d).wait_send()


def hand_over(qkv_in, out_in, gain_in, qkv_out, out_out, gain_out):
    qkv_out[...] = qkv_in[...]
    out_out[...] = out_in[...]
    gain_out[...] = gain_in[...]


def local(tokens, embed, ln_gain, w_qkv, w_out, out_grad):
    n_row = lax.axis_size("row")
    micro, rows_here, seq = tokens.shape
    vocab, width = embed.shape
    npos = rows_here * seq
    scale = HEAD_DIM ** (-0.5) / (rows_here * n_row) ** 0.5
    padded = vocab + -vocab % 16
    flat = HEADS * seq
    own_rows = width // n_row
    vm, anyspace = pl.BlockSpec(memory_space=pltpu.VMEM), pl.BlockSpec(memory_space=pl.ANY)
    dma = pltpu.SemaphoreType.DMA
    sums = pl.pallas_call(
        functools.partial(kernel, n_row, scale),
        out_shape=(
            jax.ShapeDtypeStruct((1, own_rows, 3 * width), F32),
            jax.ShapeDtypeStruct((1, own_rows, width), F32),
            jax.ShapeDtypeStruct((1, own_rows), F32),
        ),
        in_specs=[vm, vm, vm, anyspace, anyspace, anyspace],
        out_specs=(vm, vm, vm),
        scratch_shapes=[
            pltpu.VMEM((LAYERS, SIDE, 2, width // 8, 4 * width), BF),
            pltpu.VMEM((LAYERS, 1, width), F32),
            pltpu.VMEM((padded, width), BF),
            pltpu.VMEM((2, padded, 3 * width // 2), BF),
            pltpu.VMEM((LAYERS, npos, width), F32),
            pltpu.VMEM((LAYERS, npos, 3 * width), BF),
            pltpu.VMEM((LAYERS, flat, seq), BF),
            pltpu.VMEM((LAYERS, npos, width), BF),
            pltpu.VMEM((flat, seq), BF),
            pltpu.VMEM((flat // 2, seq), BF),
            pltpu.VMEM((flat // 2, seq), BF),
            pltpu.VMEM((n_row // 2, flat // n_row, seq), BF),
            pltpu.VMEM((flat, seq), BF),
            pltpu.VMEM((npos, width), F32),
            pltpu.VMEM((npos, width), BF),
            pltpu.VMEM((npos, width), BF),
            pltpu.VMEM((npos, 3 * width), BF),
            pltpu.VMEM((npos, width), BF),
            pltpu.VMEM((npos, width), F32),
            pltpu.VMEM((4, 2, SIDE, SIDE, own_rows, width), BF),
            pltpu.VMEM((2, 4, SIDE, SIDE, own_rows, width), BF),
            pltpu.VMEM((2, 4, SIDE - 1, SIDE, own_rows, width), BF),
            pltpu.VMEM((2, 4, SIDE, own_rows, width), BF),
            pltpu.VMEM((2, 4, SIDE - 1, own_rows, width), BF),
            pltpu.VMEM((4, own_rows, width), BF),
            pltpu.VMEM((4, LAYERS - 1, own_rows, width), BF),
            pltpu.VMEM((4, own_rows, width), F32),
            dma((2,)),
            dma((n_row // 2,)),
            dma((n_row // 2,)),
            dma((n_row // 2,)),
            dma((n_row // 2,)),
            dma((n_row // 2,)),
            dma((n_row // 2,)),
            dma((2,)),
            dma,
            dma((LAYERS,)),
            dma((2,)),
            dma((LAYERS,)),
            dma((LAYERS,)),
            dma((3, LAYERS)),
            dma((3,)),
            dma((3, 2, SIDE - 1)),
            dma((3, 2, SIDE - 1)),
            dma((3, 2, SIDE - 1)),
            dma((3, 2, SIDE - 1)),
            dma((3, 2)),
            dma((3, 2)),
            dma((2, CHUNKS)),
            dma((2, CHUNKS)),
            dma((2, CHUNKS)),
            dma((2, CHUNKS)),
            dma((LAYERS,)),
            dma((2,)),
            dma((4,)),
            dma((2, 4)),
            dma((4, SIDE - 1)),
            dma((2, 4, SIDE - 1)),
            dma((4, SIDE - 1)),
            dma((2, 4, SIDE - 1)),
            dma((4,)),
            dma((4, LAYERS - 1)),
        ],
        compiler_params=pltpu.CompilerParams(
            collective_id=0, has_side_effects=True, vmem_limit_bytes=67043328
        ),
    )(
        tokens,
        embed,
        ln_gain,
        w_qkv.reshape(SIDE, 2, width // 8, 3 * width),
        w_out.reshape(SIDE, 2, width // 8, width),
        out_grad.reshape(micro, npos, width),
    )
    grad_qkv, grad_out, grad_gain = pl.pallas_call(
        hand_over,
        out_shape=tuple(jax.ShapeDtypeStruct(g.shape, F32) for g in sums),
        in_specs=[vm, vm, vm],
        out_specs=(vm, vm, vm),
    )(*sums)
    return (grad_qkv, grad_out, grad_gain)


def solution(mesh):
    in_specs = (
        P(None, "row", None),
        P(),
        P("section", None),
        P("section", None, None),
        P("section", None, None),
        P(None, "row", None, None),
    )
    out_specs = (P("section", "row", None), P("section", "row", None), P("section", "row"))
    return jax.shard_map(local, mesh=mesh, in_specs=in_specs, out_specs=out_specs, check_vma=False)
```

```python
import functools

import jax
import jax.numpy as jnp
from jax import lax
from jax.experimental import pallas as pl
from jax.experimental.pallas import tpu as pltpu
from jax.sharding import PartitionSpec as P

HEADS = 12
HEAD_DIM = 64
LAYERS = 4
PAIRS = HEADS // 2
WIDTH = HEADS * HEAD_DIM
SEQ = 128
SIDE = 4
OUT, VAL, QRY, KEY = 0, 1, 2, 3
CHUNKS = 3
NEAR = sorted(
    ((z, y) for z in range(SIDE) for y in range(SIDE) if z or y),
    key=lambda step: sum(min(n, SIDE - n) for n in step),
)
CHUNK = 4 * WIDTH // CHUNKS
HALF = WIDTH // 2
MESH = pl.DeviceIdType.MESH
BF = jnp.bfloat16
F32 = jnp.float32


def dot(a, b, ca, cb):
    return lax.dot_general(a, b, (((ca,), (cb,)), ((), ())), preferred_element_type=F32)


def norm_parts(x):
    centred = x - jnp.mean(x, axis=-1, keepdims=True)
    spread = jnp.mean(centred * centred, axis=-1, keepdims=True)
    rstd = lax.rsqrt(spread + 1e-05)
    return centred * rstd, rstd


def kernel(
    n_row,
    scale,
    tok_ref,
    emb_ref,
    gain_ref,
    wqkv_hbm,
    wout_hbm,
    og_hbm,
    gq_ref,
    go_ref,
    gg_ref,
    wcat,
    gains,
    embp,
    tab,
    xs,
    qkv,
    probs,
    mixed,
    part,
    other,
    both,
    recv,
    dlog,
    dyf,
    ogb,
    dmix,
    dqkv,
    hbuf,
    dhacc,
    grad,
    pairbuf,
    line1,
    sum1,
    line2,
    xout,
    xin,
    fin,
    level_sem,
    rs_send,
    rs_recv,
    ag_send,
    ag_recv,
    hand_send,
    hand_recv,
    w_sem,
    og_sem,
    tab_send,
    tab_recv,
    gain_send,
    gain_recv,
    deal_send,
    deal_recv,
    bulk_send,
    bulk_recv,
    s1_send,
    s1_recv,
    s2_send,
    s2_recv,
    join_send,
    join_recv,
    ring_send,
    ring_recv,
    twin_send,
    twin_recv,
    first_send,
    first_recv,
    pair_send,
    pair_recv,
    c1_send,
    c1_recv,
    c2_send,
    c2_recv,
    x_send,
    x_recv,
):
    sec = lax.axis_index("section")
    me = lax.axis_index("row")
    piece = part.shape[0] // n_row
    n_chip = n_row // 2
    core = lax.rem(me, 2)
    partner = me + 1 - 2 * core
    chip = me // 2
    zc = chip // SIDE
    yc = lax.rem(chip, SIDE)

    def row_at(z, y):
        return (z * SIDE + y) * 2 + core

    def weight(l, first, count):
        block = wcat[l, :, :, :, pl.ds(first, count)]
        return block.reshape(WIDTH, count)

    local_qkv = pltpu.make_async_copy(
        wqkv_hbm, wcat.at[sec, :, :, :, pl.ds(0, 3 * WIDTH)], w_sem.at[0]
    )
    local_out = pltpu.make_async_copy(
        wout_hbm, wcat.at[sec, :, :, :, pl.ds(3 * WIDTH, WIDTH)], w_sem.at[1]
    )
    local_qkv.start()
    local_out.start()
    pltpu.make_async_copy(og_hbm.at[sec], ogb, og_sem).start()

    barrier = pltpu.get_barrier_semaphore()

    def greet(d, carry):
        peer = 2 * lax.rem(chip + d, n_chip) + core
        pl.semaphore_signal(barrier, inc=1, device_id=(sec, peer), device_id_type=MESH)
        return carry

    lax.fori_loop(1, n_chip, greet, 0)
    pl.semaphore_signal(barrier, inc=1, device_id=(sec, partner), device_id_type=MESH)
    for d in range(1, LAYERS):
        pl.semaphore_signal(
            barrier, inc=1, device_id=(lax.rem(sec + d, LAYERS), me), device_id_type=MESH
        )

    lane = lax.broadcasted_iota(jnp.int32, (1, SEQ), 1)
    low = (lane < HEAD_DIM).astype(F32).astype(BF)
    high = (lane >= HEAD_DIM).astype(F32).astype(BF)

    gains[sec] = gain_ref[...]
    padded = embp.shape[0]
    embp[...] = jnp.zeros_like(embp)
    embp[pl.ds(0, emb_ref.shape[0]), :] = emb_ref[...]
    ids = lax.broadcasted_iota(jnp.int32, (padded, SEQ), 0)
    tok = tok_ref[sec]
    picks = jnp.concatenate([(tok[r : r + 1] == ids) for r in range(2)], axis=1)
    picks = picks.astype(F32).astype(BF)
    xs[0] = dot(picks, embp[...], 0, 0)

    local_qkv.wait()

    @pl.when(sec == 0)
    def _():
        normal, _ = norm_parts(embp[...].astype(F32))
        h = (normal * gain_ref[...]).astype(BF)
        for n in range(3):
            made = dot(h, weight(0, WIDTH * n, WIDTH), 1, 0).astype(BF)
            for half in range(2):
                cols = pl.ds(HALF * n, HALF)
                tab[half, :, cols] = made[:, HALF * half : HALF * (half + 1)]

    local_out.wait()
    pl.semaphore_wait(barrier, n_chip + LAYERS - 1)

    def tab_part(who, late):
        return tab.at[who, :, pl.ds(2 * HALF, HALF) if late else pl.ds(0, 2 * HALF)]

    def tab_copy(t, late):
        return pltpu.make_async_remote_copy(
            src_ref=tab_part(core, late),
            dst_ref=tab_part(core, late),
            send_sem=tab_send.at[late, t],
            recv_sem=tab_recv.at[late, 0],
            device_id=(t, me),
            device_id_type=MESH,
        )

    def tab_twin(who, late):
        return pltpu.make_async_remote_copy(
            src_ref=tab_part(who, late),
            dst_ref=tab_part(who, late),
            send_sem=tab_send.at[late, 0],
            recv_sem=tab_recv.at[late, 1],
            device_id=(sec, partner),
            device_id_type=MESH,
        )

    def tab_take(late):
        @pl.when(sec > 0)
        def _():
            tab_copy(0, late).wait_recv()
            tab_twin(core, late).start()
            tab_twin(1 - core, late).wait_recv()

    def tab_pick(here, n):
        for half in range(2):
            made = dot(picks, tab[half, :, pl.ds(HALF * n, HALF)], 0, 0)
            here[:, pl.ds(WIDTH * n + HALF * half, HALF)] = made.astype(BF)

    @pl.when(sec == 0)
    def _():
        for late in range(2):
            for t in range(1, LAYERS):
                tab_copy(t, late).start()

    def gain_copy(d):
        return pltpu.make_async_remote_copy(
            src_ref=gain_ref,
            dst_ref=gains.at[sec],
            send_sem=gain_send.at[d],
            recv_sem=gain_recv.at[d],
            device_id=(lax.rem(sec + d, LAYERS), me),
            device_id_type=MESH,
        )

    for d in range(1, LAYERS):
        gain_copy(d).start()

    RING = LAYERS - 1

    def flow(d, k, who):
        cols = pl.ds(pl.multiple_of(k * CHUNK, 128), CHUNK)
        return wcat.at[RING, who * 2 + d, :, :, cols]

    def place(d):
        return lax.rem(sec - RING + LAYERS, LAYERS) if d == 0 else lax.rem(RING - sec, LAYERS)

    def ring_copy(d, k):
        step = 1 if d == 0 else LAYERS - 1
        ref = flow(d, k, core)
        return pltpu.make_async_remote_copy(
            src_ref=ref,
            dst_ref=ref,
            send_sem=ring_send.at[d, k],
            recv_sem=ring_recv.at[d, k],
            device_id=(lax.rem(sec + step, LAYERS), me),
            device_id_type=MESH,
        )

    def twin_copy(d, k, who):
        ref = flow(d, k, who)
        return pltpu.make_async_remote_copy(
            src_ref=ref,
            dst_ref=ref,
            send_sem=twin_send.at[d, k],
            recv_sem=twin_recv.at[d, k],
            device_id=(sec, partner),
            device_id_type=MESH,
        )

    def launch_flow():
        @pl.when(sec == RING)
        def _():
            for k in range(CHUNKS):
                for d in range(2):
                    ring_copy(d, k).start()

    def pump(slot):
        for d in range(2):
            at = place(d)
            k = slot - at

            @pl.when((at > 0) & (k >= 0) & (k < CHUNKS))
            def _():
                ring_copy(d, k).wait_recv()

                @pl.when(at < LAYERS - 1)
                def _():
                    ring_copy(d, k).start()

                twin_copy(d, k, core).start()

    def settle():
        @pl.when(sec != RING)
        def _():
            for k in range(CHUNKS):
                for d in range(2):
                    twin_copy(d, k, 1 - core).wait_recv()

    def drain():
        def one(k, carry):
            for d in range(2):
                at = place(d)

                @pl.when(at < LAYERS - 1)
                def _():
                    ring_copy(d, k).wait_send()

                @pl.when(at > 0)
                def _():
                    twin_copy(d, k, core).wait_send()

            return carry

        lax.fori_loop(0, CHUNKS, one, 0)

    def first_ref(who):
        return wcat.at[0, pl.ds(2 * who, 2), :, :, pl.ds(3 * WIDTH, WIDTH)]

    def first_copy(t):
        return pltpu.make_async_remote_copy(
            src_ref=first_ref(core),
            dst_ref=first_ref(core),
            send_sem=first_send.at[t],
            recv_sem=first_recv.at[0],
            device_id=(t, me),
            device_id_type=MESH,
        )

    def first_twin(who):
        return pltpu.make_async_remote_copy(
            src_ref=first_ref(who),
            dst_ref=first_ref(who),
            send_sem=first_send.at[0],
            recv_sem=first_recv.at[1],
            device_id=(sec, partner),
            device_id_type=MESH,
        )

    block_cols = pl.ds(pl.multiple_of((core * SIDE + yc) * HALF, 128), HALF)

    def side_cols(who):
        return pl.ds(pl.multiple_of(who * (2 * WIDTH), 128), 2 * WIDTH)

    def deal_copy(w, d):
        halves_sent = 2 if w == 1 else 1
        ref = wcat.at[w, zc, pl.ds(0, halves_sent), :, block_cols]
        return pltpu.make_async_remote_copy(
            src_ref=ref,
            dst_ref=ref,
            send_sem=deal_send.at[w - 1, d],
            recv_sem=deal_recv.at[w - 1],
            device_id=((w + d) % LAYERS, me),
            device_id_type=MESH,
        )

    def bulk_copy(d):
        ref = wcat.at[2, :, 1, :, side_cols(core)]
        return pltpu.make_async_remote_copy(
            src_ref=ref,
            dst_ref=ref,
            send_sem=bulk_send.at[d],
            recv_sem=bulk_recv,
            device_id=((2 + d) % LAYERS, me),
            device_id_type=MESH,
        )

    def line_copy(w, stage, half, d):
        along_y = (stage + half) % 2 == 0
        y = lax.rem(yc + d, SIDE) if along_y else yc
        z = zc if along_y else lax.rem(zc + d, SIDE)
        if stage == 0:
            ref = wcat.at[w, zc, half, :, block_cols]
        elif along_y:
            ref = wcat.at[w, :, half, :, block_cols]
        else:
            ref = wcat.at[w, zc, half, :, side_cols(core)]
        send, take = (s1_send, s1_recv) if stage == 0 else (s2_send, s2_recv)
        return pltpu.make_async_remote_copy(
            src_ref=ref,
            dst_ref=ref,
            send_sem=send.at[w - 1, half, d - 1],
            recv_sem=take.at[w - 1, half, d - 1],
            device_id=(sec, row_at(z, y)),
            device_id_type=MESH,
        )

    def join_copy(w, half, who):
        ref = wcat.at[w, :, half, :, side_cols(who)]
        return pltpu.make_async_remote_copy(
            src_ref=ref,
            dst_ref=ref,
            send_sem=join_send.at[w - 1, half],
            recv_sem=join_recv.at[w - 1, half],
            device_id=(sec, partner),
            device_id_type=MESH,
        )

    def plane_one(w):
        @pl.when(sec != w)
        def _():
            deal_copy(w, 0).wait_recv()
            for half in range(2 if w == 1 else 1):
                for d in range(1, SIDE):
                    line_copy(w, 0, half, d).start()

    def plane_two(w, half):
        @pl.when(sec != w)
        def _():
            for d in range(1, SIDE):
                line_copy(w, 0, half, d).wait_recv()
            for d in range(1, SIDE):
                line_copy(w, 1, half, d).start()

    def plane_three(w, half):
        @pl.when(sec != w)
        def _():
            if w == 2 and half == 1:
                bulk_copy(0).wait_recv()
            else:
                for d in range(1, SIDE):
                    line_copy(w, 1, half, d).wait_recv()
            join_copy(w, half, core).start()

    def plane_settle(w):
        @pl.when(sec != w)
        def _():
            for half in range(2):
                join_copy(w, half, 1 - core).wait_recv()

    def plane_drain(w):
        @pl.when(sec != w)
        def _():
            for half in range(2):
                for d in range(1, SIDE):
                    if w == 1 or half == 0:
                        line_copy(w, 0, half, d).wait_send()
                        line_copy(w, 1, half, d).wait_send()
                join_copy(w, half, core).wait_send()

        @pl.when(sec == w)
        def _():
            for d in range(1, LAYERS):
                deal_copy(w, d).wait_send()
                if w == 2:
                    bulk_copy(d).wait_send()

    def rows_of(k):
        return pl.ds(pl.multiple_of(k * piece, 16), piece)

    def half_rows(who):
        return pl.ds(pl.multiple_of(who * (n_chip * piece), 16), n_chip * piece)

    own_block = rows_of(core * n_chip + chip)

    def split_block(a0, a1):
        top = jnp.concatenate([a0 * low, a1 * low], axis=1)
        bottom = jnp.concatenate([a0 * high, a1 * high], axis=1)
        return jnp.concatenate([top, bottom], axis=0)

    def pair_scores(left, right, factor):
        for p in range(PAIRS):
            la, ra = left(p), right(p)
            out = dot(split_block(*la), jnp.concatenate(ra, axis=1), 1, 1)
            if factor is not None:
                out = factor * out
            part[pl.ds(2 * SEQ * p, 2 * SEQ), :] = out.astype(BF)

    def level_copy():
        return pltpu.make_async_remote_copy(
            src_ref=part.at[half_rows(1 - core)],
            dst_ref=other,
            send_sem=level_sem.at[0],
            recv_sem=level_sem.at[1],
            device_id=(sec, partner),
            device_id_type=MESH,
        )

    def chip_at(step, sign):
        z, y = ((sign * n) % SIDE for n in step)
        return lax.rem(zc + z, SIDE) * SIDE + lax.rem(yc + y, SIDE)

    def rs_copy(d):
        to = chip_at(NEAR[d - 1], 1)
        return pltpu.make_async_remote_copy(
            src_ref=both.at[rows_of(to)],
            dst_ref=recv.at[d],
            send_sem=rs_send.at[d],
            recv_sem=rs_recv.at[d],
            device_id=(sec, 2 * to + core),
            device_id_type=MESH,
        )

    def start_reduce():
        level_copy().start()
        mine = part[half_rows(core), :].astype(F32)
        level_copy().wait_recv()
        both[...] = (mine + other[...].astype(F32)).astype(BF)
        for d in reversed(range(1, n_chip)):
            rs_copy(d).start()

    def finish_reduce():
        total = both[rows_of(chip), :].astype(F32)
        for d in range(1, n_chip):
            rs_copy(d).wait_recv()
            total = total + recv[d].astype(F32)
        return total

    def ag_copy(buf, d):
        to = chip_at(NEAR[d - 1], 1)
        return pltpu.make_async_remote_copy(
            src_ref=buf.at[own_block],
            dst_ref=buf.at[own_block],
            send_sem=ag_send.at[d],
            recv_sem=ag_recv.at[d],
            device_id=(sec, 2 * to + core),
            device_id_type=MESH,
        )

    def hand_copy(buf, d):
        source = chip_at(NEAR[d - 1], -1) if d else chip
        block = rows_of(core * n_chip + source)
        return pltpu.make_async_remote_copy(
            src_ref=buf.at[block],
            dst_ref=buf.at[block],
            send_sem=hand_send.at[d],
            recv_sem=hand_recv.at[d],
            device_id=(sec, partner),
            device_id_type=MESH,
        )

    def start_gather(buf):
        for d in reversed(range(1, n_chip)):
            ag_copy(buf, d).start()
        hand_copy(buf, 0).start()

    def finish_gather(buf):
        for d in range(1, n_chip):
            ag_copy(buf, d).wait_recv()
            hand_copy(buf, d).start()
        for d in range(n_chip):
            hand_copy(buf, d).wait_recv()

    def clear_exchange(buf):
        for d in range(n_chip):
            hand_copy(buf, d).wait_send()
        for d in range(1, n_chip):
            rs_copy(d).wait_send()
            ag_copy(buf, d).wait_send()
        level_copy().wait_send()

    def halves(ref, base, p):
        cols = pl.ds(base + SEQ * p, SEQ)
        return ref[pl.ds(0, SEQ), cols], ref[pl.ds(SEQ, SEQ), cols]

    def beside(buf, p):
        return jnp.concatenate(
            [buf[pl.ds(2 * SEQ * p, SEQ), :], buf[pl.ds(2 * SEQ * p + SEQ, SEQ), :]], axis=1
        )

    def put_halves(ref, base, p, value):
        cols = pl.ds(base + SEQ * p, SEQ)
        ref[pl.ds(0, SEQ), cols] = value[:, :SEQ]
        ref[pl.ds(SEQ, SEQ), cols] = value[:, SEQ:]

    own_rows = WIDTH // n_row

    def put_grad(u, value):
        for r in range(n_row):
            q = r // 2
            grad[u, r % 2, q // SIDE, q % SIDE] = value[own_rows * r : own_rows * (r + 1)].astype(BF)

    def pair_copy(u, par):
        return pltpu.make_async_remote_copy(
            src_ref=grad.at[u, 1 - core],
            dst_ref=pairbuf.at[par, u],
            send_sem=pair_send.at[u],
            recv_sem=pair_recv.at[par, u],
            device_id=(sec, partner),
            device_id_type=MESH,
        )

    def y_first(u):
        return u % 2 == 0

    def c1_copy(u, par, d):
        if y_first(u):
            y = lax.rem(yc + d, SIDE)
            src, peer = grad.at[u, core, :, y], row_at(zc, y)
        else:
            z = lax.rem(zc + d, SIDE)
            src, peer = grad.at[u, core, z], row_at(z, yc)
        return pltpu.make_async_remote_copy(
            src_ref=src,
            dst_ref=line1.at[par, u, d - 1],
            send_sem=c1_send.at[u, d - 1],
            recv_sem=c1_recv.at[par, u, d - 1],
            device_id=(sec, peer),
            device_id_type=MESH,
        )

    def c2_copy(u, par, d):
        if y_first(u):
            at = lax.rem(zc + d, SIDE)
            peer = row_at(at, yc)
        else:
            at = lax.rem(yc + d, SIDE)
            peer = row_at(zc, at)
        return pltpu.make_async_remote_copy(
            src_ref=sum1.at[par, u, at],
            dst_ref=line2.at[par, u, d - 1],
            send_sem=c2_send.at[u, d - 1],
            recv_sem=c2_recv.at[par, u, d - 1],
            device_id=(sec, peer),
            device_id_type=MESH,
        )

    def x_copy(u, t):
        owner = LAYERS - 1 - t
        return pltpu.make_async_remote_copy(
            src_ref=xout.at[u],
            dst_ref=xin.at[u, lax.rem(sec - owner + LAYERS - 1 + LAYERS, LAYERS)],
            send_sem=x_send.at[u],
            recv_sem=x_recv.at[u, lax.rem(sec - owner + LAYERS - 1 + LAYERS, LAYERS)],
            device_id=(owner, me),
            device_id_type=MESH,
        )

    def stage_pair(u, t):
        pair_copy(u, t % 2).start()

    def stage_one(u, t):
        par = t % 2
        pair_copy(u, par).wait_recv()
        pair_copy(u, par).wait_send()
        for z in range(SIDE):
            total = grad[u, core, z].astype(F32) + pairbuf[par, u, z].astype(F32)
            grad[u, core, z] = total.astype(BF)
        for d in range(1, SIDE):
            c1_copy(u, par, d).start()

    def stage_two(u, t):
        par = t % 2
        for d in range(1, SIDE):
            c1_copy(u, par, d).wait_recv()
            c1_copy(u, par, d).wait_send()
        for k in range(SIDE):
            own = grad[u, core, k, yc] if y_first(u) else grad[u, core, zc, k]
            total = own.astype(F32)
            for d in range(SIDE - 1):
                total = total + line1[par, u, d, k].astype(F32)
            sum1[par, u, k] = total.astype(BF)
        for d in range(1, SIDE):
            c2_copy(u, par, d).start()

    def stage_three(u, t):
        par = t % 2
        owner = LAYERS - 1 - t
        for d in range(1, SIDE):
            c2_copy(u, par, d).wait_recv()
            c2_copy(u, par, d).wait_send()
        total = sum1[par, u, zc if y_first(u) else yc].astype(F32)
        for d in range(SIDE - 1):
            total = total + line2[par, u, d].astype(F32)

        @pl.when((t > 0) & (sec != owner + 1))
        def _():
            x_copy(u, t - 1).wait_send()

        @pl.when(sec == owner)
        def _():
            fin[u] = total

        @pl.when(sec != owner)
        def _():
            xout[u] = total.astype(BF)
            x_copy(u, t).start()

    for w in (1, 2):

        @pl.when(sec == w)
        def _():
            for d in range(1, LAYERS):
                deal_copy(w, d).start()
            if w == 2:
                for d in (1, 3, 2):
                    bulk_copy(d).start()

    @pl.when(sec == 0)
    def _():
        for t in (1, 3, 2):
            first_copy(t).start()

    launch_flow()

    def forward(l, carry):
        here = qkv.at[l]

        @pl.when(l == 0)
        def _():
            tab_take(0)
            for d in range(1, LAYERS):
                gain_copy(d).wait_recv()
            for n in range(2):
                tab_pick(here, n)

        @pl.when(l > 0)
        def _():
            for w in (1, 2):
                pl.when(l == w)(functools.partial(plane_settle, w))

            @pl.when(l == RING)
            def _():
                settle()

            normal, _ = norm_parts(xs[l])
            h = (normal * gains[l]).astype(BF)
            for n in range(3):
                cols = pl.ds(WIDTH * n, WIDTH)
                here[:, cols] = dot(h, weight(l, WIDTH * n, WIDTH), 1, 0).astype(BF)

        pair_scores(lambda p: halves(here, 0, p), lambda p: halves(here, WIDTH, p), scale)
        start_reduce()

        @pl.when(l == 0)
        def _():
            tab_take(1)
            tab_pick(here, 2)
            plane_one(1)
            plane_two(1, 0)

        @pl.when(l == 1)
        def _():
            plane_two(2, 0)

        for turn in range(3):
            pl.when(l == turn)(functools.partial(pump, 2 * turn + 1))

        logits = finish_reduce()
        shifted = jnp.exp(logits - jnp.max(logits, axis=-1, keepdims=True))
        own = shifted / jnp.sum(shifted, axis=-1, keepdims=True)
        probs_l = probs.at[l]
        probs_l[own_block, :] = own.astype(BF)
        start_gather(probs_l)

        @pl.when(l == 0)
        def _():
            plane_two(1, 1)
            plane_one(2)

        for turn in range(2):
            pl.when(l == turn)(functools.partial(pump, 2 * turn + 2))

        finish_gather(probs_l)
        clear_exchange(probs_l)
        mixed_l = mixed.at[l]
        for p in range(PAIRS):
            out = dot(beside(probs_l, p), split_block(*halves(here, 2 * WIDTH, p)), 1, 0)
            put_halves(mixed_l, 0, p, out.astype(BF))

        @pl.when(l == 0)
        def _():
            @pl.when(sec > 0)
            def _():
                first_copy(0).wait_recv()
                first_twin(core).start()

            plane_three(1, 0)

            @pl.when(sec > 0)
            def _():
                first_twin(1 - core).wait_recv()

        @pl.when(l == 1)
        def _():
            plane_three(2, 0)

        @pl.when(l < LAYERS - 1)
        def _():
            xs[l + 1] = xs[l] + dot(mixed_l[...], weight(l, 3 * WIDTH, WIDTH), 1, 0)

        @pl.when(l == 0)
        def _():
            plane_three(1, 1)

        @pl.when(l == 1)
        def _():
            plane_three(2, 1)

        return carry

    lax.fori_loop(0, LAYERS, forward, 0)

    pltpu.make_async_copy(og_hbm.at[sec], ogb, og_sem).wait()
    dyf[...] = ogb[...].astype(F32)

    def reduce_window(step):
        def previous():
            t = step - 1
            for u, n in ((QRY, 0), (KEY, 1)):
                put_grad(u, dot(hbuf[...], dqkv[:, pl.ds(WIDTH * n, WIDTH)], 0, 0))
                stage_pair(u, t)
            for u in (OUT, VAL):
                stage_one(u, t)

        def older():
            t = step - 2
            for u in (OUT, VAL):
                stage_three(u, t)
            for u in (QRY, KEY):
                stage_two(u, t)

        return older, previous

    def gather_window(step):
        def previous():
            t = step - 1
            for u in (OUT, VAL):
                stage_two(u, t)
            for u in (QRY, KEY):
                stage_one(u, t)

        def older():
            t = step - 2
            for u in (QRY, KEY):
                stage_three(u, t)

        return previous, older

    def backward(step, carry):
        l = LAYERS - 1 - step
        here = qkv.at[l]
        probs_l = probs.at[l]
        dyb = dyf[...].astype(BF)
        dmix[...] = dot(dyb, weight(l, 3 * WIDTH, WIDTH), 1, 1).astype(BF)
        pair_scores(lambda p: halves(dmix, 0, p), lambda p: halves(here, 2 * WIDTH, p), None)
        start_reduce()

        older, previous = reduce_window(step)
        pl.when(step >= 2)(older)
        pl.when(step >= 1)(previous)
        for p in range(PAIRS):
            rows = pl.ds(2 * SEQ * p, 2 * SEQ)
            out = dot(probs_l[rows, :], split_block(*halves(dmix, 0, p)), 0, 0)
            put_halves(dqkv, 2 * WIDTH, p, out.astype(BF))
        dprobs = finish_reduce()
        own = probs_l[own_block, :].astype(F32)
        inner = jnp.sum(dprobs * own, axis=-1, keepdims=True)
        dlog[own_block, :] = (own * (dprobs - inner)).astype(BF)
        start_gather(dlog)

        normal, rstd = norm_parts(xs[l])
        hbuf[...] = (normal * gains[l]).astype(BF)
        vcols = pl.ds(2 * WIDTH, WIDTH)
        previous, older = gather_window(step)
        pl.when(step >= 1)(previous)
        put_grad(OUT, dot(mixed[l], dyb, 0, 0))
        put_grad(VAL, dot(hbuf[...], dqkv[:, vcols], 0, 0))
        for u in (OUT, VAL):
            stage_pair(u, step)

        @pl.when(l > 0)
        def _():
            dhacc[...] = dot(dqkv[:, vcols], weight(l, 2 * WIDTH, WIDTH), 1, 1)

        pl.when(step >= 2)(older)
        finish_gather(dlog)
        clear_exchange(dlog)

        for p in range(PAIRS):
            out = dot(beside(dlog, p), split_block(*halves(here, WIDTH, p)), 1, 0)
            put_halves(dqkv, 0, p, (scale * out).astype(BF))
            rows = pl.ds(2 * SEQ * p, 2 * SEQ)
            out = dot(dlog[rows, :], split_block(*halves(here, 0, p)), 0, 0)
            put_halves(dqkv, WIDTH, p, (scale * out).astype(BF))
        qk = pl.ds(0, 2 * WIDTH)

        @pl.when(l > 0)
        def _():
            dh = dhacc[...] + dot(dqkv[:, qk], weight(l, 0, 2 * WIDTH), 1, 1)
            dn = dh.astype(BF).astype(F32) * gains[l]
            first = jnp.mean(dn, axis=-1, keepdims=True)
            second = jnp.mean(dn * normal, axis=-1, keepdims=True)
            dyf[...] = dyf[...] + rstd * (dn - first - normal * second)

        return carry

    lax.fori_loop(0, LAYERS, backward, 0)

    for work in reduce_window(LAYERS) + gather_window(LAYERS):
        work()
    reduce_window(LAYERS + 1)[0]()
    gather_window(LAYERS + 1)[1]()

    for u in range(4):

        @pl.when(sec != 0)
        def _():
            x_copy(u, LAYERS - 1).wait_send()

        total = fin[u]
        for slot in range(LAYERS - 1):
            pltpu.make_async_remote_copy(
                src_ref=xout.at[u],
                dst_ref=xin.at[u, slot],
                send_sem=x_send.at[u],
                recv_sem=x_recv.at[u, slot],
                device_id=(lax.rem(sec + 1, LAYERS), me),
                device_id_type=MESH,
            ).wait_recv()
            total = total + xin[u, slot].astype(F32)
        if u == OUT:
            go_ref[0] = total
        else:
            gq_ref[0, :, pl.ds(WIDTH * {VAL: 2, QRY: 0, KEY: 1}[u], WIDTH)] = total

    tall = wcat[sec, zc, yc // 2, pl.ds(pl.multiple_of(2 * own_rows * lax.rem(yc, 2), 16), 2 * own_rows), :]
    tall = tall[:, : 3 * WIDTH].astype(F32)
    w_own = jnp.where(core == 0, tall[:own_rows], tall[own_rows:])
    dotted = jnp.sum(w_own * gq_ref[0], axis=-1, keepdims=True)
    lanes = lax.broadcasted_iota(jnp.int32, (own_rows, WIDTH), 1)
    subs = lax.broadcasted_iota(jnp.int32, (own_rows, WIDTH), 0)
    gain_own = jnp.sum(
        jnp.where(lanes == subs + own_rows * me, gain_ref[...], 0.0), axis=-1, keepdims=True
    )
    spread = jnp.where(lanes == subs, dotted / gain_own, 0.0)
    gg_ref[...] = jnp.sum(spread, axis=0, keepdims=True)[:, :own_rows]

    drain()
    for w in (1, 2):
        plane_drain(w)

    @pl.when(sec == 0)
    def _():
        for t in range(1, LAYERS):
            for late in range(2):
                tab_copy(t, late).wait_send()
            first_copy(t).wait_send()

    @pl.when(sec > 0)
    def _():
        for late in range(2):
            tab_twin(core, late).wait_send()
        first_twin(core).wait_send()

    for d in range(1, LAYERS):
        gain_copy(d).wait_send()


def hand_over(qkv_in, out_in, gain_in, qkv_out, out_out, gain_out):
    qkv_out[...] = qkv_in[...]
    out_out[...] = out_in[...]
    gain_out[...] = gain_in[...]


def local(tokens, embed, ln_gain, w_qkv, w_out, out_grad):
    n_row = lax.axis_size("row")
    micro, rows_here, seq = tokens.shape
    vocab, width = embed.shape
    npos = rows_here * seq
    scale = HEAD_DIM ** (-0.5) / (rows_here * n_row) ** 0.5
    padded = vocab + -vocab % 16
    flat = HEADS * seq
    own_rows = width // n_row
    vm, anyspace = pl.BlockSpec(memory_space=pltpu.VMEM), pl.BlockSpec(memory_space=pl.ANY)
    dma = pltpu.SemaphoreType.DMA
    sums = pl.pallas_call(
        functools.partial(kernel, n_row, scale),
        out_shape=(
            jax.ShapeDtypeStruct((1, own_rows, 3 * width), F32),
            jax.ShapeDtypeStruct((1, own_rows, width), F32),
            jax.ShapeDtypeStruct((1, own_rows), F32),
        ),
        in_specs=[vm, vm, vm, anyspace, anyspace, anyspace],
        out_specs=(vm, vm, vm),
        scratch_shapes=[
            pltpu.VMEM((LAYERS, SIDE, 2, width // 8, 4 * width), BF),
            pltpu.VMEM((LAYERS, 1, width), F32),
            pltpu.VMEM((padded, width), BF),
            pltpu.VMEM((2, padded, 3 * width // 2), BF),
            pltpu.VMEM((LAYERS, npos, width), F32),
            pltpu.VMEM((LAYERS, npos, 3 * width), BF),
            pltpu.VMEM((LAYERS, flat, seq), BF),
            pltpu.VMEM((LAYERS, npos, width), BF),
            pltpu.VMEM((flat, seq), BF),
            pltpu.VMEM((flat // 2, seq), BF),
            pltpu.VMEM((flat // 2, seq), BF),
            pltpu.VMEM((n_row // 2, flat // n_row, seq), BF),
            pltpu.VMEM((flat, seq), BF),
            pltpu.VMEM((npos, width), F32),
            pltpu.VMEM((npos, width), BF),
            pltpu.VMEM((npos, width), BF),
            pltpu.VMEM((npos, 3 * width), BF),
            pltpu.VMEM((npos, width), BF),
            pltpu.VMEM((npos, width), F32),
            pltpu.VMEM((4, 2, SIDE, SIDE, own_rows, width), BF),
            pltpu.VMEM((2, 4, SIDE, SIDE, own_rows, width), BF),
            pltpu.VMEM((2, 4, SIDE - 1, SIDE, own_rows, width), BF),
            pltpu.VMEM((2, 4, SIDE, own_rows, width), BF),
            pltpu.VMEM((2, 4, SIDE - 1, own_rows, width), BF),
            pltpu.VMEM((4, own_rows, width), BF),
            pltpu.VMEM((4, LAYERS - 1, own_rows, width), BF),
            pltpu.VMEM((4, own_rows, width), F32),
            dma((2,)),
            dma((n_row // 2,)),
            dma((n_row // 2,)),
            dma((n_row // 2,)),
            dma((n_row // 2,)),
            dma((n_row // 2,)),
            dma((n_row // 2,)),
            dma((2,)),
            dma,
            dma((2, LAYERS)),
            dma((2, 2)),
            dma((LAYERS,)),
            dma((LAYERS,)),
            dma((2, LAYERS)),
            dma((2,)),
            dma((LAYERS,)),
            dma,
            dma((2, 2, SIDE - 1)),
            dma((2, 2, SIDE - 1)),
            dma((2, 2, SIDE - 1)),
            dma((2, 2, SIDE - 1)),
            dma((2, 2)),
            dma((2, 2)),
            dma((2, CHUNKS)),
            dma((2, CHUNKS)),
            dma((2, CHUNKS)),
            dma((2, CHUNKS)),
            dma((LAYERS,)),
            dma((2,)),
            dma((4,)),
            dma((2, 4)),
            dma((4, SIDE - 1)),
            dma((2, 4, SIDE - 1)),
            dma((4, SIDE - 1)),
            dma((2, 4, SIDE - 1)),
            dma((4,)),
            dma((4, LAYERS - 1)),
        ],
        compiler_params=pltpu.CompilerParams(
            collective_id=0, has_side_effects=True, vmem_limit_bytes=67043328
        ),
    )(
        tokens,
        embed,
        ln_gain,
        w_qkv.reshape(SIDE, 2, width // 8, 3 * width),
        w_out.reshape(SIDE, 2, width // 8, width),
        out_grad.reshape(micro, npos, width),
    )
    grad_qkv, grad_out, grad_gain = pl.pallas_call(
        hand_over,
        out_shape=tuple(jax.ShapeDtypeStruct(g.shape, F32) for g in sums),
        in_specs=[vm, vm, vm],
        out_specs=(vm, vm, vm),
    )(*sums)
    return (grad_qkv, grad_out, grad_gain)


def solution(mesh):
    in_specs = (
        P(None, "row", None),
        P(),
        P("section", None),
        P("section", None, None),
        P("section", None, None),
        P(None, "row", None, None),
    )
    out_specs = (P("section", "row", None), P("section", "row", None), P("section", "row"))
    return jax.shard_map(local, mesh=mesh, in_specs=in_specs, out_specs=out_specs, check_vma=False)
```

```python
import functools

import jax
import jax.numpy as jnp
from jax import lax
from jax.experimental import pallas as pl
from jax.experimental.pallas import tpu as pltpu
from jax.sharding import PartitionSpec as P

HEADS = 12
HEAD_DIM = 64
LAYERS = 4
PAIRS = HEADS // 2
WIDTH = HEADS * HEAD_DIM
SEQ = 128
SIDE = 4
OUT, VAL, QRY, KEY = 0, 1, 2, 3
CHUNKS = 3
NEAR = sorted(
    ((z, y) for z in range(SIDE) for y in range(SIDE) if z or y),
    key=lambda step: sum(min(n, SIDE - n) for n in step),
)
CHUNK = 4 * WIDTH // CHUNKS
HALF = WIDTH // 2
MESH = pl.DeviceIdType.MESH
BF = jnp.bfloat16
F32 = jnp.float32


def dot(a, b, ca, cb):
    return lax.dot_general(a, b, (((ca,), (cb,)), ((), ())), preferred_element_type=F32)


def norm_parts(x):
    centred = x - jnp.mean(x, axis=-1, keepdims=True)
    spread = jnp.mean(centred * centred, axis=-1, keepdims=True)
    rstd = lax.rsqrt(spread + 1e-05)
    return centred * rstd, rstd


def kernel(
    n_row,
    scale,
    tok_ref,
    emb_ref,
    gain_ref,
    wqkv_hbm,
    wout_hbm,
    og_hbm,
    gq_ref,
    go_ref,
    gg_ref,
    wcat,
    gains,
    embp,
    tab,
    xs,
    qkv,
    probs,
    mixed,
    part,
    other,
    both,
    recv,
    dlog,
    dyf,
    ogb,
    dmix,
    dqkv,
    hbuf,
    dhacc,
    grad,
    pairbuf,
    line1,
    sum1,
    line2,
    xout,
    xin,
    fin,
    level_sem,
    rs_send,
    rs_recv,
    ag_send,
    ag_recv,
    hand_send,
    hand_recv,
    w_sem,
    og_sem,
    tab_send,
    tab_recv,
    gain_send,
    gain_recv,
    deal_send,
    deal_recv,
    bulk_send,
    bulk_recv,
    s1_send,
    s1_recv,
    s2_send,
    s2_recv,
    join_send,
    join_recv,
    ring_send,
    ring_recv,
    twin_send,
    twin_recv,
    first_send,
    first_recv,
    pair_send,
    pair_recv,
    c1_send,
    c1_recv,
    c2_send,
    c2_recv,
    x_send,
    x_recv,
):
    sec = lax.axis_index("section")
    me = lax.axis_index("row")
    piece = part.shape[0] // n_row
    n_chip = n_row // 2
    core = lax.rem(me, 2)
    partner = me + 1 - 2 * core
    chip = me // 2
    zc = chip // SIDE
    yc = lax.rem(chip, SIDE)

    def row_at(z, y):
        return (z * SIDE + y) * 2 + core

    def weight(l, first, count):
        block = wcat[l, :, :, :, pl.ds(first, count)]
        return block.reshape(WIDTH, count)

    local_qkv = pltpu.make_async_copy(
        wqkv_hbm, wcat.at[sec, :, :, :, pl.ds(0, 3 * WIDTH)], w_sem.at[0]
    )
    local_out = pltpu.make_async_copy(
        wout_hbm, wcat.at[sec, :, :, :, pl.ds(3 * WIDTH, WIDTH)], w_sem.at[1]
    )
    local_qkv.start()
    local_out.start()
    pltpu.make_async_copy(og_hbm.at[sec], ogb, og_sem).start()

    barrier = pltpu.get_barrier_semaphore()

    def greet(d, carry):
        peer = 2 * lax.rem(chip + d, n_chip) + core
        pl.semaphore_signal(barrier, inc=1, device_id=(sec, peer), device_id_type=MESH)
        return carry

    lax.fori_loop(1, n_chip, greet, 0)
    pl.semaphore_signal(barrier, inc=1, device_id=(sec, partner), device_id_type=MESH)
    for d in range(1, LAYERS):
        pl.semaphore_signal(
            barrier, inc=1, device_id=(lax.rem(sec + d, LAYERS), me), device_id_type=MESH
        )

    lane = lax.broadcasted_iota(jnp.int32, (1, SEQ), 1)
    low = (lane < HEAD_DIM).astype(F32).astype(BF)
    high = (lane >= HEAD_DIM).astype(F32).astype(BF)

    gains[sec] = gain_ref[...]
    padded = embp.shape[0]
    embp[...] = jnp.zeros_like(embp)
    embp[pl.ds(0, emb_ref.shape[0]), :] = emb_ref[...]
    ids = lax.broadcasted_iota(jnp.int32, (padded, SEQ), 0)
    tok = tok_ref[sec]
    picks = jnp.concatenate([(tok[r : r + 1] == ids) for r in range(2)], axis=1)
    picks = picks.astype(F32).astype(BF)
    xs[0] = dot(picks, embp[...], 0, 0)

    local_qkv.wait()

    @pl.when(sec == 0)
    def _():
        normal, _ = norm_parts(embp[...].astype(F32))
        h = (normal * gain_ref[...]).astype(BF)
        for n in range(3):
            made = dot(h, weight(0, WIDTH * n, WIDTH), 1, 0).astype(BF)
            for half in range(2):
                cols = pl.ds(HALF * n, HALF)
                tab[half, :, cols] = made[:, HALF * half : HALF * (half + 1)]

    local_out.wait()
    pl.semaphore_wait(barrier, n_chip + LAYERS - 1)

    def tab_part(who, late):
        return tab.at[who, :, pl.ds(2 * HALF, HALF) if late else pl.ds(0, 2 * HALF)]

    def tab_copy(t, late):
        return pltpu.make_async_remote_copy(
            src_ref=tab_part(core, late),
            dst_ref=tab_part(core, late),
            send_sem=tab_send.at[late, t],
            recv_sem=tab_recv.at[late, 0],
            device_id=(t, me),
            device_id_type=MESH,
        )

    def tab_twin(who, late):
        return pltpu.make_async_remote_copy(
            src_ref=tab_part(who, late),
            dst_ref=tab_part(who, late),
            send_sem=tab_send.at[late, 0],
            recv_sem=tab_recv.at[late, 1],
            device_id=(sec, partner),
            device_id_type=MESH,
        )

    def tab_take(late):
        @pl.when(sec > 0)
        def _():
            tab_copy(0, late).wait_recv()
            tab_twin(core, late).start()
            tab_twin(1 - core, late).wait_recv()

    def tab_pick(here, n):
        for half in range(2):
            made = dot(picks, tab[half, :, pl.ds(HALF * n, HALF)], 0, 0)
            here[:, pl.ds(WIDTH * n + HALF * half, HALF)] = made.astype(BF)

    @pl.when(sec == 0)
    def _():
        for late in range(2):
            for t in range(1, LAYERS):
                tab_copy(t, late).start()

    def gain_copy(d):
        return pltpu.make_async_remote_copy(
            src_ref=gain_ref,
            dst_ref=gains.at[sec],
            send_sem=gain_send.at[d],
            recv_sem=gain_recv.at[d],
            device_id=(lax.rem(sec + d, LAYERS), me),
            device_id_type=MESH,
        )

    for d in range(1, LAYERS):
        gain_copy(d).start()

    RING = LAYERS - 1

    def flow(d, k, who):
        cols = pl.ds(pl.multiple_of(k * CHUNK, 128), CHUNK)
        return wcat.at[RING, who * 2 + d, :, :, cols]

    def place(d):
        return lax.rem(sec - RING + LAYERS, LAYERS) if d == 0 else lax.rem(RING - sec, LAYERS)

    def ring_copy(d, k):
        step = 1 if d == 0 else LAYERS - 1
        ref = flow(d, k, core)
        return pltpu.make_async_remote_copy(
            src_ref=ref,
            dst_ref=ref,
            send_sem=ring_send.at[d, k],
            recv_sem=ring_recv.at[d, k],
            device_id=(lax.rem(sec + step, LAYERS), me),
            device_id_type=MESH,
        )

    def twin_copy(d, k, who):
        ref = flow(d, k, who)
        return pltpu.make_async_remote_copy(
            src_ref=ref,
            dst_ref=ref,
            send_sem=twin_send.at[d, k],
            recv_sem=twin_recv.at[d, k],
            device_id=(sec, partner),
            device_id_type=MESH,
        )

    def launch_flow():
        @pl.when(sec == RING)
        def _():
            for k in range(CHUNKS):
                for d in range(2):
                    ring_copy(d, k).start()

    def pump(slot):
        for d in range(2):
            at = place(d)
            k = slot - at

            @pl.when((at > 0) & (k >= 0) & (k < CHUNKS))
            def _():
                ring_copy(d, k).wait_recv()

                @pl.when(at < LAYERS - 1)
                def _():
                    ring_copy(d, k).start()

                twin_copy(d, k, core).start()

    def settle():
        @pl.when(sec != RING)
        def _():
            for k in range(CHUNKS):
                for d in range(2):
                    twin_copy(d, k, 1 - core).wait_recv()

    def drain():
        def one(k, carry):
            for d in range(2):
                at = place(d)

                @pl.when(at < LAYERS - 1)
                def _():
                    ring_copy(d, k).wait_send()

                @pl.when(at > 0)
                def _():
                    twin_copy(d, k, core).wait_send()

            return carry

        lax.fori_loop(0, CHUNKS, one, 0)

    def first_ref(who):
        return wcat.at[0, pl.ds(2 * who, 2), :, :, pl.ds(3 * WIDTH, WIDTH)]

    def first_copy(t):
        return pltpu.make_async_remote_copy(
            src_ref=first_ref(core),
            dst_ref=first_ref(core),
            send_sem=first_send.at[t],
            recv_sem=first_recv.at[0],
            device_id=(t, me),
            device_id_type=MESH,
        )

    def first_twin(who):
        return pltpu.make_async_remote_copy(
            src_ref=first_ref(who),
            dst_ref=first_ref(who),
            send_sem=first_send.at[0],
            recv_sem=first_recv.at[1],
            device_id=(sec, partner),
            device_id_type=MESH,
        )

    block_cols = pl.ds(pl.multiple_of((core * SIDE + yc) * HALF, 128), HALF)

    def side_cols(who):
        return pl.ds(pl.multiple_of(who * (2 * WIDTH), 128), 2 * WIDTH)

    def deal_copy(w, d):
        halves_sent = 2 if w == 1 else 1
        ref = wcat.at[w, zc, pl.ds(0, halves_sent), :, block_cols]
        return pltpu.make_async_remote_copy(
            src_ref=ref,
            dst_ref=ref,
            send_sem=deal_send.at[w - 1, d],
            recv_sem=deal_recv.at[w - 1],
            device_id=((w + d) % LAYERS, me),
            device_id_type=MESH,
        )

    def bulk_copy(d):
        ref = wcat.at[2, :, 1, :, side_cols(core)]
        return pltpu.make_async_remote_copy(
            src_ref=ref,
            dst_ref=ref,
            send_sem=bulk_send.at[d],
            recv_sem=bulk_recv,
            device_id=((2 + d) % LAYERS, me),
            device_id_type=MESH,
        )

    def line_copy(w, stage, half, d):
        along_y = (stage + half) % 2 == 0
        y = lax.rem(yc + d, SIDE) if along_y else yc
        z = zc if along_y else lax.rem(zc + d, SIDE)
        if stage == 0:
            ref = wcat.at[w, zc, half, :, block_cols]
        elif along_y:
            ref = wcat.at[w, :, half, :, block_cols]
        else:
            ref = wcat.at[w, zc, half, :, side_cols(core)]
        send, take = (s1_send, s1_recv) if stage == 0 else (s2_send, s2_recv)
        return pltpu.make_async_remote_copy(
            src_ref=ref,
            dst_ref=ref,
            send_sem=send.at[w - 1, half, d - 1],
            recv_sem=take.at[w - 1, half, d - 1],
            device_id=(sec, row_at(z, y)),
            device_id_type=MESH,
        )

    def join_copy(w, half, who):
        ref = wcat.at[w, :, half, :, side_cols(who)]
        return pltpu.make_async_remote_copy(
            src_ref=ref,
            dst_ref=ref,
            send_sem=join_send.at[w - 1, half],
            recv_sem=join_recv.at[w - 1, half],
            device_id=(sec, partner),
            device_id_type=MESH,
        )

    def plane_one(w):
        @pl.when(sec != w)
        def _():
            deal_copy(w, 0).wait_recv()
            for half in range(2 if w == 1 else 1):
                for d in range(1, SIDE):
                    line_copy(w, 0, half, d).start()

    def plane_two(w, half):
        @pl.when(sec != w)
        def _():
            for d in range(1, SIDE):
                line_copy(w, 0, half, d).wait_recv()
            for d in range(1, SIDE):
                line_copy(w, 1, half, d).start()

    def plane_three(w, half):
        @pl.when(sec != w)
        def _():
            if w == 2 and half == 1:
                bulk_copy(0).wait_recv()
            else:
                for d in range(1, SIDE):
                    line_copy(w, 1, half, d).wait_recv()
            join_copy(w, half, core).start()

    def plane_settle(w):
        @pl.when(sec != w)
        def _():
            for half in range(2):
                join_copy(w, half, 1 - core).wait_recv()

    def plane_drain(w):
        @pl.when(sec != w)
        def _():
            for half in range(2):
                for d in range(1, SIDE):
                    if w == 1 or half == 0:
                        line_copy(w, 0, half, d).wait_send()
                        line_copy(w, 1, half, d).wait_send()
                join_copy(w, half, core).wait_send()

        @pl.when(sec == w)
        def _():
            for d in range(1, LAYERS):
                deal_copy(w, d).wait_send()
                if w == 2:
                    bulk_copy(d).wait_send()

    def rows_of(k):
        return pl.ds(pl.multiple_of(k * piece, 16), piece)

    def half_rows(who):
        return pl.ds(pl.multiple_of(who * (n_chip * piece), 16), n_chip * piece)

    own_block = rows_of(core * n_chip + chip)

    def split_block(a0, a1):
        top = jnp.concatenate([a0 * low, a1 * low], axis=1)
        bottom = jnp.concatenate([a0 * high, a1 * high], axis=1)
        return jnp.concatenate([top, bottom], axis=0)

    def pair_scores(left, right, factor):
        for p in range(PAIRS):
            la, ra = left(p), right(p)
            out = dot(split_block(*la), jnp.concatenate(ra, axis=1), 1, 1)
            if factor is not None:
                out = factor * out
            part[pl.ds(2 * SEQ * p, 2 * SEQ), :] = out.astype(BF)

    def level_copy():
        return pltpu.make_async_remote_copy(
            src_ref=part.at[half_rows(1 - core)],
            dst_ref=other,
            send_sem=level_sem.at[0],
            recv_sem=level_sem.at[1],
            device_id=(sec, partner),
            device_id_type=MESH,
        )

    def chip_at(step, sign):
        z, y = ((sign * n) % SIDE for n in step)
        return lax.rem(zc + z, SIDE) * SIDE + lax.rem(yc + y, SIDE)

    def rs_copy(d):
        to = chip_at(NEAR[d - 1], 1)
        return pltpu.make_async_remote_copy(
            src_ref=both.at[rows_of(to)],
            dst_ref=recv.at[d],
            send_sem=rs_send.at[d],
            recv_sem=rs_recv.at[d],
            device_id=(sec, 2 * to + core),
            device_id_type=MESH,
        )

    def start_reduce():
        level_copy().start()
        mine = part[half_rows(core), :].astype(F32)
        level_copy().wait_recv()
        both[...] = (mine + other[...].astype(F32)).astype(BF)
        for d in reversed(range(1, n_chip)):
            rs_copy(d).start()

    def finish_reduce():
        total = both[rows_of(chip), :].astype(F32)
        for d in range(1, n_chip):
            rs_copy(d).wait_recv()
            total = total + recv[d].astype(F32)
        return total

    def ag_copy(buf, d):
        to = chip_at(NEAR[d - 1], 1)
        return pltpu.make_async_remote_copy(
            src_ref=buf.at[own_block],
            dst_ref=buf.at[own_block],
            send_sem=ag_send.at[d],
            recv_sem=ag_recv.at[d],
            device_id=(sec, 2 * to + core),
            device_id_type=MESH,
        )

    def hand_copy(buf, d):
        source = chip_at(NEAR[d - 1], -1) if d else chip
        block = rows_of(core * n_chip + source)
        return pltpu.make_async_remote_copy(
            src_ref=buf.at[block],
            dst_ref=buf.at[block],
            send_sem=hand_send.at[d],
            recv_sem=hand_recv.at[d],
            device_id=(sec, partner),
            device_id_type=MESH,
        )

    def start_gather(buf):
        for d in reversed(range(1, n_chip)):
            ag_copy(buf, d).start()
        hand_copy(buf, 0).start()
        for d in range(1, n_chip):
            rs_copy(d).wait_send()
        level_copy().wait_send()

    def finish_gather(buf):
        for d in range(1, n_chip):
            ag_copy(buf, d).wait_recv()
            hand_copy(buf, d).start()
        for d in range(n_chip):
            hand_copy(buf, d).wait_recv()

    def clear_exchange(buf):
        for d in range(n_chip):
            hand_copy(buf, d).wait_send()
        for d in range(1, n_chip):
            ag_copy(buf, d).wait_send()

    def halves(ref, base, p):
        cols = pl.ds(base + SEQ * p, SEQ)
        return ref[pl.ds(0, SEQ), cols], ref[pl.ds(SEQ, SEQ), cols]

    def beside(buf, p):
        return jnp.concatenate(
            [buf[pl.ds(2 * SEQ * p, SEQ), :], buf[pl.ds(2 * SEQ * p + SEQ, SEQ), :]], axis=1
        )

    def put_halves(ref, base, p, value):
        cols = pl.ds(base + SEQ * p, SEQ)
        ref[pl.ds(0, SEQ), cols] = value[:, :SEQ]
        ref[pl.ds(SEQ, SEQ), cols] = value[:, SEQ:]

    own_rows = WIDTH // n_row

    def put_grad(u, value):
        for r in range(n_row):
            q = r // 2
            grad[u, r % 2, q // SIDE, q % SIDE] = value[own_rows * r : own_rows * (r + 1)].astype(BF)

    def pair_copy(u, par):
        return pltpu.make_async_remote_copy(
            src_ref=grad.at[u, 1 - core],
            dst_ref=pairbuf.at[par, u],
            send_sem=pair_send.at[u],
            recv_sem=pair_recv.at[par, u],
            device_id=(sec, partner),
            device_id_type=MESH,
        )

    def y_first(u):
        return u % 2 == 0

    def c1_copy(u, par, d):
        if y_first(u):
            y = lax.rem(yc + d, SIDE)
            src, peer = grad.at[u, core, :, y], row_at(zc, y)
        else:
            z = lax.rem(zc + d, SIDE)
            src, peer = grad.at[u, core, z], row_at(z, yc)
        return pltpu.make_async_remote_copy(
            src_ref=src,
            dst_ref=line1.at[par, u, d - 1],
            send_sem=c1_send.at[u, d - 1],
            recv_sem=c1_recv.at[par, u, d - 1],
            device_id=(sec, peer),
            device_id_type=MESH,
        )

    def c2_copy(u, par, d):
        if y_first(u):
            at = lax.rem(zc + d, SIDE)
            peer = row_at(at, yc)
        else:
            at = lax.rem(yc + d, SIDE)
            peer = row_at(zc, at)
        return pltpu.make_async_remote_copy(
            src_ref=sum1.at[par, u, at],
            dst_ref=line2.at[par, u, d - 1],
            send_sem=c2_send.at[u, d - 1],
            recv_sem=c2_recv.at[par, u, d - 1],
            device_id=(sec, peer),
            device_id_type=MESH,
        )

    def x_copy(u, t):
        owner = LAYERS - 1 - t
        return pltpu.make_async_remote_copy(
            src_ref=xout.at[u],
            dst_ref=xin.at[u, lax.rem(sec - owner + LAYERS - 1 + LAYERS, LAYERS)],
            send_sem=x_send.at[u],
            recv_sem=x_recv.at[u, lax.rem(sec - owner + LAYERS - 1 + LAYERS, LAYERS)],
            device_id=(owner, me),
            device_id_type=MESH,
        )

    def stage_pair(u, t):
        pair_copy(u, t % 2).start()

    def stage_one(u, t):
        par = t % 2
        pair_copy(u, par).wait_recv()
        pair_copy(u, par).wait_send()
        for z in range(SIDE):
            total = grad[u, core, z].astype(F32) + pairbuf[par, u, z].astype(F32)
            grad[u, core, z] = total.astype(BF)
        for d in range(1, SIDE):
            c1_copy(u, par, d).start()

    def stage_two(u, t):
        par = t % 2
        for d in range(1, SIDE):
            c1_copy(u, par, d).wait_recv()
            c1_copy(u, par, d).wait_send()
        for k in range(SIDE):
            own = grad[u, core, k, yc] if y_first(u) else grad[u, core, zc, k]
            total = own.astype(F32)
            for d in range(SIDE - 1):
                total = total + line1[par, u, d, k].astype(F32)
            sum1[par, u, k] = total.astype(BF)
        for d in range(1, SIDE):
            c2_copy(u, par, d).start()

    def stage_three(u, t):
        par = t % 2
        owner = LAYERS - 1 - t
        for d in range(1, SIDE):
            c2_copy(u, par, d).wait_recv()
            c2_copy(u, par, d).wait_send()
        total = sum1[par, u, zc if y_first(u) else yc].astype(F32)
        for d in range(SIDE - 1):
            total = total + line2[par, u, d].astype(F32)

        @pl.when((t > 0) & (sec != owner + 1))
        def _():
            x_copy(u, t - 1).wait_send()

        @pl.when(sec == owner)
        def _():
            fin[u] = total

        @pl.when(sec != owner)
        def _():
            xout[u] = total.astype(BF)
            x_copy(u, t).start()

    for w in (1, 2):

        @pl.when(sec == w)
        def _():
            for d in range(1, LAYERS):
                deal_copy(w, d).start()
            if w == 2:
                for d in (1, 3, 2):
                    bulk_copy(d).start()

    @pl.when(sec == 0)
    def _():
        for t in (1, 3, 2):
            first_copy(t).start()

    launch_flow()

    def forward(l, carry):
        here = qkv.at[l]

        @pl.when(l == 0)
        def _():
            tab_take(0)
            for d in range(1, LAYERS):
                gain_copy(d).wait_recv()
            for n in range(2):
                tab_pick(here, n)

        @pl.when(l > 0)
        def _():
            for w in (1, 2):
                pl.when(l == w)(functools.partial(plane_settle, w))

            @pl.when(l == RING)
            def _():
                settle()

            normal, _ = norm_parts(xs[l])
            h = (normal * gains[l]).astype(BF)
            for n in range(3):
                cols = pl.ds(WIDTH * n, WIDTH)
                here[:, cols] = dot(h, weight(l, WIDTH * n, WIDTH), 1, 0).astype(BF)

        pair_scores(lambda p: halves(here, 0, p), lambda p: halves(here, WIDTH, p), scale)
        start_reduce()

        @pl.when(l == 0)
        def _():
            tab_take(1)
            tab_pick(here, 2)
            plane_one(1)
            plane_two(1, 0)

        @pl.when(l == 1)
        def _():
            plane_two(2, 0)

        for turn in range(3):
            pl.when(l == turn)(functools.partial(pump, 2 * turn + 1))

        logits = finish_reduce()
        shifted = jnp.exp(logits - jnp.max(logits, axis=-1, keepdims=True))
        own = shifted / jnp.sum(shifted, axis=-1, keepdims=True)
        probs_l = probs.at[l]
        probs_l[own_block, :] = own.astype(BF)
        start_gather(probs_l)

        @pl.when(l == 0)
        def _():
            plane_two(1, 1)
            plane_one(2)

        for turn in range(2):
            pl.when(l == turn)(functools.partial(pump, 2 * turn + 2))

        finish_gather(probs_l)
        clear_exchange(probs_l)
        mixed_l = mixed.at[l]
        for p in range(PAIRS):
            out = dot(beside(probs_l, p), split_block(*halves(here, 2 * WIDTH, p)), 1, 0)
            put_halves(mixed_l, 0, p, out.astype(BF))

        @pl.when(l == 0)
        def _():
            @pl.when(sec > 0)
            def _():
                first_copy(0).wait_recv()
                first_twin(core).start()

            plane_three(1, 0)

            @pl.when(sec > 0)
            def _():
                first_twin(1 - core).wait_recv()

        @pl.when(l == 1)
        def _():
            plane_three(2, 0)

        @pl.when(l < LAYERS - 1)
        def _():
            xs[l + 1] = xs[l] + dot(mixed_l[...], weight(l, 3 * WIDTH, WIDTH), 1, 0)

        @pl.when(l == 0)
        def _():
            plane_three(1, 1)

        @pl.when(l == 1)
        def _():
            plane_three(2, 1)

        return carry

    lax.fori_loop(0, LAYERS, forward, 0)

    pltpu.make_async_copy(og_hbm.at[sec], ogb, og_sem).wait()
    dyf[...] = ogb[...].astype(F32)

    def reduce_window(step):
        def previous():
            t = step - 1
            for u, n in ((QRY, 0), (KEY, 1)):
                put_grad(u, dot(hbuf[...], dqkv[:, pl.ds(WIDTH * n, WIDTH)], 0, 0))
                stage_pair(u, t)
            for u in (OUT, VAL):
                stage_one(u, t)

        def older():
            t = step - 2
            for u in (OUT, VAL):
                stage_three(u, t)
            for u in (QRY, KEY):
                stage_two(u, t)

        return older, previous

    def gather_window(step):
        def previous():
            t = step - 1
            for u in (OUT, VAL):
                stage_two(u, t)
            for u in (QRY, KEY):
                stage_one(u, t)

        def older():
            t = step - 2
            for u in (QRY, KEY):
                stage_three(u, t)

        return previous, older

    def backward(step, carry):
        l = LAYERS - 1 - step
        here = qkv.at[l]
        probs_l = probs.at[l]
        dyb = dyf[...].astype(BF)
        dmix[...] = dot(dyb, weight(l, 3 * WIDTH, WIDTH), 1, 1).astype(BF)
        pair_scores(lambda p: halves(dmix, 0, p), lambda p: halves(here, 2 * WIDTH, p), None)
        start_reduce()

        older, previous = reduce_window(step)
        pl.when(step >= 2)(older)
        pl.when(step >= 1)(previous)
        for p in range(PAIRS):
            rows = pl.ds(2 * SEQ * p, 2 * SEQ)
            out = dot(probs_l[rows, :], split_block(*halves(dmix, 0, p)), 0, 0)
            put_halves(dqkv, 2 * WIDTH, p, out.astype(BF))
        dprobs = finish_reduce()
        own = probs_l[own_block, :].astype(F32)
        inner = jnp.sum(dprobs * own, axis=-1, keepdims=True)
        dlog[own_block, :] = (own * (dprobs - inner)).astype(BF)
        start_gather(dlog)

        normal, rstd = norm_parts(xs[l])
        hbuf[...] = (normal * gains[l]).astype(BF)
        vcols = pl.ds(2 * WIDTH, WIDTH)
        previous, older = gather_window(step)
        pl.when(step >= 1)(previous)
        put_grad(OUT, dot(mixed[l], dyb, 0, 0))
        put_grad(VAL, dot(hbuf[...], dqkv[:, vcols], 0, 0))
        for u in (OUT, VAL):
            stage_pair(u, step)

        @pl.when(l > 0)
        def _():
            dhacc[...] = dot(dqkv[:, vcols], weight(l, 2 * WIDTH, WIDTH), 1, 1)

        pl.when(step >= 2)(older)
        finish_gather(dlog)
        clear_exchange(dlog)

        for p in range(PAIRS):
            out = dot(beside(dlog, p), split_block(*halves(here, WIDTH, p)), 1, 0)
            put_halves(dqkv, 0, p, (scale * out).astype(BF))
            rows = pl.ds(2 * SEQ * p, 2 * SEQ)
            out = dot(dlog[rows, :], split_block(*halves(here, 0, p)), 0, 0)
            put_halves(dqkv, WIDTH, p, (scale * out).astype(BF))
        qk = pl.ds(0, 2 * WIDTH)

        @pl.when(l > 0)
        def _():
            dh = dhacc[...] + dot(dqkv[:, qk], weight(l, 0, 2 * WIDTH), 1, 1)
            dn = dh.astype(BF).astype(F32) * gains[l]
            first = jnp.mean(dn, axis=-1, keepdims=True)
            second = jnp.mean(dn * normal, axis=-1, keepdims=True)
            dyf[...] = dyf[...] + rstd * (dn - first - normal * second)

        return carry

    lax.fori_loop(0, LAYERS, backward, 0)

    for work in reduce_window(LAYERS) + gather_window(LAYERS):
        work()
    reduce_window(LAYERS + 1)[0]()
    gather_window(LAYERS + 1)[1]()

    for u in range(4):

        @pl.when(sec != 0)
        def _():
            x_copy(u, LAYERS - 1).wait_send()

        total = fin[u]
        for slot in range(LAYERS - 1):
            pltpu.make_async_remote_copy(
                src_ref=xout.at[u],
                dst_ref=xin.at[u, slot],
                send_sem=x_send.at[u],
                recv_sem=x_recv.at[u, slot],
                device_id=(lax.rem(sec + 1, LAYERS), me),
                device_id_type=MESH,
            ).wait_recv()
            total = total + xin[u, slot].astype(F32)
        if u == OUT:
            go_ref[0] = total
        else:
            gq_ref[0, :, pl.ds(WIDTH * {VAL: 2, QRY: 0, KEY: 1}[u], WIDTH)] = total

    tall = wcat[sec, zc, yc // 2, pl.ds(pl.multiple_of(2 * own_rows * lax.rem(yc, 2), 16), 2 * own_rows), :]
    tall = tall[:, : 3 * WIDTH].astype(F32)
    w_own = jnp.where(core == 0, tall[:own_rows], tall[own_rows:])
    dotted = jnp.sum(w_own * gq_ref[0], axis=-1, keepdims=True)
    lanes = lax.broadcasted_iota(jnp.int32, (own_rows, WIDTH), 1)
    subs = lax.broadcasted_iota(jnp.int32, (own_rows, WIDTH), 0)
    gain_own = jnp.sum(
        jnp.where(lanes == subs + own_rows * me, gain_ref[...], 0.0), axis=-1, keepdims=True
    )
    spread = jnp.where(lanes == subs, dotted / gain_own, 0.0)
    gg_ref[...] = jnp.sum(spread, axis=0, keepdims=True)[:, :own_rows]

    drain()
    for w in (1, 2):
        plane_drain(w)

    @pl.when(sec == 0)
    def _():
        for t in range(1, LAYERS):
            for late in range(2):
                tab_copy(t, late).wait_send()
            first_copy(t).wait_send()

    @pl.when(sec > 0)
    def _():
        for late in range(2):
            tab_twin(core, late).wait_send()
        first_twin(core).wait_send()

    for d in range(1, LAYERS):
        gain_copy(d).wait_send()


def hand_over(qkv_in, out_in, gain_in, qkv_out, out_out, gain_out):
    qkv_out[...] = qkv_in[...]
    out_out[...] = out_in[...]
    gain_out[...] = gain_in[...]


def local(tokens, embed, ln_gain, w_qkv, w_out, out_grad):
    n_row = lax.axis_size("row")
    micro, rows_here, seq = tokens.shape
    vocab, width = embed.shape
    npos = rows_here * seq
    scale = HEAD_DIM ** (-0.5) / (rows_here * n_row) ** 0.5
    padded = vocab + -vocab % 16
    flat = HEADS * seq
    own_rows = width // n_row
    vm, anyspace = pl.BlockSpec(memory_space=pltpu.VMEM), pl.BlockSpec(memory_space=pl.ANY)
    dma = pltpu.SemaphoreType.DMA
    sums = pl.pallas_call(
        functools.partial(kernel, n_row, scale),
        out_shape=(
            jax.ShapeDtypeStruct((1, own_rows, 3 * width), F32),
            jax.ShapeDtypeStruct((1, own_rows, width), F32),
            jax.ShapeDtypeStruct((1, own_rows), F32),
        ),
        in_specs=[vm, vm, vm, anyspace, anyspace, anyspace],
        out_specs=(vm, vm, vm),
        scratch_shapes=[
            pltpu.VMEM((LAYERS, SIDE, 2, width // 8, 4 * width), BF),
            pltpu.VMEM((LAYERS, 1, width), F32),
            pltpu.VMEM((padded, width), BF),
            pltpu.VMEM((2, padded, 3 * width // 2), BF),
            pltpu.VMEM((LAYERS, npos, width), F32),
            pltpu.VMEM((LAYERS, npos, 3 * width), BF),
            pltpu.VMEM((LAYERS, flat, seq), BF),
            pltpu.VMEM((LAYERS, npos, width), BF),
            pltpu.VMEM((flat, seq), BF),
            pltpu.VMEM((flat // 2, seq), BF),
            pltpu.VMEM((flat // 2, seq), BF),
            pltpu.VMEM((n_row // 2, flat // n_row, seq), BF),
            pltpu.VMEM((flat, seq), BF),
            pltpu.VMEM((npos, width), F32),
            pltpu.VMEM((npos, width), BF),
            pltpu.VMEM((npos, width), BF),
            pltpu.VMEM((npos, 3 * width), BF),
            pltpu.VMEM((npos, width), BF),
            pltpu.VMEM((npos, width), F32),
            pltpu.VMEM((4, 2, SIDE, SIDE, own_rows, width), BF),
            pltpu.VMEM((2, 4, SIDE, SIDE, own_rows, width), BF),
            pltpu.VMEM((2, 4, SIDE - 1, SIDE, own_rows, width), BF),
            pltpu.VMEM((2, 4, SIDE, own_rows, width), BF),
            pltpu.VMEM((2, 4, SIDE - 1, own_rows, width), BF),
            pltpu.VMEM((4, own_rows, width), BF),
            pltpu.VMEM((4, LAYERS - 1, own_rows, width), BF),
            pltpu.VMEM((4, own_rows, width), F32),
            dma((2,)),
            dma((n_row // 2,)),
            dma((n_row // 2,)),
            dma((n_row // 2,)),
            dma((n_row // 2,)),
            dma((n_row // 2,)),
            dma((n_row // 2,)),
            dma((2,)),
            dma,
            dma((2, LAYERS)),
            dma((2, 2)),
            dma((LAYERS,)),
            dma((LAYERS,)),
            dma((2, LAYERS)),
            dma((2,)),
            dma((LAYERS,)),
            dma,
            dma((2, 2, SIDE - 1)),
            dma((2, 2, SIDE - 1)),
            dma((2, 2, SIDE - 1)),
            dma((2, 2, SIDE - 1)),
            dma((2, 2)),
            dma((2, 2)),
            dma((2, CHUNKS)),
            dma((2, CHUNKS)),
            dma((2, CHUNKS)),
            dma((2, CHUNKS)),
            dma((LAYERS,)),
            dma((2,)),
            dma((4,)),
            dma((2, 4)),
            dma((4, SIDE - 1)),
            dma((2, 4, SIDE - 1)),
            dma((4, SIDE - 1)),
            dma((2, 4, SIDE - 1)),
            dma((4,)),
            dma((4, LAYERS - 1)),
        ],
        compiler_params=pltpu.CompilerParams(
            collective_id=0, has_side_effects=True, vmem_limit_bytes=67043328
        ),
    )(
        tokens,
        embed,
        ln_gain,
        w_qkv.reshape(SIDE, 2, width // 8, 3 * width),
        w_out.reshape(SIDE, 2, width // 8, width),
        out_grad.reshape(micro, npos, width),
    )
    grad_qkv, grad_out, grad_gain = pl.pallas_call(
        hand_over,
        out_shape=tuple(jax.ShapeDtypeStruct(g.shape, F32) for g in sums),
        in_specs=[vm, vm, vm],
        out_specs=(vm, vm, vm),
    )(*sums)
    return (grad_qkv, grad_out, grad_gain)


def solution(mesh):
    in_specs = (
        P(None, "row", None),
        P(),
        P("section", None),
        P("section", None, None),
        P("section", None, None),
        P(None, "row", None, None),
    )
    out_specs = (P("section", "row", None), P("section", "row", None), P("section", "row"))
    return jax.shard_map(local, mesh=mesh, in_specs=in_specs, out_specs=out_specs, check_vma=False)
```
